256 devices in a mesh: lat: 16 (over x, y), lon: 8 (over z), ens: 2 (over core).
Axes of the slice: x: 4, y: 4, z: 8, core: 2. Of those that a mesh axis runs over, the one named last changes fastest.
Arguments:
- parameters: float32 [2, 128, 128, 1024], P(None, 'ens', 'lat', 'lon'), may hold values from -1.2 to 1.2, as said below
- initial_height: float32 [128, 1024], P('lat', 'lon'), may hold values from -6 to 6
- initial_speed: float32 [2, 128, 1024], P(None, 'lat', 'lon'), may hold values from -4 to 4
- obs_slots: int32 [2, 128, 128, 8], P(None, ('lat', 'lon')), may hold values from -1 to 1023, as said below
- obs_values: float32 [2, 128, 128, 8], P(None, ('lat', 'lon')), may hold values from -6 to 6
- obs_precision: float32 [2, 128, 128, 8], P(None, ('lat', 'lon')), may hold values from 0 to 2, as said below
Outputs:
- calibrated: float32 [2, 128, 128, 1024], P(None, 'ens', 'lat', 'lon')
The draws below stay inside these ranges and needn't reach their ends.
Inputs may be any that keep to these rules, and one draw needn't show every extreme that they name: `obs_slots`: for each iteration and owner, the live slots towards one receiver come first and name distinct cells of the owner's block (local index row * 128 + column); no cell is named twice by one owner in one iteration; in each iteration some receiving block has all 8 slots live from every owner. `obs_precision`: zero exactly where the matching slot of obs_slots (with receiver and owner swapped) is empty, 0.5 or more elsewhere. `parameters`: friction rates lie in 0.02 to 0.2, forcing in -1.2 to 1.2.
All inputs are finite; a program needn't handle non-finite values.
Results may differ from the reference program's by a relative error of at most 0.0003.
Values sent between devices are 32-bit elements; how exact they have to be, the bound alone decides.
No kernel may reach another device: no remote copies, remote signals or barrier semaphores. Data moves between devices by JAX's collectives and lax.ppermute only.
A program may use at most 64 MiB of HBM per device.

```python
import jax
import jax.numpy as jnp
from jax import lax

CLAT = 8
CLON = 128
MEMBERS = 128
STEPS = 6
ITERS = 2
CAP = 8
NLAT = 128
NLON = 1024
OWNERS = 128
N_LAT = 16
N_LON = 8


def live_counts(key):
    owners = N_LAT * N_LON
    base = jax.random.fold_in(key, 7)
    counts = jax.random.randint(base, (ITERS, owners, owners), CAP // 4, CAP + 1)
    full_dest = jax.random.randint(jax.random.fold_in(base, 1), (ITERS,), 0, owners)
    receivers = jnp.arange(owners)
    counts = jnp.where(receivers[None, None, :] == full_dest[:, None, None], CAP, counts)
    slot_ids = jnp.arange(CAP)
    return slot_ids[None, None, None, :] < counts[..., None]


def draw_obs_slots(key, part):
    owners = N_LAT * N_LON
    live = live_counts(key)
    subkeys = jax.random.split(jax.random.fold_in(key, 11), ITERS * owners)
    orders = jax.vmap(lambda sub: jax.random.permutation(sub, CLAT * CLON))(subkeys)
    chosen = orders[:, :owners * CAP].reshape(ITERS, owners, owners, CAP).astype(jnp.int32)
    return jnp.where(live, chosen, -1).astype(jnp.int32)


def draw_obs_precision(key, part):
    owners = N_LAT * N_LON
    live = jnp.transpose(live_counts(key), (0, 2, 1, 3))
    sub = jax.random.fold_in(key, 23)
    values = jnp.exp(jax.random.uniform(sub, (ITERS, owners, owners, CAP), jnp.float32, jnp.log(0.5), jnp.log(2.0)))
    return jnp.where(live, values, 0.0).astype(jnp.float32)


def draw_parameters(key, part):
    first = jax.random.fold_in(key, 31)
    second = jax.random.fold_in(key, 37)
    friction = jnp.exp(jax.random.uniform(first, (MEMBERS, NLAT, NLON), jnp.float32, jnp.log(0.02), jnp.log(0.2)))
    forcing = jnp.clip(0.3 * jax.random.normal(second, (MEMBERS, NLAT, NLON), jnp.float32), -1.2, 1.2)
    return jnp.stack([friction, forcing]).astype(jnp.float32)


def levels(rng, shape, pieces, smallest, top_value):
    def one(position, shards_of):
        heights = jax.random.uniform(jax.random.fold_in(jax.random.fold_in(rng, 6), position), (shards_of,), jnp.float32, smallest / len(pieces), top_value / len(pieces))
        return jnp.repeat(jnp.exp(heights), shape[position] // shards_of).reshape((-1,) + (1,) * (len(shape) - position - 1))

    loudness = one(*pieces[0])
    for cut in pieces[1:]:
        loudness = loudness * one(*cut)
    return loudness


def bell_draw(stream_key, dims, deviation, most, pieces=(), held_as=jnp.bfloat16):
    gain = levels(stream_key, dims, pieces, -0.22, 0.18) if pieces else 1.0
    entries = jax.random.normal(stream_key, dims, jnp.float32) * deviation * gain
    return jnp.minimum(jnp.maximum(entries, -most), most).astype(held_as)


def setup_inputs(seed: int = 0) -> dict:
    arg_keys = jax.random.split(jax.random.key(seed), 7)
    parameters = draw_parameters(jax.random.fold_in(arg_keys[6], 71), 0)
    initial_height = bell_draw(arg_keys[1], (NLAT, NLON), 1.0, 6.0, ((0, 16), (1, 8)), jnp.float32)
    initial_speed = bell_draw(arg_keys[2], (2, NLAT, NLON), 0.5, 4.0, ((1, 16), (2, 8)), jnp.float32)
    obs_slots = draw_obs_slots(jax.random.fold_in(arg_keys[6], 71), 0)
    obs_values = bell_draw(arg_keys[4], (ITERS, OWNERS, OWNERS, CAP), 1.0, 6.0, ((1, 128),), jnp.float32)
    obs_precision = draw_obs_precision(jax.random.fold_in(arg_keys[6], 71), 0)
    return dict(parameters=parameters, initial_height=initial_height, initial_speed=initial_speed, obs_slots=obs_slots, obs_values=obs_values, obs_precision=obs_precision)


depth_step = 0.7
gravity_step = 0.7
coriolis = 0.1

def pad_grid(field):
    wrapped = jnp.concatenate([field[..., -1:], field, field[..., :1]], axis=-1)
    widths = [(0, 0)] * (field.ndim - 2) + [(1, 1), (0, 0)]
    return jnp.pad(wrapped, widths)

def forward(parameters, initial_height, initial_speed):
    members = parameters.shape[1]
    height = jnp.broadcast_to(initial_height, (members,) + initial_height.shape)
    speeds = jnp.broadcast_to(initial_speed[:, None], (2, members) + initial_height.shape)
    friction = parameters[0]
    forcing = parameters[1]
    for substep in range(STEPS):
        padded = pad_grid(speeds)
        east_diff = padded[0, :, 1:-1, 2:] - padded[0, :, 1:-1, :-2]
        north_diff = padded[1, :, 2:, 1:-1] - padded[1, :, :-2, 1:-1]
        height = height - depth_step * (east_diff + north_diff) + forcing
        padded_height = pad_grid(height)
        slope_east = padded_height[:, 1:-1, 2:] - padded_height[:, 1:-1, :-2]
        slope_north = padded_height[:, 2:, 1:-1] - padded_height[:, :-2, 1:-1]
        eastward = (1.0 - friction) * speeds[0] - gravity_step * slope_east + coriolis * speeds[1]
        northward = (1.0 - friction) * speeds[1] - gravity_step * slope_north - coriolis * speeds[0]
        speeds = jnp.stack([eastward, northward])
    return height

def gram_terms(predicted, observed, precision):
    members = predicted.shape[1]
    centre = lax.optimization_barrier(jnp.mean(predicted, axis=1, keepdims=True))
    spread = predicted - centre
    weighted = spread * precision[:, None]
    misfit = observed[:, None] - predicted
    gram_part = jnp.dot(spread.T, weighted, precision=lax.Precision.HIGHEST) / members
    cross_part = jnp.dot(weighted.T, misfit, precision=lax.Precision.HIGHEST) / jnp.sqrt(jnp.float32(members))
    return (gram_part, cross_part)

def solve_weights(gram_part, cross_part):
    members = gram_part.shape[0]
    system = jnp.eye(members, dtype=jnp.float32) + gram_part
    factor = jnp.linalg.cholesky(system)
    weights = jax.scipy.linalg.cho_solve((factor, True), cross_part) / jnp.sqrt(jnp.float32(members))
    return weights - lax.optimization_barrier(jnp.mean(weights, axis=0, keepdims=True))

def reference(parameters, initial_height, initial_speed, obs_slots, obs_values, obs_precision):
    owners = N_LAT * N_LON
    members = parameters.shape[1]
    owner_ids = jnp.arange(owners, dtype=jnp.int32)[:, None, None]
    for iteration in range(ITERS):
        height = forward(parameters, initial_height, initial_speed)
        cells = obs_slots[iteration]
        local = jnp.maximum(cells, 0)
        grid_row = owner_ids // N_LON * CLAT + local // CLON
        grid_col = owner_ids % N_LON * CLON + local % CLON
        global_ids = jnp.transpose(grid_row * NLON + grid_col, (1, 0, 2)).reshape(-1).astype(jnp.int32)
        live = jnp.transpose(cells >= 0, (1, 0, 2)).reshape(-1)
        flattened = height.reshape(members, -1)
        predicted = jnp.take(flattened, global_ids, axis=1).T
        predicted = jnp.where(live[:, None], predicted, jnp.float32(0.0))
        observed = obs_values[iteration].reshape(-1)
        precision = obs_precision[iteration].reshape(-1)
        gram_part, cross_part = gram_terms(predicted, observed, precision)
        centred = solve_weights(gram_part, cross_part)
        stacked = parameters.reshape(2, members, -1)
        increment = jnp.einsum('pjc,jm->pmc', stacked, centred, precision=lax.Precision.HIGHEST)
        parameters = parameters + increment.reshape(parameters.shape)
    return parameters
```

```python
import functools

import jax
import jax.numpy as jnp
from jax import lax
from jax.experimental import pallas as pl
from jax.experimental.pallas import tpu as pltpu
from jax.sharding import Mesh
from jax.sharding import PartitionSpec as P

STEPS = 6
LAT = ("lat_0", "lat_1")
LAT_LON = ("lat_0", "lat_1", "lon")
LON_ENS = ("lon", "ens")

DEPTH = 0.7
GRAVITY = 0.7
CORIOLIS = 0.1

MEMBERS = 128
HALF = 64
ROWS = 8
COLS = 128
EXT = 28
WIDE = 112
LEFT = 24
RIGHT = LEFT + HALF
INIT = 24
GLOBAL_ROWS = 128

F32 = jnp.float32
HIGHEST = lax.Precision.HIGHEST
VMEM = pl.BlockSpec(memory_space=pltpu.VMEM)
SMEM = pl.BlockSpec(memory_space=pltpu.SMEM)


def params():
    return pltpu.CompilerParams(vmem_limit_bytes=48 * 1024 * 1024)


def shape(*dims):
    return jax.ShapeDtypeStruct(dims, F32)


def iota(dims, axis):
    return lax.broadcasted_iota(jnp.int32, dims, axis)


def spread_members(pos, own, other, init, fr, fo, up2, dn2, right, left):
    def emit(low, high, first):
        for f, out in ((0, fr), (1, fo)):
            for r in range(ROWS):
                start = f * HALF * ROWS + r
                block = jnp.concatenate(
                    [low[pl.ds(start, HALF, stride=ROWS), :], high[pl.ds(start, HALF, stride=ROWS), :]],
                    axis=0,
                )
                turned = block.T[first : first + HALF]
                out[r * HALF : (r + 1) * HALF] = turned
                at = (f * ROWS + r) * 16
                right[at : at + 16] = turned[HALF - 16 :]
                left[at : at + 16] = turned[:16]
                if f == 1 and r >= 6:
                    up2[(r - 6) * HALF : (r - 5) * HALF] = turned
                if f == 0 and r == 7:
                    up2[2 * HALF : 3 * HALF] = turned
                if f == 1 and r < 2:
                    dn2[r * HALF : (r + 1) * HALF] = turned
                if f == 0 and r == 0:
                    dn2[2 * HALF : 3 * HALF] = turned

    fields = init[...]
    fo[ROWS * HALF :] = fields
    up2[3 * HALF :] = fields
    dn2[3 * HALF :] = fields

    @pl.when(pos[1] == 0)
    def _():
        emit(own, other, 0)

    @pl.when(pos[1] == 1)
    def _():
        emit(other, own, HALF)


FO_ROWS = [r for r in range(EXT) if not 10 <= r < 18]
FR_ROWS = [r for r in range(1, EXT - 1) if not 10 <= r < 18]
EDGE = 16 * (len(FO_ROWS) + len(FR_ROWS)) + 5 * INIT


def row_source(field, r, own, m1, p1, m2, p2):
    own, m1, p1 = own[field], m1[field], p1[field]
    if 10 <= r < 18:
        return own, (r - 10) * HALF
    if 2 <= r < 10:
        return m1, (r - 2) * HALF
    if 18 <= r < 26:
        return p1, (r - 18) * HALF
    ref = m2 if r < 2 else p2
    if field == 1:
        return ref, (r if r < 2 else r - 26) * HALF
    return ref, 2 * HALF


def pack_edges(fr, fo, m1_fr, m1_fo, p1_fr, p1_fo, m2, p2, right, left):
    at = 0
    for field, rows in ((1, FO_ROWS), (0, FR_ROWS)):
        for r in rows:
            ref, start = row_source(field, r, (fr, fo), (m1_fr, m1_fo), (p1_fr, p1_fo), m2, p2)
            right[at : at + 16] = ref[start + HALF - 16 : start + HALF]
            left[at : at + 16] = ref[start : start + 16]
            at += 16
    for ref, start in ((m2, 3 * HALF), (m1_fo, ROWS * HALF), (fo, ROWS * HALF), (p1_fo, ROWS * HALF), (p2, 3 * HALF)):
        fields = ref[start : start + INIT]
        right[at : at + INIT] = fields
        left[at : at + INIT] = fields
        at += INIT


def scatter_obs(pos, slots, values, precision, weights, observed):
    lines = ROWS * HALF
    k = iota((lines, MEMBERS), 0)
    cell = (k // HALF) * COLS + pos[1] * HALF + k % HALF
    for t in range(2):
        found_w = jnp.zeros((lines, MEMBERS), F32)
        found_y = jnp.zeros((lines, MEMBERS), F32)
        for s in range(8):
            at = t * 8 + s
            hit = cell == slots[at : at + 1, :]
            found_w = found_w + jnp.where(hit, precision[at : at + 1, :], 0.0)
            found_y = found_y + jnp.where(hit, values[at : at + 1, :], 0.0)
        weights[t] = jnp.broadcast_to(jnp.sum(found_w, axis=1, keepdims=True), (lines, MEMBERS))
        observed[t] = jnp.broadcast_to(jnp.sum(found_y, axis=1, keepdims=True), (lines, MEMBERS))


def inside(lat, r):
    row = lat * ROWS + r - 10
    return jnp.logical_and(row >= 0, row < GLOBAL_ROWS)


def initial_table(pos, tiles, lz, rz):
    first = 16 * (len(FO_ROWS) + len(FR_ROWS))
    lane = iota((ROWS, COLS), 1)
    row = iota((ROWS, COLS), 0)
    e = pos[1]
    fields = [[], [], []]
    for k, (ref, start) in enumerate(tiles):
        for f in range(3):
            own = ref[start + f * ROWS : start + (f + 1) * ROWS]
            at = first + k * INIT + f * ROWS
            before = lz[at : at + ROWS]
            after = rz[at : at + ROWS]
            low = pltpu.roll(jnp.where(lane >= 112, before, own), 16, 1)
            high = pltpu.roll(jnp.where(lane < 16, after, own), 80, 1)
            window = jnp.where(e == 0, low, high)
            place = pos[0] * ROWS + (k - 2) * ROWS + row
            ok = jnp.logical_and(place >= 0, place < GLOBAL_ROWS)
            fields[f].append(jnp.where(ok, window, 0.0))
    h, u, v = (jnp.concatenate(f, axis=0) for f in fields)
    east = pltpu.roll(u, COLS - 1, 1) - pltpu.roll(u, 1, 1)
    north = jnp.concatenate([v[1:], v[:1]], axis=0) - jnp.concatenate([v[-1:], v[:-1]], axis=0)
    place = pos[0] * ROWS - 16 + iota((40, COLS), 0)
    ok = jnp.logical_and(place >= 0, place < GLOBAL_ROWS)
    base = jnp.where(ok, h - DEPTH * (east + north), 0.0)
    return jnp.concatenate([base, u, v, jnp.zeros((8, COLS), F32)], axis=0).T


def forward(lat, table, FR, FO, H, U, V):
    first = table[0:96]

    def start(f, r):
        lane = f * 40 + r + 6
        return jnp.broadcast_to(first[:, lane : lane + 1], (96, MEMBERS))

    def gains(r):
        ok = inside(lat, r)
        return jnp.where(ok, F32(GRAVITY), F32(0.0)), jnp.where(ok, F32(CORIOLIS), F32(0.0))

    for r in range(EXT):
        H[r, 8:104] = start(0, r) + FO[r, 8:104]
    for r in range(1, EXT - 1):
        g, c = gains(r)
        u, v = start(1, r), start(2, r)
        keep = 1.0 - FR[r, 8:104]
        U[r, 8:104] = keep * u - g * (H[r, 9:105] - H[r, 7:103]) + c * v
        V[r, 8:104] = keep * v - g * (H[r + 1, 8:104] - H[r - 1, 8:104]) - c * u

    def height_row(a, b, r):
        g, _ = gains(r)
        n = b - a
        east = U[r, pl.ds(a + 1, n)] - U[r, pl.ds(a - 1, n)]
        north = V[r + 1, pl.ds(a, n)] - V[r - 1, pl.ds(a, n)]
        H[r, pl.ds(a, n)] = H[r, pl.ds(a, n)] - g * (east + north) + FO[r, pl.ds(a, n)]

    def speed_row(a, b, r):
        g, c = gains(r)
        n = b - a
        u, v = U[r, pl.ds(a, n)], V[r, pl.ds(a, n)]
        keep = 1.0 - FR[r, pl.ds(a, n)]
        east = H[r, pl.ds(a + 1, n)] - H[r, pl.ds(a - 1, n)]
        north = H[r + 1, pl.ds(a, n)] - H[r - 1, pl.ds(a, n)]
        U[r, pl.ds(a, n)] = keep * u - g * east + c * v
        V[r, pl.ds(a, n)] = keep * v - g * north - c * u

    def sweep(row, reach, a, b):
        def body(i, carry):
            row(a, b, 10 - reach + 2 * i)
            row(a, b, 11 - reach + 2 * i)
            return carry

        lax.fori_loop(0, (ROWS + 2 * reach) // 2, body, 0)

    for step in range(1, STEPS):
        reach = 2 * (STEPS - 1 - step)
        a, b = (16, 96) if reach else (LEFT, RIGHT)
        sweep(height_row, reach, a, b)
        if reach:
            sweep(speed_row, reach - 1, a, b)


def gram(pos, H, weights, observed, keep, send):
    lines = ROWS * HALF
    h = H[10:18, LEFT:RIGHT].reshape(lines, MEMBERS)
    centre = jnp.mean(h, axis=1, keepdims=True)
    spread = h - centre
    weighted = spread * weights
    g = lax.dot_general(spread, weighted, (((0,), (0,)), ((), ())), precision=HIGHEST, preferred_element_type=F32)
    d = jnp.sum(weighted * (observed - centre), axis=0, keepdims=True)
    row, lane = iota((HALF, MEMBERS), 0), iota((HALF, MEMBERS), 1)
    top, bottom = g[:HALF], g[HALF:]
    packed = jnp.where(jnp.logical_and(lane < HALF, lane > row), pltpu.roll(bottom, HALF, 1), top)
    diagonal = jnp.sum(jnp.where(lane == row + HALF, bottom, 0.0), axis=0, keepdims=True)
    line = iota((8, MEMBERS), 0)
    rest = jnp.where(line == 0, d, jnp.where(line == 1, diagonal, 0.0))
    one = jnp.concatenate([packed[:32], rest], axis=0)
    two = jnp.concatenate([packed[32:], jnp.zeros((8, MEMBERS), F32)], axis=0)
    e = pos[1]
    keep[...] = jnp.where(e == 0, one, two)
    send[...] = jnp.where(e == 0, two, one)


def first_run(pos, fr, fo, m1_fr, m1_fo, p1_fr, p1_fo, m2, p2, lz0, rz0, lz, rz, weights, observed,
              FR, FO, table, keep, send, H, U, V):
    at = 0
    for field, out, rows in ((1, FO, FO_ROWS), (0, FR, FR_ROWS)):
        for r in range(EXT):
            if field == 0 and r not in FR_ROWS and not 10 <= r < 18:
                continue
            ref, begin = row_source(field, r, (fr, fo), (m1_fr, m1_fo), (p1_fr, p1_fo), m2, p2)
            if 10 <= r < 18:
                k = (field * ROWS + r - 10) * 16
                west, east = lz0[k : k + 16], rz0[k : k + 16]
            else:
                west, east = lz[at : at + 16], rz[at : at + 16]
                at += 16
            middle = ref[begin : begin + HALF]
            if field == 1 and not 10 <= r < 18:
                ok = inside(pos[0], r)
                west, middle, east = (jnp.where(ok, x, 0.0) for x in (west, middle, east))
            out[r, LEFT - 16 : LEFT] = west
            out[r, LEFT:RIGHT] = middle
            out[r, RIGHT : RIGHT + 16] = east
    tiles = ((m2, 3 * HALF), (m1_fo, ROWS * HALF), (fo, ROWS * HALF), (p1_fo, ROWS * HALF), (p2, 3 * HALF))
    table[...] = initial_table(pos, tiles, lz, rz)
    forward(pos[0], table[...], FR, FO, H, U, V)
    gram(pos, H, weights[0], observed[0], keep, send)


def weights_of(pos, mine, other):
    e = pos[1]
    one = jnp.where(e == 0, mine, other)
    two = jnp.where(e == 0, other, mine)
    packed = jnp.concatenate([one[:32], two[:32]], axis=0)
    d, diagonal = one[32:33], one[33:34]
    turned = jnp.concatenate([packed, jnp.zeros((HALF, MEMBERS), F32)], axis=0).T
    row, lane = iota((HALF, MEMBERS), 0), iota((HALF, MEMBERS), 1)
    a = jnp.where(lane <= row, packed, turned[:HALF])
    c = pltpu.roll(jnp.where(lane > row, packed, turned[:HALF]), HALF, 1)
    c = jnp.where(lane == row + HALF, diagonal, c)
    top = jnp.where(lane < HALF, a, packed)
    bottom = jnp.where(lane < HALF, turned[HALF:], c)
    g = jnp.concatenate([top, bottom], axis=0)
    row, lane = iota((MEMBERS, MEMBERS), 0), iota((MEMBERS, MEMBERS), 1)
    x = g * (1.0 / MEMBERS) + jnp.where(row == lane, 1.0, 0.0)
    lane1 = iota((1, MEMBERS), 1)
    for k in range(MEMBERS):
        pivot_row = x[k : k + 1]
        inverse = 1.0 / pivot_row[:, k : k + 1]
        scaled = jnp.where(lane1 == k, inverse, pivot_row * inverse)
        column = x[:, k : k + 1]
        x = jnp.where(row == k, scaled, jnp.where(lane == k, 0.0, x) - column * scaled)
    shift = jnp.sum(x * d, axis=1, keepdims=True) * (1.0 / MEMBERS)
    z = x + shift
    return z - jnp.mean(z, axis=0, keepdims=True) + 1.0 / MEMBERS


def second_run(pos, mine, other, fr, fo, table, weights, observed, k1, keep, send, FR, FO, H, U, V):
    k = weights_of(pos, mine[...], other[...])
    k1[...] = k
    for src, out in ((fr, FR), (fo, FO)):
        new = jnp.dot(src[...].reshape(EXT * WIDE, MEMBERS), k, precision=HIGHEST, preferred_element_type=F32)
        out[...] = new.reshape(EXT, WIDE, MEMBERS)
    forward(pos[0], table[...], FR, FO, H, U, V)
    gram(pos, H, weights[1], observed[1], keep, send)


def last_update(pos, mine, other, k1, own_p, other_p, out):
    k = jnp.dot(k1[...], weights_of(pos, mine[...], other[...]), precision=HIGHEST, preferred_element_type=F32)

    def emit(low, high, first):
        kt = k.T[first : first + HALF]
        for f in range(2):
            for r in range(ROWS):
                start = f * HALF * ROWS + r
                block = jnp.concatenate(
                    [low[pl.ds(start, HALF, stride=ROWS), :], high[pl.ds(start, HALF, stride=ROWS), :]],
                    axis=0,
                )
                out[pl.ds(start, HALF, stride=ROWS), :] = jnp.dot(
                    kt, block, precision=HIGHEST, preferred_element_type=F32
                )

    @pl.when(pos[1] == 0)
    def _():
        emit(own_p, other_p, 0)

    @pl.when(pos[1] == 1)
    def _():
        emit(other_p, own_p, HALF)


def swap(value):
    return lax.ppermute(value, "ens", [(0, 1), (1, 0)])


def moved(value, axes, by):
    n = lax.axis_size(axes)
    return lax.ppermute(value, axes, [(i, (i + by) % n) for i in range(n)])


def reduced(keep, send):
    value = keep + swap(send)
    for axis in ("lon", "lat_1", "lat_0"):
        n = lax.axis_size(axis)
        bit = 1
        while bit < n:
            value = value + lax.ppermute(value, axis, [(i, i ^ bit) for i in range(n)])
            bit *= 2
    return value, swap(value)


def call(kernel, out_shape, scalars, *args, scratch=()):
    return pl.pallas_call(
        kernel,
        out_shape=out_shape,
        in_specs=[SMEM] + [VMEM] * len(args),
        out_specs=jax.tree.map(lambda _: VMEM, out_shape),
        scratch_shapes=list(scratch),
        compiler_params=params(),
    )(scalars, *args)


def per_device(parameters, initial_height, initial_speed, obs_slots, obs_values, obs_precision):
    pos = jnp.stack([lax.axis_index(LAT), lax.axis_index("ens")]).astype(jnp.int32)
    own_p = parameters.reshape(2 * HALF * ROWS, COLS)
    other_p = swap(own_p)
    init = jnp.concatenate([initial_height, initial_speed[0], initial_speed[1]], axis=0)

    fr, fo, up2, dn2, right0, left0 = call(
        spread_members,
        [shape(512, 128), shape(536, 128), shape(216, 128), shape(216, 128), shape(256, 128), shape(256, 128)],
        pos, own_p, other_p, init,
    )
    m2, p2 = moved(up2, LAT, 2), moved(dn2, LAT, -2)
    m1_fr, p1_fr = moved(fr, LAT, 1), moved(fr, LAT, -1)
    m1_fo, p1_fo = moved(fo, LAT, 1), moved(fo, LAT, -1)
    lz0, rz0 = moved(right0, LON_ENS, 1), moved(left0, LON_ENS, -1)

    obs = jnp.stack([obs_values[:, 0], obs_precision[:, 0]]).transpose(2, 0, 1, 3).reshape(128, 32)
    obs = lax.all_to_all(obs, LAT_LON, 0, 0, tiled=True).T
    slots = obs_slots[:, 0].transpose(0, 2, 1).reshape(16, 128)
    weights, observed = call(
        scatter_obs, [shape(2, 512, 128), shape(2, 512, 128)], pos, slots, obs[:16], obs[16:]
    )

    right, left = pl.pallas_call(
        pack_edges,
        out_shape=[shape(EDGE, 128)] * 2,
        in_specs=[VMEM] * 8,
        out_specs=[VMEM] * 2,
        compiler_params=params(),
    )(fr, fo, m1_fr, m1_fo, p1_fr, p1_fo, m2, p2)
    lz, rz = moved(right, LON_ENS, 1), moved(left, LON_ENS, -1)

    field = shape(EXT, WIDE, MEMBERS)
    half = shape(40, MEMBERS)
    square = shape(MEMBERS, MEMBERS)
    state = [pltpu.VMEM((EXT, WIDE, MEMBERS), F32)]
    ext_fr, ext_fo, table, keep, send = call(
        first_run, [field, field, square, half, half],
        pos, fr, fo, m1_fr, m1_fo, p1_fr, p1_fo, m2, p2, lz0, rz0, lz, rz, weights, observed,
        scratch=state * 3,
    )
    mine, other = reduced(keep, send)
    k1, keep, send = call(
        second_run, [square, half, half],
        pos, mine, other, ext_fr, ext_fo, table, weights, observed,
        scratch=state * 5,
    )
    mine, other = reduced(keep, send)
    out = call(last_update, shape(2 * HALF * ROWS, COLS), pos, mine, other, k1, own_p, other_p)
    return out.reshape(parameters.shape)


def solution(mesh):
    torus = Mesh(
        mesh.devices.reshape(4, 4, mesh.shape["lon"], mesh.shape["ens"]),
        ("lat_0", "lat_1", "lon", "ens"),
    )
    in_specs = (
        P(None, "ens", LAT, "lon"),
        P(LAT, "lon"),
        P(None, LAT, "lon"),
        P(None, LAT_LON, None, None),
        P(None, LAT_LON, None, None),
        P(None, LAT_LON, None, None),
    )
    out_specs = P(None, "ens", LAT, "lon")
    return jax.shard_map(
        per_device, mesh=torus, in_specs=in_specs, out_specs=out_specs, check_vma=False
    )
```

```python
import functools

import jax
import jax.numpy as jnp
from jax import lax
from jax.experimental import pallas as pl
from jax.experimental.pallas import tpu as pltpu
from jax.sharding import Mesh
from jax.sharding import PartitionSpec as P

STEPS = 6
LAT = ("lat_0", "lat_1")
LAT_LON = ("lat_0", "lat_1", "lon")
LON_ENS = ("lon", "ens")

DEPTH = 0.7
GRAVITY = 0.7
CORIOLIS = 0.1

MEMBERS = 128
HALF = 64
ROWS = 8
COLS = 128
EXT = 28
WIDE = 112
LEFT = 24
RIGHT = LEFT + HALF
INIT = 24
GLOBAL_ROWS = 128
OWN = 2 * ROWS * HALF
PIVOTS = 16

F32 = jnp.float32
HIGHEST = lax.Precision.HIGHEST
VMEM = pl.BlockSpec(memory_space=pltpu.VMEM)
SMEM = pl.BlockSpec(memory_space=pltpu.SMEM)


def params():
    return pltpu.CompilerParams(vmem_limit_bytes=24 * 1024 * 1024)


def shape(*dims):
    return jax.ShapeDtypeStruct(dims, F32)


def iota(dims, axis):
    return lax.broadcasted_iota(jnp.int32, dims, axis)


def spread_members(pos, own, other, height, speed, values, precision, out, up2, dn2, obs):
    def emit(low, high, first):
        for f in range(2):
            for r in range(ROWS):
                start = f * HALF * ROWS + r
                block = jnp.concatenate(
                    [low[pl.ds(start, HALF, stride=ROWS), :], high[pl.ds(start, HALF, stride=ROWS), :]],
                    axis=0,
                )
                turned = block.T[first : first + HALF]
                at = (f * ROWS + r) * HALF
                out[at : at + HALF] = turned
                if f == 1 and r >= 6:
                    up2[(r - 6) * HALF : (r - 5) * HALF] = turned
                if f == 0 and r == 7:
                    up2[2 * HALF : 3 * HALF] = turned
                if f == 1 and r < 2:
                    dn2[r * HALF : (r + 1) * HALF] = turned
                if f == 0 and r == 0:
                    dn2[2 * HALF : 3 * HALF] = turned

    for ref, at in ((out, OWN), (up2, 3 * HALF), (dn2, 3 * HALF)):
        ref[at : at + ROWS] = height[...]
        ref[at + ROWS : at + INIT] = speed[...]
    lines = [values[...], precision[...], jnp.zeros((96, MEMBERS), F32)]
    obs[...] = jnp.concatenate(lines, axis=0).T

    @pl.when(pos[1] == 0)
    def _():
        emit(own, other, 0)

    @pl.when(pos[1] == 1)
    def _():
        emit(other, own, HALF)


def edge_rows():
    rows = []
    for field, first in ((1, 0), (0, 1)):
        for r in range(first, EXT - first):
            away = max(10 - r, r - 17, 0)
            need = 9 + field - away
            rows.append((field, r, 16 if need > 8 else 8))
    return rows


EDGE_ROWS = edge_rows()
EDGE_FIELDS = sum(n for _, _, n in EDGE_ROWS)
EDGE = EDGE_FIELDS + 5 * INIT


def row_source(field, r, own, m1, p1, m2, p2):
    at = field * ROWS * HALF
    if 10 <= r < 18:
        return own, at + (r - 10) * HALF
    if 2 <= r < 10:
        return m1, at + (r - 2) * HALF
    if 18 <= r < 26:
        return p1, at + (r - 18) * HALF
    ref = m2 if r < 2 else p2
    if field == 1:
        return ref, (r if r < 2 else r - 26) * HALF
    return ref, 2 * HALF


def initial_tiles(own, m1, p1, m2, p2):
    return ((m2, 3 * HALF), (m1, OWN), (own, OWN), (p1, OWN), (p2, 3 * HALF))


def pack_edges(own, m1, p1, m2, p2, _, right, left):
    at = 0
    for field, r, n in EDGE_ROWS:
        ref, start = row_source(field, r, own, m1, p1, m2, p2)
        right[at : at + n] = ref[start + HALF - n : start + HALF]
        left[at : at + n] = ref[start : start + n]
        at += n
    for ref, start in initial_tiles(own, m1, p1, m2, p2):
        fields = ref[start : start + INIT]
        right[at : at + INIT] = fields
        left[at : at + INIT] = fields
        at += INIT


def scatter_obs(pos, slots, received, weights, observed):
    received = received[...].T
    values, precision = received[:16], received[16:32]
    lines = ROWS * HALF
    k = iota((lines, MEMBERS), 0)
    cell = (k // HALF) * COLS + pos[1] * HALF + k % HALF
    for t in range(2):
        found_w = jnp.zeros((lines, MEMBERS), F32)
        found_y = jnp.zeros((lines, MEMBERS), F32)
        for s in range(8):
            at = t * 8 + s
            hit = cell == slots[at : at + 1, :]
            found_w = found_w + jnp.where(hit, precision[at : at + 1, :], 0.0)
            found_y = found_y + jnp.where(hit, values[at : at + 1, :], 0.0)
        weights[t] = jnp.broadcast_to(jnp.sum(found_w, axis=1, keepdims=True), (lines, MEMBERS))
        observed[t] = jnp.broadcast_to(jnp.sum(found_y, axis=1, keepdims=True), (lines, MEMBERS))


def inside(lat, r):
    row = lat * ROWS + r - 10
    return jnp.logical_and(row >= 0, row < GLOBAL_ROWS)


def initial_table(pos, tiles, lz, rz):
    first = EDGE_FIELDS
    lane = iota((ROWS, COLS), 1)
    row = iota((ROWS, COLS), 0)
    e = pos[1]
    fields = [[], [], []]
    for k, (ref, start) in enumerate(tiles):
        for f in range(3):
            own = ref[start + f * ROWS : start + (f + 1) * ROWS]
            at = first + k * INIT + f * ROWS
            before = lz[at : at + ROWS]
            after = rz[at : at + ROWS]
            low = pltpu.roll(jnp.where(lane >= 112, before, own), 16, 1)
            high = pltpu.roll(jnp.where(lane < 16, after, own), 80, 1)
            window = jnp.where(e == 0, low, high)
            place = pos[0] * ROWS + (k - 2) * ROWS + row
            ok = jnp.logical_and(place >= 0, place < GLOBAL_ROWS)
            fields[f].append(jnp.where(ok, window, 0.0))
    h, u, v = (jnp.concatenate(f, axis=0) for f in fields)
    east = pltpu.roll(u, COLS - 1, 1) - pltpu.roll(u, 1, 1)
    north = jnp.concatenate([v[1:], v[:1]], axis=0) - jnp.concatenate([v[-1:], v[:-1]], axis=0)
    place = pos[0] * ROWS - 16 + iota((40, COLS), 0)
    ok = jnp.logical_and(place >= 0, place < GLOBAL_ROWS)
    base = jnp.where(ok, h - DEPTH * (east + north), 0.0)
    return jnp.concatenate([base, u, v, jnp.zeros((8, COLS), F32)], axis=0).T


def forward(lat, table, FR, FO, H, U, V):
    first = table[0:96]

    def start(f, r):
        lane = f * 40 + r + 6
        return jnp.broadcast_to(first[:, lane : lane + 1], (96, MEMBERS))

    def gains(r):
        ok = inside(lat, r)
        return jnp.where(ok, F32(GRAVITY), F32(0.0)), jnp.where(ok, F32(CORIOLIS), F32(0.0))

    for r in range(EXT):
        H[r, 8:104] = start(0, r) + FO[r, 8:104]
    for r in range(1, EXT - 1):
        g, c = gains(r)
        u, v = start(1, r), start(2, r)
        keep = 1.0 - FR[r, 8:104]
        U[r, 8:104] = keep * u - g * (H[r, 9:105] - H[r, 7:103]) + c * v
        V[r, 8:104] = keep * v - g * (H[r + 1, 8:104] - H[r - 1, 8:104]) - c * u

    def height_row(a, b, r):
        g, _ = gains(r)
        n = b - a
        east = U[r, pl.ds(a + 1, n)] - U[r, pl.ds(a - 1, n)]
        north = V[r + 1, pl.ds(a, n)] - V[r - 1, pl.ds(a, n)]
        H[r, pl.ds(a, n)] = H[r, pl.ds(a, n)] - g * (east + north) + FO[r, pl.ds(a, n)]

    def speed_row(a, b, r):
        g, c = gains(r)
        n = b - a
        u, v = U[r, pl.ds(a, n)], V[r, pl.ds(a, n)]
        keep = 1.0 - FR[r, pl.ds(a, n)]
        east = H[r, pl.ds(a + 1, n)] - H[r, pl.ds(a - 1, n)]
        north = H[r + 1, pl.ds(a, n)] - H[r - 1, pl.ds(a, n)]
        U[r, pl.ds(a, n)] = keep * u - g * east + c * v
        V[r, pl.ds(a, n)] = keep * v - g * north - c * u

    def sweep(row, reach, a, b):
        def body(i, carry):
            row(a, b, 10 - reach + 2 * i)
            row(a, b, 11 - reach + 2 * i)
            return carry

        lax.fori_loop(0, (ROWS + 2 * reach) // 2, body, 0)

    for step in range(1, STEPS):
        reach = 2 * (STEPS - 1 - step)
        a, b = (16, 96) if reach else (LEFT, RIGHT)
        sweep(height_row, reach, a, b)
        if reach:
            sweep(speed_row, reach - 1, a, b)


def gram(pos, H, weights, observed, keep, send):
    lines = ROWS * HALF
    h = H[10:18, LEFT:RIGHT].reshape(lines, MEMBERS)
    centre = jnp.mean(h, axis=1, keepdims=True)
    spread = h - centre
    weighted = spread * weights
    g = lax.dot_general(spread, weighted, (((0,), (0,)), ((), ())), precision=HIGHEST, preferred_element_type=F32)
    d = jnp.sum(weighted * (observed - centre), axis=0, keepdims=True)
    row, lane = iota((HALF, MEMBERS), 0), iota((HALF, MEMBERS), 1)
    top, bottom = g[:HALF], g[HALF:]
    packed = jnp.where(jnp.logical_and(lane < HALF, lane > row), pltpu.roll(bottom, HALF, 1), top)
    diagonal = jnp.sum(jnp.where(lane == row + HALF, bottom, 0.0), axis=0, keepdims=True)
    line = iota((8, MEMBERS), 0)
    rest = jnp.where(line == 0, d, jnp.where(line == 1, diagonal, 0.0))
    one = jnp.concatenate([packed[:32], rest], axis=0)
    two = jnp.concatenate([packed[32:], jnp.zeros((8, MEMBERS), F32)], axis=0)
    e = pos[1]
    keep[...] = jnp.where(e == 0, one, two)
    send[...] = jnp.where(e == 0, two, one)


def first_run(pos, own, m1, p1, m2, p2, lz, rz, weights, observed, FR, FO, table, keep, send, H, U, V):
    at = 0
    for field, r, n in EDGE_ROWS:
        ref, begin = row_source(field, r, own, m1, p1, m2, p2)
        west, middle, east = lz[at : at + n], ref[begin : begin + HALF], rz[at : at + n]
        at += n
        if field == 1 and not 10 <= r < 18:
            ok = inside(pos[0], r)
            west, middle, east = (jnp.where(ok, x, 0.0) for x in (west, middle, east))
        out = FO if field else FR
        out[r, LEFT - n : LEFT] = west
        out[r, LEFT:RIGHT] = middle
        out[r, RIGHT : RIGHT + n] = east
    table[...] = initial_table(pos, initial_tiles(own, m1, p1, m2, p2), lz, rz)
    forward(pos[0], table[...], FR, FO, H, U, V)
    gram(pos, H, weights[0], observed[0], keep, send)


def inverse(x):
    n = PIVOTS
    panels = [x[k : k + n] for k in range(0, MEMBERS, n)]
    row, lane = iota((n, MEMBERS), 0), iota((n, MEMBERS), 1)
    lower, scaled = [], []

    def spread(panel, column):
        return jnp.broadcast_to(panel[:, column : column + 1], (n, MEMBERS))

    for k in range(len(panels)):
        first = k * n
        block = jnp.logical_and(lane >= first, lane < first + n)
        columns = [spread(panels[k], first + j) for j in range(n)]
        top = jnp.where(block, jnp.where(lane - first == row, 1.0, 0.0), panels[k])
        lower.append(jnp.where(lane < first + n, top, 0.0))
        for j in range(n):
            over = 1.0 / columns[j][j : j + 1]

            def eliminate(m, j=j, over=over):
                pivot = m[j : j + 1] * over
                return jnp.where(row == j, pivot, m - columns[j] * pivot)

            top = eliminate(top)
            columns[j + 1 :] = [eliminate(m) for m in columns[j + 1 :]]
        scaled.append(jnp.where(lane < first + n, top, 0.0))
        for i in range(k + 1, len(panels)):
            terms = [spread(panels[i], first + j) * top[j : j + 1] for j in range(n)]
            while len(terms) > 1:
                terms = [a + b for a, b in zip(terms[::2], terms[1::2])]
            panels[i] = jnp.where(block, 0.0, panels[i]) - terms[0]
    lower, scaled = jnp.concatenate(lower, axis=0), jnp.concatenate(scaled, axis=0)
    return lax.dot_general(lower, scaled, (((0,), (0,)), ((), ())), precision=HIGHEST, preferred_element_type=F32)


def weights_of(pos, mine, other):
    e = pos[1]
    one = jnp.where(e == 0, mine, other)
    two = jnp.where(e == 0, other, mine)
    packed = jnp.concatenate([one[:32], two[:32]], axis=0)
    d, diagonal = one[32:33], one[33:34]
    turned = jnp.concatenate([packed, jnp.zeros((HALF, MEMBERS), F32)], axis=0).T
    row, lane = iota((HALF, MEMBERS), 0), iota((HALF, MEMBERS), 1)
    a = jnp.where(lane <= row, packed, turned[:HALF])
    c = pltpu.roll(jnp.where(lane > row, packed, turned[:HALF]), HALF, 1)
    c = jnp.where(lane == row + HALF, diagonal, c)
    top = jnp.where(lane < HALF, a, packed)
    bottom = jnp.where(lane < HALF, turned[HALF:], c)
    g = jnp.concatenate([top, bottom], axis=0)
    row, lane = iota((MEMBERS, MEMBERS), 0), iota((MEMBERS, MEMBERS), 1)
    x = g * (1.0 / MEMBERS) + jnp.where(row == lane, 1.0, 0.0)
    x = inverse(x)
    shift = jnp.sum(x * d, axis=1, keepdims=True) * (1.0 / MEMBERS)
    z = x + shift
    return z - jnp.mean(z, axis=0, keepdims=True) + 1.0 / MEMBERS


def second_run(pos, mine, other, fr, fo, table, weights, observed, k1, keep, send, FR, FO, H, U, V):
    k = weights_of(pos, mine[...], other[...])
    k1[...] = k
    for src, out in ((fr, FR), (fo, FO)):
        new = jnp.dot(src[...].reshape(EXT * WIDE, MEMBERS), k, precision=HIGHEST, preferred_element_type=F32)
        out[...] = new.reshape(EXT, WIDE, MEMBERS)
    forward(pos[0], table[...], FR, FO, H, U, V)
    gram(pos, H, weights[1], observed[1], keep, send)


def last_update(pos, mine, other, k1, own_p, other_p, out):
    k = jnp.dot(k1[...], weights_of(pos, mine[...], other[...]), precision=HIGHEST, preferred_element_type=F32)

    def emit(low, high, first):
        kt = k.T[first : first + HALF]
        for f in range(2):
            for r in range(ROWS):
                start = f * HALF * ROWS + r
                block = jnp.concatenate(
                    [low[pl.ds(start, HALF, stride=ROWS), :], high[pl.ds(start, HALF, stride=ROWS), :]],
                    axis=0,
                )
                out[pl.ds(start, HALF, stride=ROWS), :] = jnp.dot(
                    kt, block, precision=HIGHEST, preferred_element_type=F32
                )

    @pl.when(pos[1] == 0)
    def _():
        emit(own_p, other_p, 0)

    @pl.when(pos[1] == 1)
    def _():
        emit(other_p, own_p, HALF)


def swap(value):
    return lax.ppermute(value, "ens", [(0, 1), (1, 0)])


def moved(value, axes, by):
    n = lax.axis_size(axes)
    return lax.ppermute(value, axes, [(i, (i + by) % n) for i in range(n)])


def exchanged(value, axis, bits):
    n = lax.axis_size(axis)
    masks = [0]
    for bit in bits:
        masks += [m | bit for m in masks]
    terms = [value] + [lax.ppermute(value, axis, [(i, i ^ m) for i in range(n)]) for m in masks[1:]]
    while len(terms) > 1:
        terms = [a + b for a, b in zip(terms[::2], terms[1::2])]
    return terms[0]


def reduced(keep, send):
    value = keep + swap(send)
    for axis, bits in (("lat_0", (1, 2)), ("lat_1", (1, 2)), ("lon", (1,)), ("lon", (2, 4))):
        value = exchanged(value, axis, bits)
    return value, swap(value)


def call(kernel, out_shape, scalars, *args, scratch=()):
    return pl.pallas_call(
        kernel,
        out_shape=out_shape,
        in_specs=[SMEM] + [VMEM] * len(args),
        out_specs=jax.tree.map(lambda _: VMEM, out_shape),
        scratch_shapes=list(scratch),
        compiler_params=params(),
    )(scalars, *args)


def per_device(parameters, initial_height, initial_speed, obs_slots, obs_values, obs_precision):
    pos = jnp.stack([lax.axis_index(LAT), lax.axis_index("ens")]).astype(jnp.int32)
    own_p = parameters.reshape(2 * HALF * ROWS, COLS)
    other_p = swap(own_p)
    by_slot = [x[:, 0].transpose(0, 2, 1).reshape(16, 128) for x in (obs_slots, obs_values, obs_precision)]

    own, up2, dn2, obs = call(
        spread_members,
        [shape(OWN + INIT, 128), shape(216, 128), shape(216, 128), shape(128, 128)],
        pos, own_p, other_p, initial_height, initial_speed.reshape(16, COLS), by_slot[1], by_slot[2],
    )
    m2, p2 = moved(up2, LAT, 2), moved(dn2, LAT, -2)
    m1, p1 = moved(own, LAT, 1), moved(own, LAT, -1)

    obs = lax.all_to_all(obs, LAT_LON, 0, 0, tiled=True)
    weights, observed = call(scatter_obs, [shape(2, 512, 128), shape(2, 512, 128)], pos, by_slot[0], obs)

    right, left = pl.pallas_call(
        pack_edges,
        out_shape=[shape(EDGE, 128)] * 2,
        in_specs=[VMEM] * 6,
        out_specs=[VMEM] * 2,
        compiler_params=params(),
    )(own, m1, p1, m2, p2, weights)
    lz, rz = moved(right, LON_ENS, 1), moved(left, LON_ENS, -1)

    field = shape(EXT, WIDE, MEMBERS)
    half = shape(40, MEMBERS)
    square = shape(MEMBERS, MEMBERS)
    state = [pltpu.VMEM((EXT, WIDE, MEMBERS), F32)]
    ext_fr, ext_fo, table, keep, send = call(
        first_run, [field, field, square, half, half],
        pos, own, m1, p1, m2, p2, lz, rz, weights, observed,
        scratch=state * 3,
    )
    mine, other = reduced(keep, send)
    k1, keep, send = call(
        second_run, [square, half, half],
        pos, mine, other, ext_fr, ext_fo, table, weights, observed,
        scratch=state * 5,
    )
    mine, other = reduced(keep, send)
    out = call(last_update, shape(2 * HALF * ROWS, COLS), pos, mine, other, k1, own_p, other_p)
    return out.reshape(parameters.shape)


def solution(mesh):
    torus = Mesh(
        mesh.devices.reshape(4, 4, mesh.shape["lon"], mesh.shape["ens"]),
        ("lat_0", "lat_1", "lon", "ens"),
    )
    in_specs = (
        P(None, "ens", LAT, "lon"),
        P(LAT, "lon"),
        P(None, LAT, "lon"),
        P(None, LAT_LON, None, None),
        P(None, LAT_LON, None, None),
        P(None, LAT_LON, None, None),
    )
    out_specs = P(None, "ens", LAT, "lon")
    return jax.shard_map(
        per_device, mesh=torus, in_specs=in_specs, out_specs=out_specs, check_vma=False
    )
```

```python
import functools

import jax
import jax.numpy as jnp
from jax import lax
from jax.experimental import pallas as pl
from jax.experimental.pallas import tpu as pltpu
from jax.sharding import Mesh
from jax.sharding import PartitionSpec as P

STEPS = 6
LAT = ("lat_0", "lat_1")
LAT_LON = ("lat_0", "lat_1", "lon")
LON_ENS = ("lon", "ens")

DEPTH = 0.7
GRAVITY = 0.7
CORIOLIS = 0.1

MEMBERS = 128
HALF = 64
ROWS = 8
COLS = 128
EXT = 28
WIDE = 112
LEFT = 24
RIGHT = LEFT + HALF
INIT = 24
GLOBAL_ROWS = 128
OWN = 2 * ROWS * HALF
PIVOTS = 16

F32 = jnp.float32
HIGHEST = lax.Precision.HIGHEST
VMEM = pl.BlockSpec(memory_space=pltpu.VMEM)
SMEM = pl.BlockSpec(memory_space=pltpu.SMEM)


def params():
    return pltpu.CompilerParams(vmem_limit_bytes=24 * 1024 * 1024)


def shape(*dims):
    return jax.ShapeDtypeStruct(dims, F32)


def iota(dims, axis):
    return lax.broadcasted_iota(jnp.int32, dims, axis)


def gather_small(height, speed, values, precision, own, fields, obs):
    del own
    fields[:ROWS] = height[...]
    fields[ROWS:] = speed[...]
    lines = [values[...], precision[...], jnp.zeros((96, MEMBERS), F32)]
    by_owner = jnp.concatenate(lines, axis=0).T
    for x in range(4):
        parts = [by_owner[(4 * x + y) * 8 : (4 * x + y + 1) * 8] for y in range(4)]
        obs[8 * x : 8 * x + 8] = (
            parts[0] + pltpu.roll(parts[1], 32, 1) + pltpu.roll(parts[2], 64, 1) + pltpu.roll(parts[3], 96, 1)
        )


def spread_members(pos, own, other, fields, out, up2, dn2):
    def emit(low, high, first):
        for f in range(2):
            for r in range(ROWS):
                start = f * HALF * ROWS + r
                block = jnp.concatenate(
                    [low[pl.ds(start, HALF, stride=ROWS), :], high[pl.ds(start, HALF, stride=ROWS), :]],
                    axis=0,
                )
                turned = block.T[first : first + HALF]
                at = (f * ROWS + r) * HALF
                out[at : at + HALF] = turned
                if f == 1 and r >= 6:
                    up2[(r - 6) * HALF : (r - 5) * HALF] = turned
                if f == 0 and r == 7:
                    up2[2 * HALF : 3 * HALF] = turned
                if f == 1 and r < 2:
                    dn2[r * HALF : (r + 1) * HALF] = turned
                if f == 0 and r == 0:
                    dn2[2 * HALF : 3 * HALF] = turned

    for ref, at in ((out, OWN), (up2, 3 * HALF), (dn2, 3 * HALF)):
        ref[at : at + INIT] = fields[...]

    @pl.when(pos[1] == 0)
    def _():
        emit(own, other, 0)

    @pl.when(pos[1] == 1)
    def _():
        emit(other, own, HALF)


def edge_rows():
    rows = []
    for field, first in ((1, 0), (0, 1)):
        for r in range(first, EXT - first):
            away = max(10 - r, r - 17, 0)
            need = 9 + field - away
            rows.append((field, r, 16 if need > 8 else 8))
    return rows


EDGE_ROWS = edge_rows()
EDGE = sum(n for _, _, n in EDGE_ROWS)


def row_source(field, r, own, m1, p1, m2, p2):
    at = field * ROWS * HALF
    if 10 <= r < 18:
        return own, at + (r - 10) * HALF
    if 2 <= r < 10:
        return m1, at + (r - 2) * HALF
    if 18 <= r < 26:
        return p1, at + (r - 18) * HALF
    ref = m2 if r < 2 else p2
    if field == 1:
        return ref, (r if r < 2 else r - 26) * HALF
    return ref, 2 * HALF


def initial_tiles(own, m1, p1, m2, p2):
    return ((m2, 3 * HALF), (m1, OWN), (own, OWN), (p1, OWN), (p2, 3 * HALF))


def pack_edges(own, m1, p1, m2, p2, obs, right, left):
    del obs
    at = 0
    for field, r, n in EDGE_ROWS:
        ref, start = row_source(field, r, own, m1, p1, m2, p2)
        right[at : at + n] = ref[start + HALF - n : start + HALF]
        left[at : at + n] = ref[start : start + n]
        at += n
    for ref, start in initial_tiles(own, m1, p1, m2, p2):
        fields = ref[start : start + INIT]
        right[at : at + INIT] = fields
        left[at : at + INIT] = fields
        at += INIT


def scatter_obs(pos, slots, part0, part1, part2, part3, weights, observed):
    y = pos[2]
    parts = [pltpu.roll(part[...], (4 - y) * 32 % COLS, 1) for part in (part0, part1, part2, part3)]
    by_y = []
    for k in range(4):
        m = y ^ k
        by_y.append(jnp.where(m < 2, jnp.where(m == 0, parts[0], parts[1]), jnp.where(m == 2, parts[2], parts[3])))
    tiles = [by_y[k][8 * x : 8 * x + 8] for x in range(4) for k in range(4)]
    received = jnp.concatenate(tiles, axis=0).T
    values, precision = received[:16], received[16:32]
    lines = ROWS * HALF
    k = iota((lines, MEMBERS), 0)
    cell = (k // HALF) * COLS + pos[1] * HALF + k % HALF
    for t in range(2):
        found_w = jnp.zeros((lines, MEMBERS), F32)
        found_y = jnp.zeros((lines, MEMBERS), F32)
        for s in range(8):
            at = t * 8 + s
            hit = cell == slots[at : at + 1, :]
            found_w = found_w + jnp.where(hit, precision[at : at + 1, :], 0.0)
            found_y = found_y + jnp.where(hit, values[at : at + 1, :], 0.0)
        weights[t] = jnp.broadcast_to(jnp.sum(found_w, axis=1, keepdims=True), (lines, MEMBERS))
        observed[t] = jnp.broadcast_to(jnp.sum(found_y, axis=1, keepdims=True), (lines, MEMBERS))


def inside(lat, r):
    row = lat * ROWS + r - 10
    return jnp.logical_and(row >= 0, row < GLOBAL_ROWS)


def initial_table(pos, tiles, lz, rz):
    lane = iota((ROWS, COLS), 1)
    row = iota((ROWS, COLS), 0)
    e = pos[1]
    fields = [[], [], []]
    for k, (ref, start) in enumerate(tiles):
        for f in range(3):
            own = ref[start + f * ROWS : start + (f + 1) * ROWS]
            at = EDGE + k * INIT + f * ROWS
            before = lz[at : at + ROWS]
            after = rz[at : at + ROWS]
            low = pltpu.roll(jnp.where(lane >= 112, before, own), 16, 1)
            high = pltpu.roll(jnp.where(lane < 16, after, own), 80, 1)
            window = jnp.where(e == 0, low, high)
            place = pos[0] * ROWS + (k - 2) * ROWS + row
            ok = jnp.logical_and(place >= 0, place < GLOBAL_ROWS)
            fields[f].append(jnp.where(ok, window, 0.0))
    h, u, v = (jnp.concatenate(f, axis=0) for f in fields)
    east = pltpu.roll(u, COLS - 1, 1) - pltpu.roll(u, 1, 1)
    north = jnp.concatenate([v[1:], v[:1]], axis=0) - jnp.concatenate([v[-1:], v[:-1]], axis=0)
    place = pos[0] * ROWS - 16 + iota((40, COLS), 0)
    ok = jnp.logical_and(place >= 0, place < GLOBAL_ROWS)
    base = jnp.where(ok, h - DEPTH * (east + north), 0.0)
    return jnp.concatenate([base, u, v, jnp.zeros((8, COLS), F32)], axis=0).T


def forward(lat, table, FR, FO, H, U, V):
    first = table[0:96]

    def start(f, r):
        lane = f * 40 + r + 6
        return jnp.broadcast_to(first[:, lane : lane + 1], (96, MEMBERS))

    def gains(r):
        ok = inside(lat, r)
        return jnp.where(ok, F32(GRAVITY), F32(0.0)), jnp.where(ok, F32(CORIOLIS), F32(0.0))

    for r in range(EXT):
        H[r, 8:104] = start(0, r) + FO[r, 8:104]
    for r in range(1, EXT - 1):
        g, c = gains(r)
        u, v = start(1, r), start(2, r)
        keep = 1.0 - FR[r, 8:104]
        U[r, 8:104] = keep * u - g * (H[r, 9:105] - H[r, 7:103]) + c * v
        V[r, 8:104] = keep * v - g * (H[r + 1, 8:104] - H[r - 1, 8:104]) - c * u

    def height_row(a, b, r):
        g, _ = gains(r)
        n = b - a
        east = U[r, pl.ds(a + 1, n)] - U[r, pl.ds(a - 1, n)]
        north = V[r + 1, pl.ds(a, n)] - V[r - 1, pl.ds(a, n)]
        H[r, pl.ds(a, n)] = H[r, pl.ds(a, n)] - g * (east + north) + FO[r, pl.ds(a, n)]

    def speed_row(a, b, r):
        g, c = gains(r)
        n = b - a
        u, v = U[r, pl.ds(a, n)], V[r, pl.ds(a, n)]
        keep = 1.0 - FR[r, pl.ds(a, n)]
        east = H[r, pl.ds(a + 1, n)] - H[r, pl.ds(a - 1, n)]
        north = H[r + 1, pl.ds(a, n)] - H[r - 1, pl.ds(a, n)]
        U[r, pl.ds(a, n)] = keep * u - g * east + c * v
        V[r, pl.ds(a, n)] = keep * v - g * north - c * u

    def sweep(row, reach, a, b):
        def body(i, carry):
            row(a, b, 10 - reach + 2 * i)
            row(a, b, 11 - reach + 2 * i)
            return carry

        lax.fori_loop(0, (ROWS + 2 * reach) // 2, body, 0)

    for step in range(1, STEPS):
        reach = 2 * (STEPS - 1 - step)
        a, b = (16, 96) if reach else (LEFT, RIGHT)
        sweep(height_row, reach, a, b)
        if reach:
            sweep(speed_row, reach - 1, a, b)


def gram(H, weights, observed, total):
    lines = ROWS * HALF
    h = H[10:18, LEFT:RIGHT].reshape(lines, MEMBERS)
    centre = jnp.mean(h, axis=1, keepdims=True)
    spread = h - centre
    weighted = spread * weights
    g = lax.dot_general(spread, weighted, (((0,), (0,)), ((), ())), precision=HIGHEST, preferred_element_type=F32)
    d = jnp.sum(weighted * (observed - centre), axis=0, keepdims=True)
    row, lane = iota((HALF, MEMBERS), 0), iota((HALF, MEMBERS), 1)
    top, bottom = g[:HALF], g[HALF:]
    packed = jnp.where(jnp.logical_and(lane < HALF, lane > row), pltpu.roll(bottom, HALF, 1), top)
    diagonal = jnp.sum(jnp.where(lane == row + HALF, bottom, 0.0), axis=0, keepdims=True)
    line = iota((8, MEMBERS), 0)
    rest = jnp.where(line == 0, d, jnp.where(line == 1, diagonal, 0.0))
    total[...] = jnp.concatenate([packed, rest], axis=0)


def first_run(pos, own, m1, p1, m2, p2, lz, rz, weights, observed, FR, FO, table, total, H, U, V):
    at = 0
    for field, r, n in EDGE_ROWS:
        ref, begin = row_source(field, r, own, m1, p1, m2, p2)
        west, middle, east = lz[at : at + n], ref[begin : begin + HALF], rz[at : at + n]
        at += n
        if field == 1 and not 10 <= r < 18:
            ok = inside(pos[0], r)
            west, middle, east = (jnp.where(ok, x, 0.0) for x in (west, middle, east))
        out = FO if field else FR
        out[r, LEFT - n : LEFT] = west
        out[r, LEFT:RIGHT] = middle
        out[r, RIGHT : RIGHT + n] = east
    table[...] = initial_table(pos, initial_tiles(own, m1, p1, m2, p2), lz, rz)
    forward(pos[0], table[...], FR, FO, H, U, V)
    gram(H, weights[0], observed[0], total)


def inverse(x):
    n = PIVOTS
    panels = [x[k : k + n] for k in range(0, MEMBERS, n)]
    row, lane = iota((n, MEMBERS), 0), iota((n, MEMBERS), 1)
    lower, scaled = [], []

    def spread(panel, column):
        return jnp.broadcast_to(panel[:, column : column + 1], (n, MEMBERS))

    for k in range(len(panels)):
        first = k * n
        block = jnp.logical_and(lane >= first, lane < first + n)
        columns = [spread(panels[k], first + j) for j in range(n)]
        top = jnp.where(block, jnp.where(lane - first == row, 1.0, 0.0), panels[k])
        lower.append(jnp.where(lane < first + n, top, 0.0))
        for j in range(n):
            over = 1.0 / columns[j][j : j + 1]

            def eliminate(m, j=j, over=over):
                pivot = m[j : j + 1] * over
                return jnp.where(row == j, pivot, m - columns[j] * pivot)

            top = eliminate(top)
            columns[j + 1 :] = [eliminate(m) for m in columns[j + 1 :]]
        scaled.append(jnp.where(lane < first + n, top, 0.0))
        for i in range(k + 1, len(panels)):
            terms = [spread(panels[i], first + j) * top[j : j + 1] for j in range(n)]
            while len(terms) > 1:
                terms = [a + b for a, b in zip(terms[::2], terms[1::2])]
            panels[i] = jnp.where(block, 0.0, panels[i]) - terms[0]
    lower, scaled = jnp.concatenate(lower, axis=0), jnp.concatenate(scaled, axis=0)
    return lax.dot_general(lower, scaled, (((0,), (0,)), ((), ())), precision=HIGHEST, preferred_element_type=F32)


def weights_of(pos, mine, other):
    total = jnp.where(pos[1] == 1, mine, other)
    packed, d, diagonal = total[:HALF], total[HALF : HALF + 1], total[HALF + 1 : HALF + 2]
    turned = jnp.concatenate([packed, jnp.zeros((HALF, MEMBERS), F32)], axis=0).T
    row, lane = iota((HALF, MEMBERS), 0), iota((HALF, MEMBERS), 1)
    a = jnp.where(lane <= row, packed, turned[:HALF])
    c = pltpu.roll(jnp.where(lane > row, packed, turned[:HALF]), HALF, 1)
    c = jnp.where(lane == row + HALF, diagonal, c)
    top = jnp.where(lane < HALF, a, packed)
    bottom = jnp.where(lane < HALF, turned[HALF:], c)
    g = jnp.concatenate([top, bottom], axis=0)
    row, lane = iota((MEMBERS, MEMBERS), 0), iota((MEMBERS, MEMBERS), 1)
    x = g * (1.0 / MEMBERS) + jnp.where(row == lane, 1.0, 0.0)
    x = inverse(x)
    shift = jnp.sum(x * d, axis=1, keepdims=True) * (1.0 / MEMBERS)
    z = x + shift
    return z - jnp.mean(z, axis=0, keepdims=True) + 1.0 / MEMBERS


def second_run(pos, mine, other, fr, fo, table, weights, observed, k1, total, FR, FO, H, U, V):
    k = weights_of(pos, mine[...], other[...])
    k1[...] = k
    for src, out in ((fr, FR), (fo, FO)):
        new = jnp.dot(src[...].reshape(EXT * WIDE, MEMBERS), k, precision=HIGHEST, preferred_element_type=F32)
        out[...] = new.reshape(EXT, WIDE, MEMBERS)
    forward(pos[0], table[...], FR, FO, H, U, V)
    gram(H, weights[1], observed[1], total)


def last_update(pos, mine, other, k1, own_p, other_p, out):
    k = jnp.dot(k1[...], weights_of(pos, mine[...], other[...]), precision=HIGHEST, preferred_element_type=F32)

    def emit(low, high, first):
        kt = k.T[first : first + HALF]
        for f in range(2):
            for r in range(ROWS):
                start = f * HALF * ROWS + r
                block = jnp.concatenate(
                    [low[pl.ds(start, HALF, stride=ROWS), :], high[pl.ds(start, HALF, stride=ROWS), :]],
                    axis=0,
                )
                out[pl.ds(start, HALF, stride=ROWS), :] = jnp.dot(
                    kt, block, precision=HIGHEST, preferred_element_type=F32
                )

    @pl.when(pos[1] == 0)
    def _():
        emit(own_p, other_p, 0)

    @pl.when(pos[1] == 1)
    def _():
        emit(other_p, own_p, HALF)


def swap(value):
    return lax.ppermute(value, "ens", [(0, 1), (1, 0)])


def moved(value, axes, by):
    n = lax.axis_size(axes)
    return lax.ppermute(value, axes, [(i, (i + by) % n) for i in range(n)])


def exchanged(value, axis, bits):
    masks = [0]
    for bit in bits:
        masks += [m | bit for m in masks]
    terms = [value]
    for m in masks[1:]:
        pairs = [(2 * i + 1, 2 * (i ^ m) + 1) for i in range(lax.axis_size(axis))]
        terms.append(lax.ppermute(value, (axis, "ens"), pairs))
    while len(terms) > 1:
        terms = [a + b for a, b in zip(terms[::2], terms[1::2])]
    return terms[0]


def reduced(total):
    value = total + lax.ppermute(total, "ens", [(0, 1)])
    for axis, bits in (("lat_0", (1, 2)), ("lat_1", (1, 2)), ("lon", (1,)), ("lon", (2, 4))):
        value = exchanged(value, axis, bits)
    return value, lax.ppermute(value, "ens", [(1, 0)])


def call(kernel, out_shape, scalars, *args, scratch=()):
    scalars = [] if scalars is None else [scalars]
    return pl.pallas_call(
        kernel,
        out_shape=out_shape,
        in_specs=[SMEM] * len(scalars) + [VMEM] * len(args),
        out_specs=jax.tree.map(lambda _: VMEM, out_shape),
        scratch_shapes=list(scratch),
        compiler_params=params(),
    )(*scalars, *args)


def per_device(parameters, initial_height, initial_speed, obs_slots, obs_values, obs_precision):
    pos = jnp.stack([lax.axis_index(a) for a in (LAT, "ens", "lat_1")]).astype(jnp.int32)
    own_p = parameters.reshape(2 * HALF * ROWS, COLS)
    other_p = swap(own_p)
    by_slot = [x[:, 0].transpose(0, 2, 1).reshape(16, 128) for x in (obs_slots, obs_values, obs_precision)]

    fields, obs = call(
        gather_small, [shape(INIT, 128), shape(32, 128)],
        None, initial_height, initial_speed.reshape(16, COLS), by_slot[1], by_slot[2], own_p,
    )
    own, up2, dn2 = call(
        spread_members, [shape(OWN + INIT, 128), shape(216, 128), shape(216, 128)], pos, own_p, other_p, fields
    )
    m2, p2 = moved(up2, LAT, 2), moved(dn2, LAT, -2)
    m1, p1 = moved(own, LAT, 1), moved(own, LAT, -1)

    obs = lax.all_to_all(obs, ("lat_0", "lon"), 0, 0, tiled=True)
    parts = [obs] + [lax.ppermute(obs, "lat_1", [(i, i ^ m) for i in range(4)]) for m in (1, 2, 3)]
    weights, observed = call(scatter_obs, [shape(2, 512, 128), shape(2, 512, 128)], pos, by_slot[0], *parts)

    edge = shape(EDGE + 5 * INIT, 128)
    right, left = call(pack_edges, [edge, edge], None, own, m1, p1, m2, p2, obs)
    lz, rz = moved(right, LON_ENS, 1), moved(left, LON_ENS, -1)

    field = shape(EXT, WIDE, MEMBERS)
    sums = shape(HALF + 8, MEMBERS)
    square = shape(MEMBERS, MEMBERS)
    state = [pltpu.VMEM((EXT, WIDE, MEMBERS), F32)]
    ext_fr, ext_fo, table, total = call(
        first_run, [field, field, square, sums],
        pos, own, m1, p1, m2, p2, lz, rz, weights, observed,
        scratch=state * 3,
    )
    mine, other = reduced(total)
    k1, total = call(
        second_run, [square, sums],
        pos, mine, other, ext_fr, ext_fo, table, weights, observed,
        scratch=state * 5,
    )
    mine, other = reduced(total)
    out = call(last_update, shape(2 * HALF * ROWS, COLS), pos, mine, other, k1, own_p, other_p)
    return out.reshape(parameters.shape)


def solution(mesh):
    torus = Mesh(
        mesh.devices.reshape(4, 4, mesh.shape["lon"], mesh.shape["ens"]),
        ("lat_0", "lat_1", "lon", "ens"),
    )
    in_specs = (
        P(None, "ens", LAT, "lon"),
        P(LAT, "lon"),
        P(None, LAT, "lon"),
        P(None, LAT_LON, None, None),
        P(None, LAT_LON, None, None),
        P(None, LAT_LON, None, None),
    )
    out_specs = P(None, "ens", LAT, "lon")
    return jax.shard_map(
        per_device, mesh=torus, in_specs=in_specs, out_specs=out_specs, check_vma=False
    )
```

```python
import functools

import jax
import jax.numpy as jnp
from jax import lax
from jax.experimental import pallas as pl
from jax.experimental.pallas import tpu as pltpu
from jax.sharding import Mesh
from jax.sharding import PartitionSpec as P

STEPS = 6
LAT = ("lat_0", "lat_1")
LAT_LON = ("lat_0", "lat_1", "lon")
LON_ENS = ("lon", "ens")

DEPTH = 0.7
GRAVITY = 0.7
CORIOLIS = 0.1

MEMBERS = 128
HALF = 64
ROWS = 8
COLS = 128
EXT = 28
WIDE = 112
LEFT = 24
RIGHT = LEFT + HALF
INIT = 24
GLOBAL_ROWS = 128
OWN = 2 * ROWS * HALF
PIVOTS = 16

F32 = jnp.float32
HIGHEST = lax.Precision.HIGHEST
VMEM = pl.BlockSpec(memory_space=pltpu.VMEM)
SMEM = pl.BlockSpec(memory_space=pltpu.SMEM)


def params():
    return pltpu.CompilerParams(vmem_limit_bytes=24 * 1024 * 1024)


def shape(*dims):
    return jax.ShapeDtypeStruct(dims, F32)


def iota(dims, axis):
    return lax.broadcasted_iota(jnp.int32, dims, axis)


def collect(own_hbm, height_hbm, speed_hbm, values_hbm, precision_hbm,
            out, up2, dn2, obs, values, precision, sems):
    pairs = (
        (values_hbm, values), (precision_hbm, precision), (own_hbm, out.at[:OWN]),
        (height_hbm, out.at[OWN : OWN + ROWS]), (speed_hbm, out.at[OWN + ROWS :]),
    )
    copies = [pltpu.make_async_copy(src, dst, sems.at[k]) for k, (src, dst) in enumerate(pairs)]
    for copy in copies:
        copy.start()
    for copy in copies[:2]:
        copy.wait()
    lines = [values[...], precision[...], jnp.zeros((96, MEMBERS), F32)]
    obs[...] = jnp.concatenate(lines, axis=0).T
    for copy in copies[2:]:
        copy.wait()
    for k, (f, up_row, down_row) in enumerate(((1, 6, 0), (1, 7, 1), (0, 7, 0))):
        start = f * HALF * ROWS
        up2[k * HALF : (k + 1) * HALF] = out[pl.ds(start + up_row, HALF, stride=ROWS), :]
        dn2[k * HALF : (k + 1) * HALF] = out[pl.ds(start + down_row, HALF, stride=ROWS), :]
    up2[3 * HALF :] = out[OWN:]
    dn2[3 * HALF :] = out[OWN:]


def edge_rows():
    rows = []
    for field, first in ((1, 0), (0, 1)):
        for r in range(first, EXT - first):
            away = max(10 - r, r - 17, 0)
            need = 9 + field - away
            rows.append((field, r, 16 if need > 8 else 8))
    return rows


EDGE_ROWS = edge_rows()
EDGE = sum(n for _, _, n in EDGE_ROWS)


def turn_rows(pos, own, m1, p1, m2, p2, own_o, m1_o, p1_o, m2_o, p2_o, FR, FO, tiles, right, left):
    def row_source(field, r):
        if 2 <= r < 26:
            which = (r - 2) // ROWS
            return (m1, own, p1)[which], (m1_o, own_o, p1_o)[which], field * HALF * ROWS + (r - 2) % ROWS, ROWS
        k = 2 if field == 0 else (r if r < 2 else r - 26)
        refs = (m2, m2_o) if r < 2 else (p2, p2_o)
        return *refs, k * HALF, 1

    def emit(first):
        at = 0
        for field, r, n in EDGE_ROWS:
            mine, others, start, stride = row_source(field, r)
            low, high = (mine, others) if first == 0 else (others, mine)
            lines = pl.ds(start, HALF, stride=stride)
            turned = jnp.concatenate([low[lines, :], high[lines, :]], axis=0).T[first : first + HALF]
            if field == 1 and not 10 <= r < 18:
                turned = jnp.where(inside(pos[0], r), turned, 0.0)
            (FO if field else FR)[r, LEFT:RIGHT] = turned
            right[at : at + n] = turned[HALF - n :]
            left[at : at + n] = turned[:n]
            at += n

    fields = ((m2, 3 * HALF), (m1, OWN), (own, OWN), (p1, OWN), (p2, 3 * HALF))
    for k, (ref, start) in enumerate(fields):
        tile = ref[start : start + INIT]
        for out, at in ((tiles, 0), (right, EDGE), (left, EDGE)):
            out[at + k * INIT : at + (k + 1) * INIT] = tile

    @pl.when(pos[1] == 0)
    def _():
        emit(0)

    @pl.when(pos[1] == 1)
    def _():
        emit(HALF)


def scatter_obs(pos, slots, received, weights, observed):
    received = received[...].T
    values, precision = received[:16], received[16:32]
    lines = ROWS * HALF
    k = iota((lines, MEMBERS), 0)
    cell = (k // HALF) * COLS + pos[1] * HALF + k % HALF
    for t in range(2):
        found_w = jnp.zeros((lines, MEMBERS), F32)
        found_y = jnp.zeros((lines, MEMBERS), F32)
        for s in range(8):
            at = t * 8 + s
            hit = cell == slots[at : at + 1, :]
            found_w = found_w + jnp.where(hit, precision[at : at + 1, :], 0.0)
            found_y = found_y + jnp.where(hit, values[at : at + 1, :], 0.0)
        weights[t] = jnp.broadcast_to(jnp.sum(found_w, axis=1, keepdims=True), (lines, MEMBERS))
        observed[t] = jnp.broadcast_to(jnp.sum(found_y, axis=1, keepdims=True), (lines, MEMBERS))


def inside(lat, r):
    row = lat * ROWS + r - 10
    return jnp.logical_and(row >= 0, row < GLOBAL_ROWS)


def initial_table(pos, tiles, lz, rz):
    lane = iota((ROWS, COLS), 1)
    row = iota((ROWS, COLS), 0)
    e = pos[1]
    fields = [[], [], []]
    for k in range(5):
        for f in range(3):
            at = k * INIT + f * ROWS
            own = tiles[at : at + ROWS]
            at += EDGE
            before = lz[at : at + ROWS]
            after = rz[at : at + ROWS]
            low = pltpu.roll(jnp.where(lane >= 112, before, own), 16, 1)
            high = pltpu.roll(jnp.where(lane < 16, after, own), 80, 1)
            window = jnp.where(e == 0, low, high)
            place = pos[0] * ROWS + (k - 2) * ROWS + row
            ok = jnp.logical_and(place >= 0, place < GLOBAL_ROWS)
            fields[f].append(jnp.where(ok, window, 0.0))
    h, u, v = (jnp.concatenate(f, axis=0) for f in fields)
    east = pltpu.roll(u, COLS - 1, 1) - pltpu.roll(u, 1, 1)
    north = jnp.concatenate([v[1:], v[:1]], axis=0) - jnp.concatenate([v[-1:], v[:-1]], axis=0)
    place = pos[0] * ROWS - 16 + iota((40, COLS), 0)
    ok = jnp.logical_and(place >= 0, place < GLOBAL_ROWS)
    base = jnp.where(ok, h - DEPTH * (east + north), 0.0)
    return jnp.concatenate([base, u, v, jnp.zeros((8, COLS), F32)], axis=0).T


def forward(lat, table, FR, FO, H, U, V):
    first = table[0:96]

    def start(f, r):
        lane = f * 40 + r + 6
        return jnp.broadcast_to(first[:, lane : lane + 1], (96, MEMBERS))

    def gains(r):
        ok = inside(lat, r)
        return jnp.where(ok, F32(GRAVITY), F32(0.0)), jnp.where(ok, F32(CORIOLIS), F32(0.0))

    for r in range(EXT):
        H[r, 8:104] = start(0, r) + FO[r, 8:104]
    for r in range(1, EXT - 1):
        g, c = gains(r)
        u, v = start(1, r), start(2, r)
        keep = 1.0 - FR[r, 8:104]
        U[r, 8:104] = keep * u - g * (H[r, 9:105] - H[r, 7:103]) + c * v
        V[r, 8:104] = keep * v - g * (H[r + 1, 8:104] - H[r - 1, 8:104]) - c * u

    def height_row(a, b, r):
        g, _ = gains(r)
        n = b - a
        east = U[r, pl.ds(a + 1, n)] - U[r, pl.ds(a - 1, n)]
        north = V[r + 1, pl.ds(a, n)] - V[r - 1, pl.ds(a, n)]
        H[r, pl.ds(a, n)] = H[r, pl.ds(a, n)] - g * (east + north) + FO[r, pl.ds(a, n)]

    def speed_row(a, b, r):
        g, c = gains(r)
        n = b - a
        u, v = U[r, pl.ds(a, n)], V[r, pl.ds(a, n)]
        keep = 1.0 - FR[r, pl.ds(a, n)]
        east = H[r, pl.ds(a + 1, n)] - H[r, pl.ds(a - 1, n)]
        north = H[r + 1, pl.ds(a, n)] - H[r - 1, pl.ds(a, n)]
        U[r, pl.ds(a, n)] = keep * u - g * east + c * v
        V[r, pl.ds(a, n)] = keep * v - g * north - c * u

    def sweep(row, reach, a, b):
        def body(i, carry):
            row(a, b, 10 - reach + 2 * i)
            row(a, b, 11 - reach + 2 * i)
            return carry

        lax.fori_loop(0, (ROWS + 2 * reach) // 2, body, 0)

    for step in range(1, STEPS):
        reach = 2 * (STEPS - 1 - step)
        a, b = (16, 96) if reach else (LEFT, RIGHT)
        sweep(height_row, reach, a, b)
        if reach:
            sweep(speed_row, reach - 1, a, b)


def gram(pos, H, weights, observed, keep, send):
    lines = ROWS * HALF
    h = H[10:18, LEFT:RIGHT].reshape(lines, MEMBERS)
    centre = jnp.mean(h, axis=1, keepdims=True)
    spread = h - centre
    weighted = spread * weights
    g = lax.dot_general(spread, weighted, (((0,), (0,)), ((), ())), precision=HIGHEST, preferred_element_type=F32)
    d = jnp.sum(weighted * (observed - centre), axis=0, keepdims=True)
    row, lane = iota((HALF, MEMBERS), 0), iota((HALF, MEMBERS), 1)
    top, bottom = g[:HALF], g[HALF:]
    packed = jnp.where(jnp.logical_and(lane < HALF, lane > row), pltpu.roll(bottom, HALF, 1), top)
    diagonal = jnp.sum(jnp.where(lane == row + HALF, bottom, 0.0), axis=0, keepdims=True)
    line = iota((8, MEMBERS), 0)
    rest = jnp.where(line == 0, d, jnp.where(line == 1, diagonal, 0.0))
    one = jnp.concatenate([packed[:32], rest], axis=0)
    two = jnp.concatenate([packed[32:], jnp.zeros((8, MEMBERS), F32)], axis=0)
    keep[...] = jnp.where(pos[1] == 0, one, two)
    send[...] = jnp.where(pos[1] == 0, two, one)


def first_run(pos, fr, fo, tiles, lz, rz, weights, observed, FR, FO, table, keep, send, H, U, V):
    del fr, fo
    at = 0
    for field, r, n in EDGE_ROWS:
        out = FO if field else FR
        out[r, LEFT - n : LEFT] = lz[at : at + n]
        out[r, RIGHT : RIGHT + n] = rz[at : at + n]
        at += n
    table[...] = initial_table(pos, tiles, lz, rz)
    forward(pos[0], table[...], FR, FO, H, U, V)
    gram(pos, H, weights[0], observed[0], keep, send)


def inverse(x):
    n = PIVOTS
    panels = [x[k : k + n] for k in range(0, MEMBERS, n)]
    row, lane = iota((n, MEMBERS), 0), iota((n, MEMBERS), 1)
    lower, scaled = [], []

    def spread(panel, column):
        return jnp.broadcast_to(panel[:, column : column + 1], (n, MEMBERS))

    for k in range(len(panels)):
        first = k * n
        block = jnp.logical_and(lane >= first, lane < first + n)
        columns = [spread(panels[k], first + j) for j in range(n)]
        top = jnp.where(block, jnp.where(lane - first == row, 1.0, 0.0), panels[k])
        lower.append(jnp.where(lane < first + n, top, 0.0))
        for j in range(n):
            over = 1.0 / columns[j][j : j + 1]

            def eliminate(m, j=j, over=over):
                pivot = m[j : j + 1] * over
                return jnp.where(row == j, pivot, m - columns[j] * pivot)

            top = eliminate(top)
            columns[j + 1 :] = [eliminate(m) for m in columns[j + 1 :]]
        scaled.append(jnp.where(lane < first + n, top, 0.0))
        for i in range(k + 1, len(panels)):
            terms = [spread(panels[i], first + j) * top[j : j + 1] for j in range(n)]
            while len(terms) > 1:
                terms = [a + b for a, b in zip(terms[::2], terms[1::2])]
            panels[i] = jnp.where(block, 0.0, panels[i]) - terms[0]
    lower, scaled = jnp.concatenate(lower, axis=0), jnp.concatenate(scaled, axis=0)
    return lax.dot_general(lower, scaled, (((0,), (0,)), ((), ())), precision=HIGHEST, preferred_element_type=F32)


def weights_of(pos, mine, other):
    one = jnp.where(pos[1] == 0, mine, other)
    two = jnp.where(pos[1] == 0, other, mine)
    packed = jnp.concatenate([one[:32], two[:32]], axis=0)
    d, diagonal = one[32:33], one[33:34]
    turned = jnp.concatenate([packed, jnp.zeros((HALF, MEMBERS), F32)], axis=0).T
    row, lane = iota((HALF, MEMBERS), 0), iota((HALF, MEMBERS), 1)
    a = jnp.where(lane <= row, packed, turned[:HALF])
    c = pltpu.roll(jnp.where(lane > row, packed, turned[:HALF]), HALF, 1)
    c = jnp.where(lane == row + HALF, diagonal, c)
    top = jnp.where(lane < HALF, a, packed)
    bottom = jnp.where(lane < HALF, turned[HALF:], c)
    g = jnp.concatenate([top, bottom], axis=0)
    row, lane = iota((MEMBERS, MEMBERS), 0), iota((MEMBERS, MEMBERS), 1)
    x = g * (1.0 / MEMBERS) + jnp.where(row == lane, 1.0, 0.0)
    x = inverse(x)
    shift = jnp.sum(x * d, axis=1, keepdims=True) * (1.0 / MEMBERS)
    z = x + shift
    return z - jnp.mean(z, axis=0, keepdims=True) + 1.0 / MEMBERS


def second_run(pos, mine, other, fr, fo, table, weights, observed, k1, keep, send, FR, FO, H, U, V):
    k = weights_of(pos, mine[...], other[...])
    k1[...] = k
    for src, out in ((fr, FR), (fo, FO)):
        new = jnp.dot(src[...].reshape(EXT * WIDE, MEMBERS), k, precision=HIGHEST, preferred_element_type=F32)
        out[...] = new.reshape(EXT, WIDE, MEMBERS)
    forward(pos[0], table[...], FR, FO, H, U, V)
    gram(pos, H, weights[1], observed[1], keep, send)


def last_update(pos, mine, other, k1, own_p, other_p, out):
    k = jnp.dot(k1[...], weights_of(pos, mine[...], other[...]), precision=HIGHEST, preferred_element_type=F32)

    def emit(low, high, first):
        kt = k.T[first : first + HALF]
        for f in range(2):
            for r in range(ROWS):
                start = f * HALF * ROWS + r
                block = jnp.concatenate(
                    [low[pl.ds(start, HALF, stride=ROWS), :], high[pl.ds(start, HALF, stride=ROWS), :]],
                    axis=0,
                )
                out[pl.ds(start, HALF, stride=ROWS), :] = jnp.dot(
                    kt, block, precision=HIGHEST, preferred_element_type=F32
                )

    @pl.when(pos[1] == 0)
    def _():
        emit(own_p, other_p, 0)

    @pl.when(pos[1] == 1)
    def _():
        emit(other_p, own_p, HALF)


def swap(value):
    return lax.ppermute(value, "ens", [(0, 1), (1, 0)])


def moved(value, axes, by):
    n = lax.axis_size(axes)
    return lax.ppermute(value, axes, [(i, (i + by) % n) for i in range(n)])


def exchanged(value, axis, bits):
    n = lax.axis_size(axis)
    masks = [0]
    for bit in bits:
        masks += [m | bit for m in masks]
    terms = [value] + [lax.ppermute(value, axis, [(i, i ^ m) for i in range(n)]) for m in masks[1:]]
    while len(terms) > 1:
        terms = [a + b for a, b in zip(terms[::2], terms[1::2])]
    return terms[0]


def reduced(keep, send):
    value = keep + swap(send)
    for axis, bits in (("lat_0", (1, 2)), ("lat_1", (1, 2)), ("lon", (1,)), ("lon", (2, 4))):
        value = exchanged(value, axis, bits)
    return value, swap(value)


def call(kernel, out_shape, scalars, *args, scratch=(), aliases=None):
    return pl.pallas_call(
        kernel,
        out_shape=out_shape,
        in_specs=[SMEM] + [VMEM] * len(args),
        out_specs=jax.tree.map(lambda _: VMEM, out_shape),
        scratch_shapes=list(scratch),
        input_output_aliases=aliases or {},
        compiler_params=params(),
    )(scalars, *args)


def per_device(parameters, initial_height, initial_speed, obs_slots, obs_values, obs_precision):
    pos = jnp.stack([lax.axis_index(LAT), lax.axis_index("ens")]).astype(jnp.int32)
    own_p = parameters.reshape(2 * HALF * ROWS, COLS)
    slots, values, precision = (
        x[:, 0].transpose(0, 2, 1).reshape(16, 128) for x in (obs_slots, obs_values, obs_precision)
    )
    two_far = shape(3 * HALF + INIT, COLS)
    own, up2, dn2, obs = pl.pallas_call(
        collect,
        out_shape=[shape(OWN + INIT, COLS), two_far, two_far, shape(128, 128)],
        in_specs=[pl.BlockSpec(memory_space=pl.ANY)] * 5,
        out_specs=[VMEM] * 4,
        scratch_shapes=[pltpu.VMEM((16, COLS), F32)] * 2 + [pltpu.SemaphoreType.DMA((5,))],
    )(own_p, initial_height, initial_speed.reshape(16, COLS), values, precision)
    near = [moved(own, LAT, 1), moved(own, LAT, -1)]
    far = [moved(up2, LAT, 2), moved(dn2, LAT, -2)]
    own_other = swap(own)
    obs = lax.all_to_all(obs, LAT_LON, 0, 0, tiled=True)
    *halo, obs = lax.optimization_barrier((*near, *far, obs))
    blocks = [own, *halo]
    others = [own_other] + [swap(x) for x in halo]
    weights, observed = call(scatter_obs, [shape(2, 512, 128), shape(2, 512, 128)], pos, slots, obs)

    field = shape(EXT, WIDE, MEMBERS)
    half = shape(40, MEMBERS)
    square = shape(MEMBERS, MEMBERS)
    edge = shape(EDGE + 5 * INIT, MEMBERS)
    ext_fr, ext_fo, tiles, right, left = call(
        turn_rows, [field, field, shape(5 * INIT, COLS), edge, edge], pos, *blocks, *others
    )
    lz, rz = moved(right, LON_ENS, 1), moved(left, LON_ENS, -1)
    state = [pltpu.VMEM((EXT, WIDE, MEMBERS), F32)]
    ext_fr, ext_fo, table, keep, send = call(
        first_run, [field, field, square, half, half],
        pos, ext_fr, ext_fo, tiles, lz, rz, weights, observed,
        scratch=state * 3, aliases={1: 0, 2: 1},
    )
    mine, other = reduced(keep, send)
    k1, keep, send = call(
        second_run, [square, half, half],
        pos, mine, other, ext_fr, ext_fo, table, weights, observed,
        scratch=state * 5,
    )
    mine, other = reduced(keep, send)
    out = call(last_update, shape(2 * HALF * ROWS, COLS), pos, mine, other, k1, own_p, others[0])
    return out.reshape(parameters.shape)


def solution(mesh):
    torus = Mesh(
        mesh.devices.reshape(4, 4, mesh.shape["lon"], mesh.shape["ens"]),
        ("lat_0", "lat_1", "lon", "ens"),
    )
    in_specs = (
        P(None, "ens", LAT, "lon"),
        P(LAT, "lon"),
        P(None, LAT, "lon"),
        P(None, LAT_LON, None, None),
        P(None, LAT_LON, None, None),
        P(None, LAT_LON, None, None),
    )
    out_specs = P(None, "ens", LAT, "lon")
    return jax.shard_map(
        per_device, mesh=torus, in_specs=in_specs, out_specs=out_specs, check_vma=False
    )
```

```python
import functools

import jax
import jax.numpy as jnp
from jax import lax
from jax.experimental import pallas as pl
from jax.experimental.pallas import tpu as pltpu
from jax.sharding import Mesh
from jax.sharding import PartitionSpec as P

STEPS = 6
LAT = ("lat_0", "lat_1")
LAT_LON = ("lat_0", "lat_1", "lon")
LON_ENS = ("lon", "ens")

DEPTH = 0.7
GRAVITY = 0.7
CORIOLIS = 0.1

MEMBERS = 128
HALF = 64
ROWS = 8
COLS = 128
EXT = 28
WIDE = 112
LEFT = 24
RIGHT = LEFT + HALF
INIT = 24
GLOBAL_ROWS = 128
OWN = 2 * ROWS * HALF
PIVOTS = 16

F32 = jnp.float32
HIGHEST = lax.Precision.HIGHEST
VMEM = pl.BlockSpec(memory_space=pltpu.VMEM)
SMEM = pl.BlockSpec(memory_space=pltpu.SMEM)


def params():
    return pltpu.CompilerParams(vmem_limit_bytes=24 * 1024 * 1024)


def shape(*dims):
    return jax.ShapeDtypeStruct(dims, F32)


def iota(dims, axis):
    return lax.broadcasted_iota(jnp.int32, dims, axis)


def collect(own_hbm, height_hbm, speed_hbm, values_hbm, precision_hbm,
            out, up2, dn2, obs, values, precision, sems):
    pairs = (
        (values_hbm, values), (precision_hbm, precision), (own_hbm, out.at[:OWN]),
        (height_hbm, out.at[OWN : OWN + ROWS]), (speed_hbm, out.at[OWN + ROWS :]),
    )
    copies = [pltpu.make_async_copy(src, dst, sems.at[k]) for k, (src, dst) in enumerate(pairs)]
    for copy in copies:
        copy.start()
    for copy in copies[:2]:
        copy.wait()
    lines = [values[...], precision[...], jnp.zeros((96, MEMBERS), F32)]
    obs[...] = jnp.concatenate(lines, axis=0).T[:, :32]
    for copy in copies[2:]:
        copy.wait()
    for k, (f, up_row, down_row) in enumerate(((1, 6, 0), (1, 7, 1), (0, 7, 0))):
        start = f * HALF * ROWS
        up2[k * HALF : (k + 1) * HALF] = out[pl.ds(start + up_row, HALF, stride=ROWS), :]
        dn2[k * HALF : (k + 1) * HALF] = out[pl.ds(start + down_row, HALF, stride=ROWS), :]
    up2[3 * HALF :] = out[OWN:]
    dn2[3 * HALF :] = out[OWN:]


def edge_rows():
    rows = []
    for field, first in ((1, 0), (0, 1)):
        for r in range(first, EXT - first):
            away = max(10 - r, r - 17, 0)
            need = 9 + field - away
            rows.append((field, r, 16 if need > 8 else 8))
    return rows


EDGE_ROWS = edge_rows()
EDGE = sum(n for _, _, n in EDGE_ROWS)


def both_cores(first, mine, others, start, stride):
    lines = pl.ds(start, HALF, stride=stride)
    mine, others = mine[lines, :], others[lines, :]
    return jnp.concatenate([jnp.where(first, mine, others), jnp.where(first, others, mine)], axis=0)


def turn_rows(pos, own, m1, p1, m2, p2, own_o, m1_o, p1_o, m2_o, p2_o, FR, FO, tiles, right, left):
    def row_source(field, r):
        if 2 <= r < 26:
            which = (r - 2) // ROWS
            return (m1, own, p1)[which], (m1_o, own_o, p1_o)[which], field * HALF * ROWS + (r - 2) % ROWS, ROWS
        k = 2 if field == 0 else (r if r < 2 else r - 26)
        refs = (m2, m2_o) if r < 2 else (p2, p2_o)
        return *refs, k * HALF, 1

    first = pos[1] == 0
    at = 0
    for field, r, n in EDGE_ROWS:
        mine, others, start, stride = row_source(field, r)
        turned = both_cores(first, mine, others, start, stride).T
        turned = jnp.where(first, turned[:HALF], turned[HALF:])
        if field == 1 and not 10 <= r < 18:
            turned = jnp.where(inside(pos[0], r), turned, 0.0)
        (FO if field else FR)[r, LEFT:RIGHT] = turned
        right[at : at + n] = turned[HALF - n :]
        left[at : at + n] = turned[:n]
        at += n

    fields = ((m2, 3 * HALF), (m1, OWN), (own, OWN), (p1, OWN), (p2, 3 * HALF))
    for k, (ref, start) in enumerate(fields):
        tile = ref[start : start + INIT]
        for out, at in ((tiles, 0), (right, EDGE), (left, EDGE)):
            out[at + k * INIT : at + (k + 1) * INIT] = tile


def scatter_obs(pos, slots, received, weights, observed):
    received = jnp.concatenate([received[...], jnp.zeros((MEMBERS, 96), F32)], axis=1).T
    values, precision = received[:16], received[16:32]
    lines = ROWS * HALF
    k = iota((lines, MEMBERS), 0)
    cell = (k // HALF) * COLS + pos[1] * HALF + k % HALF
    for t in range(2):
        found_w = jnp.zeros((lines, MEMBERS), F32)
        found_y = jnp.zeros((lines, MEMBERS), F32)
        for s in range(8):
            at = t * 8 + s
            hit = cell == slots[at : at + 1, :]
            found_w = found_w + jnp.where(hit, precision[at : at + 1, :], 0.0)
            found_y = found_y + jnp.where(hit, values[at : at + 1, :], 0.0)
        weights[t] = jnp.broadcast_to(jnp.sum(found_w, axis=1, keepdims=True), (lines, MEMBERS))
        observed[t] = jnp.broadcast_to(jnp.sum(found_y, axis=1, keepdims=True), (lines, MEMBERS))


def inside(lat, r):
    row = lat * ROWS + r - 10
    return jnp.logical_and(row >= 0, row < GLOBAL_ROWS)


def initial_table(pos, tiles, lz, rz):
    lane = iota((ROWS, COLS), 1)
    row = iota((ROWS, COLS), 0)
    e = pos[1]
    fields = [[], [], []]
    for k in range(5):
        for f in range(3):
            at = k * INIT + f * ROWS
            own = tiles[at : at + ROWS]
            at += EDGE
            before = lz[at : at + ROWS]
            after = rz[at : at + ROWS]
            low = pltpu.roll(jnp.where(lane >= 112, before, own), 16, 1)
            high = pltpu.roll(jnp.where(lane < 16, after, own), 80, 1)
            window = jnp.where(e == 0, low, high)
            place = pos[0] * ROWS + (k - 2) * ROWS + row
            ok = jnp.logical_and(place >= 0, place < GLOBAL_ROWS)
            fields[f].append(jnp.where(ok, window, 0.0))
    h, u, v = (jnp.concatenate(f, axis=0) for f in fields)
    east = pltpu.roll(u, COLS - 1, 1) - pltpu.roll(u, 1, 1)
    north = jnp.concatenate([v[1:], v[:1]], axis=0) - jnp.concatenate([v[-1:], v[:-1]], axis=0)
    place = pos[0] * ROWS - 16 + iota((40, COLS), 0)
    ok = jnp.logical_and(place >= 0, place < GLOBAL_ROWS)
    base = jnp.where(ok, h - DEPTH * (east + north), 0.0)
    return jnp.concatenate([base, u, v, jnp.zeros((8, COLS), F32)], axis=0).T


def forward(lat, table, FR, FO, H, U, V):
    first = table[0:96]

    def start(f, r):
        lane = f * 40 + r + 6
        return jnp.broadcast_to(first[:, lane : lane + 1], (96, MEMBERS))

    def gains(r):
        ok = inside(lat, r)
        return jnp.where(ok, F32(GRAVITY), F32(0.0)), jnp.where(ok, F32(CORIOLIS), F32(0.0))

    for r in range(EXT):
        H[r, 8:104] = start(0, r) + FO[r, 8:104]
    for r in range(1, EXT - 1):
        g, c = gains(r)
        u, v = start(1, r), start(2, r)
        keep = 1.0 - FR[r, 8:104]
        U[r, 8:104] = keep * u - g * (H[r, 9:105] - H[r, 7:103]) + c * v
        V[r, 8:104] = keep * v - g * (H[r + 1, 8:104] - H[r - 1, 8:104]) - c * u

    def height_row(a, b, r):
        g, _ = gains(r)
        n = b - a
        east = U[r, pl.ds(a + 1, n)] - U[r, pl.ds(a - 1, n)]
        north = V[r + 1, pl.ds(a, n)] - V[r - 1, pl.ds(a, n)]
        H[r, pl.ds(a, n)] = H[r, pl.ds(a, n)] - g * (east + north) + FO[r, pl.ds(a, n)]

    def speed_row(a, b, r):
        g, c = gains(r)
        n = b - a
        u, v = U[r, pl.ds(a, n)], V[r, pl.ds(a, n)]
        keep = 1.0 - FR[r, pl.ds(a, n)]
        east = H[r, pl.ds(a + 1, n)] - H[r, pl.ds(a - 1, n)]
        north = H[r + 1, pl.ds(a, n)] - H[r - 1, pl.ds(a, n)]
        U[r, pl.ds(a, n)] = keep * u - g * east + c * v
        V[r, pl.ds(a, n)] = keep * v - g * north - c * u

    def sweep(row, reach, a, b):
        def body(i, carry):
            row(a, b, 10 - reach + 2 * i)
            row(a, b, 11 - reach + 2 * i)
            return carry

        lax.fori_loop(0, (ROWS + 2 * reach) // 2, body, 0)

    for step in range(1, STEPS):
        reach = 2 * (STEPS - 1 - step)
        a, b = (16, 96) if reach else (LEFT, RIGHT)
        sweep(height_row, reach, a, b)
        if reach:
            sweep(speed_row, reach - 1, a, b)


def gram(pos, H, weights, observed, keep, send):
    lines = ROWS * HALF
    h = H[10:18, LEFT:RIGHT].reshape(lines, MEMBERS)
    centre = jnp.mean(h, axis=1, keepdims=True)
    spread = h - centre
    weighted = spread * weights
    g = lax.dot_general(spread, weighted, (((0,), (0,)), ((), ())), precision=HIGHEST, preferred_element_type=F32)
    d = jnp.sum(weighted * (observed - centre), axis=0, keepdims=True)
    row, lane = iota((HALF, MEMBERS), 0), iota((HALF, MEMBERS), 1)
    top, bottom = g[:HALF], g[HALF:]
    packed = jnp.where(jnp.logical_and(lane < HALF, lane > row), pltpu.roll(bottom, HALF, 1), top)
    diagonal = jnp.sum(jnp.where(lane == row + HALF, bottom, 0.0), axis=0, keepdims=True)
    line = iota((8, MEMBERS), 0)
    rest = jnp.where(line == 0, d, jnp.where(line == 1, diagonal, 0.0))
    one = jnp.concatenate([packed[:32], rest], axis=0)
    two = jnp.concatenate([packed[32:], jnp.zeros((8, MEMBERS), F32)], axis=0)
    keep[...] = jnp.where(pos[1] == 0, one, two)
    send[...] = jnp.where(pos[1] == 0, two, one)


def first_run(pos, fr, fo, tiles, lz, rz, weights, observed, FR, FO, table, keep, send, H, U, V):
    del fr, fo
    at = 0
    for field, r, n in EDGE_ROWS:
        out = FO if field else FR
        out[r, LEFT - n : LEFT] = lz[at : at + n]
        out[r, RIGHT : RIGHT + n] = rz[at : at + n]
        at += n
    table[...] = initial_table(pos, tiles, lz, rz)
    forward(pos[0], table[...], FR, FO, H, U, V)
    gram(pos, H, weights[0], observed[0], keep, send)


def inverse(x):
    n = PIVOTS
    panels = [x[k : k + n] for k in range(0, MEMBERS, n)]
    row, lane = iota((n, MEMBERS), 0), iota((n, MEMBERS), 1)
    lower, scaled = [], []

    def spread(panel, column):
        return jnp.broadcast_to(panel[:, column : column + 1], (n, MEMBERS))

    for k in range(len(panels)):
        first = k * n
        block = jnp.logical_and(lane >= first, lane < first + n)
        columns = [spread(panels[k], first + j) for j in range(n)]
        top = jnp.where(block, jnp.where(lane - first == row, 1.0, 0.0), panels[k])
        lower.append(jnp.where(lane < first + n, top, 0.0))
        for j in range(n):
            over = 1.0 / columns[j][j : j + 1]

            def eliminate(m, j=j, over=over):
                pivot = m[j : j + 1] * over
                return jnp.where(row == j, pivot, m - columns[j] * pivot)

            top = eliminate(top)
            columns[j + 1 :] = [eliminate(m) for m in columns[j + 1 :]]
        scaled.append(jnp.where(lane < first + n, top, 0.0))
        for i in range(k + 1, len(panels)):
            terms = [spread(panels[i], first + j) * top[j : j + 1] for j in range(n)]
            while len(terms) > 1:
                terms = [a + b for a, b in zip(terms[::2], terms[1::2])]
            panels[i] = jnp.where(block, 0.0, panels[i]) - terms[0]
    lower, scaled = jnp.concatenate(lower, axis=0), jnp.concatenate(scaled, axis=0)
    return lax.dot_general(lower, scaled, (((0,), (0,)), ((), ())), precision=HIGHEST, preferred_element_type=F32)


def weights_of(pos, mine, other):
    one = jnp.where(pos[1] == 0, mine, other)
    two = jnp.where(pos[1] == 0, other, mine)
    packed = jnp.concatenate([one[:32], two[:32]], axis=0)
    d, diagonal = one[32:33], one[33:34]
    turned = jnp.concatenate([packed, jnp.zeros((HALF, MEMBERS), F32)], axis=0).T
    row, lane = iota((HALF, MEMBERS), 0), iota((HALF, MEMBERS), 1)
    a = jnp.where(lane <= row, packed, turned[:HALF])
    c = pltpu.roll(jnp.where(lane > row, packed, turned[:HALF]), HALF, 1)
    c = jnp.where(lane == row + HALF, diagonal, c)
    top = jnp.where(lane < HALF, a, packed)
    bottom = jnp.where(lane < HALF, turned[HALF:], c)
    g = jnp.concatenate([top, bottom], axis=0)
    row, lane = iota((MEMBERS, MEMBERS), 0), iota((MEMBERS, MEMBERS), 1)
    x = g * (1.0 / MEMBERS) + jnp.where(row == lane, 1.0, 0.0)
    x = inverse(x)
    shift = jnp.sum(x * d, axis=1, keepdims=True) * (1.0 / MEMBERS)
    z = x + shift
    return z - jnp.mean(z, axis=0, keepdims=True) + 1.0 / MEMBERS


def second_run(pos, mine, other, fr, fo, table, weights, observed, k1, keep, send, FR, FO, H, U, V):
    k = weights_of(pos, mine[...], other[...])
    k1[...] = k
    for src, out in ((fr, FR), (fo, FO)):
        new = jnp.dot(src[...].reshape(EXT * WIDE, MEMBERS), k, precision=HIGHEST, preferred_element_type=F32)
        out[...] = new.reshape(EXT, WIDE, MEMBERS)
    forward(pos[0], table[...], FR, FO, H, U, V)
    gram(pos, H, weights[1], observed[1], keep, send)


def last_update(pos, mine, other, k1, own_p, other_p, out):
    k = jnp.dot(k1[...], weights_of(pos, mine[...], other[...]), precision=HIGHEST, preferred_element_type=F32)

    first = pos[1] == 0
    kt = k.T
    kt = jnp.where(first, kt[:HALF], kt[HALF:])
    for start in [f * HALF * ROWS + r for f in range(2) for r in range(ROWS)]:
        block = both_cores(first, own_p, other_p, start, ROWS)
        out[pl.ds(start, HALF, stride=ROWS), :] = jnp.dot(kt, block, precision=HIGHEST, preferred_element_type=F32)


def swap(value):
    return lax.ppermute(value, "ens", [(0, 1), (1, 0)])


def moved(value, axes, by):
    n = lax.axis_size(axes)
    return lax.ppermute(value, axes, [(i, (i + by) % n) for i in range(n)])


def copied_sum(*refs):
    *parts, out = refs
    terms = [ref[k] for ref in parts for k in range(ref.shape[0])]
    total = terms[0]
    for term in terms[1:]:
        total = total + term
    for k in range(out.shape[0]):
        out[k] = total


def summed(copies, *parts):
    return pl.pallas_call(
        copied_sum,
        out_shape=shape(copies, *parts[0].shape[1:]),
        in_specs=[VMEM] * len(parts),
        out_specs=VMEM,
        compiler_params=pltpu.CompilerParams(vmem_limit_bytes=4 * 1024 * 1024),
    )(*parts)


def reduced(keep, send):
    parts = keep[None], swap(send)[None]
    for axes in (LAT, "lon"):
        parts = [lax.all_to_all(summed(lax.axis_size(axes), *parts), axes, 0, 0, tiled=True)]
    value = summed(1, *parts)[0]
    return value, swap(value)


def call(kernel, out_shape, scalars, *args, scratch=(), aliases=None):
    return pl.pallas_call(
        kernel,
        out_shape=out_shape,
        in_specs=[SMEM] + [VMEM] * len(args),
        out_specs=jax.tree.map(lambda _: VMEM, out_shape),
        scratch_shapes=list(scratch),
        input_output_aliases=aliases or {},
        compiler_params=params(),
    )(scalars, *args)


def per_device(parameters, initial_height, initial_speed, obs_slots, obs_values, obs_precision):
    pos = jnp.stack([lax.axis_index(LAT), lax.axis_index("ens")]).astype(jnp.int32)
    own_p = parameters.reshape(2 * HALF * ROWS, COLS)
    slots, values, precision = (
        x[:, 0].transpose(0, 2, 1).reshape(16, 128) for x in (obs_slots, obs_values, obs_precision)
    )
    two_far = shape(3 * HALF + INIT, COLS)
    own, up2, dn2, obs = pl.pallas_call(
        collect,
        out_shape=[shape(OWN + INIT, COLS), two_far, two_far, shape(128, 32)],
        in_specs=[pl.BlockSpec(memory_space=pl.ANY)] * 5,
        out_specs=[VMEM] * 4,
        scratch_shapes=[pltpu.VMEM((16, COLS), F32)] * 2 + [pltpu.SemaphoreType.DMA((5,))],
    )(own_p, initial_height, initial_speed.reshape(16, COLS), values, precision)
    near = [moved(own, LAT, 1), moved(own, LAT, -1)]
    far = [moved(up2, LAT, 2), moved(dn2, LAT, -2)]
    own_other = swap(own)
    obs = lax.all_to_all(obs, LAT_LON, 0, 0, tiled=True)
    *halo, obs = lax.optimization_barrier((*near, *far, obs))
    blocks = [own, *halo]
    others = [own_other] + [swap(x) for x in halo]
    weights, observed = call(scatter_obs, [shape(2, 512, 128), shape(2, 512, 128)], pos, slots, obs)

    field = shape(EXT, WIDE, MEMBERS)
    half = shape(40, MEMBERS)
    square = shape(MEMBERS, MEMBERS)
    edge = shape(EDGE + 5 * INIT, MEMBERS)
    ext_fr, ext_fo, tiles, right, left = call(
        turn_rows, [field, field, shape(5 * INIT, COLS), edge, edge], pos, *blocks, *others
    )
    lz, rz = moved(right, LON_ENS, 1), moved(left, LON_ENS, -1)
    state = [pltpu.VMEM((EXT, WIDE, MEMBERS), F32)]
    ext_fr, ext_fo, table, keep, send = call(
        first_run, [field, field, square, half, half],
        pos, ext_fr, ext_fo, tiles, lz, rz, weights, observed,
        scratch=state * 3, aliases={1: 0, 2: 1},
    )
    mine, other = reduced(keep, send)
    k1, keep, send = call(
        second_run, [square, half, half],
        pos, mine, other, ext_fr, ext_fo, table, weights, observed,
        scratch=state * 5,
    )
    mine, other = reduced(keep, send)
    out = call(last_update, shape(2 * HALF * ROWS, COLS), pos, mine, other, k1, own_p, others[0])
    return out.reshape(parameters.shape)


def solution(mesh):
    torus = Mesh(
        mesh.devices.reshape(4, 4, mesh.shape["lon"], mesh.shape["ens"]),
        ("lat_0", "lat_1", "lon", "ens"),
    )
    in_specs = (
        P(None, "ens", LAT, "lon"),
        P(LAT, "lon"),
        P(None, LAT, "lon"),
        P(None, LAT_LON, None, None),
        P(None, LAT_LON, None, None),
        P(None, LAT_LON, None, None),
    )
    out_specs = P(None, "ens", LAT, "lon")
    return jax.shard_map(
        per_device, mesh=torus, in_specs=in_specs, out_specs=out_specs, check_vma=False
    )
```

```python
import functools

import jax
import jax.numpy as jnp
from jax import lax
from jax.experimental import pallas as pl
from jax.experimental.pallas import tpu as pltpu
from jax.sharding import Mesh
from jax.sharding import PartitionSpec as P

STEPS = 6
LAT = ("lat_0", "lat_1")
LAT_LON = ("lat_0", "lat_1", "lon")
LON_ENS = ("lon", "ens")

DEPTH = 0.7
GRAVITY = 0.7
CORIOLIS = 0.1

MEMBERS = 128
HALF = 64
ROWS = 8
COLS = 128
EXT = 28
WIDE = 112
LEFT = 24
RIGHT = LEFT + HALF
INIT = 24
GLOBAL_ROWS = 128
OWN = 2 * ROWS * HALF
PIVOTS = 16

F32 = jnp.float32
HIGHEST = lax.Precision.HIGHEST
VMEM = pl.BlockSpec(memory_space=pltpu.VMEM)
SMEM = pl.BlockSpec(memory_space=pltpu.SMEM)


def params():
    return pltpu.CompilerParams(vmem_limit_bytes=24 * 1024 * 1024)


def shape(*dims):
    return jax.ShapeDtypeStruct(dims, F32)


def iota(dims, axis):
    return lax.broadcasted_iota(jnp.int32, dims, axis)


def collect(own_hbm, height_hbm, speed_hbm, values_hbm, precision_hbm,
            out, up2, dn2, obs, values, precision, sems):
    pairs = (
        (values_hbm, values), (precision_hbm, precision), (own_hbm, out.at[:OWN]),
        (height_hbm, out.at[OWN : OWN + ROWS]), (speed_hbm, out.at[OWN + ROWS :]),
    )
    copies = [pltpu.make_async_copy(src, dst, sems.at[k]) for k, (src, dst) in enumerate(pairs)]
    for copy in copies:
        copy.start()
    for copy in copies[:2]:
        copy.wait()
    lines = [values[...], precision[...], jnp.zeros((96, MEMBERS), F32)]
    by_owner = jnp.concatenate(lines, axis=0).T
    for x in range(4):
        line = jnp.zeros((ROWS, MEMBERS), F32)
        for y in range(4):
            at = (4 * x + y) * 8
            line = line + pltpu.roll(by_owner[at : at + 8], 32 * y, 1)
        obs[pl.ds(x, 8, stride=4), :] = line
    for copy in copies[2:]:
        copy.wait()
    for k, (f, up_row, down_row) in enumerate(((1, 6, 0), (1, 7, 1), (0, 7, 0))):
        start = f * HALF * ROWS
        up2[k * HALF : (k + 1) * HALF] = out[pl.ds(start + up_row, HALF, stride=ROWS), :]
        dn2[k * HALF : (k + 1) * HALF] = out[pl.ds(start + down_row, HALF, stride=ROWS), :]
    up2[3 * HALF :] = out[OWN:]
    dn2[3 * HALF :] = out[OWN:]


def edge_rows():
    rows = []
    for field, first in ((1, 0), (0, 1)):
        for r in range(first, EXT - first):
            away = max(10 - r, r - 17, 0)
            need = 9 + field - away
            rows.append((field, r, 16 if need > 8 else 8))
    return rows


EDGE_ROWS = edge_rows()
EDGE = sum(n for _, _, n in EDGE_ROWS)


def both_cores(first, mine, others, start, stride):
    lines = pl.ds(start, HALF, stride=stride)
    mine, others = mine[lines, :], others[lines, :]
    return jnp.concatenate([jnp.where(first, mine, others), jnp.where(first, others, mine)], axis=0)


def turn_rows(pos, own, m1, p1, m2, p2, own_o, m1_o, p1_o, m2_o, p2_o, FR, FO, tiles, right, left):
    def row_source(field, r):
        if 2 <= r < 26:
            which = (r - 2) // ROWS
            return (m1, own, p1)[which], (m1_o, own_o, p1_o)[which], field * HALF * ROWS + (r - 2) % ROWS, ROWS
        k = 2 if field == 0 else (r if r < 2 else r - 26)
        refs = (m2, m2_o) if r < 2 else (p2, p2_o)
        return *refs, k * HALF, 1

    first = pos[1] == 0
    at = 0
    for field, r, n in EDGE_ROWS:
        mine, others, start, stride = row_source(field, r)
        turned = both_cores(first, mine, others, start, stride).T
        turned = jnp.where(first, turned[:HALF], turned[HALF:])
        if field == 1 and not 10 <= r < 18:
            turned = jnp.where(inside(pos[0], r), turned, 0.0)
        (FO if field else FR)[r, LEFT:RIGHT] = turned
        right[at : at + n] = turned[HALF - n :]
        left[at : at + n] = turned[:n]
        at += n

    fields = ((m2, 3 * HALF), (m1, OWN), (own, OWN), (p1, OWN), (p2, 3 * HALF))
    for k, (ref, start) in enumerate(fields):
        tile = ref[start : start + INIT]
        for out, at in ((tiles, 0), (right, EDGE), (left, EDGE)):
            out[at + k * INIT : at + (k + 1) * INIT] = tile


def by_xy(received, out):
    for x in range(4):
        line = received[pl.ds(x, 8, stride=4), :]
        for y in range(4):
            at = (4 * x + y) * 8
            out[at : at + 8] = pltpu.roll(line, (4 - y) % 4 * 32, 1)


def scatter_obs(pos, slots, received, weights, observed):
    received = received[...].T
    values, precision = received[:16], received[16:32]
    lines = ROWS * HALF
    k = iota((lines, MEMBERS), 0)
    cell = (k // HALF) * COLS + pos[1] * HALF + k % HALF
    for t in range(2):
        found_w = jnp.zeros((lines, MEMBERS), F32)
        found_y = jnp.zeros((lines, MEMBERS), F32)
        for s in range(8):
            at = t * 8 + s
            hit = cell == slots[at : at + 1, :]
            found_w = found_w + jnp.where(hit, precision[at : at + 1, :], 0.0)
            found_y = found_y + jnp.where(hit, values[at : at + 1, :], 0.0)
        weights[t] = jnp.broadcast_to(jnp.sum(found_w, axis=1, keepdims=True), (lines, MEMBERS))
        observed[t] = jnp.broadcast_to(jnp.sum(found_y, axis=1, keepdims=True), (lines, MEMBERS))


def inside(lat, r):
    row = lat * ROWS + r - 10
    return jnp.logical_and(row >= 0, row < GLOBAL_ROWS)


def initial_table(pos, tiles, lz, rz):
    lane = iota((ROWS, COLS), 1)
    row = iota((ROWS, COLS), 0)
    e = pos[1]
    fields = [[], [], []]
    for k in range(5):
        for f in range(3):
            at = k * INIT + f * ROWS
            own = tiles[at : at + ROWS]
            at += EDGE
            before = lz[at : at + ROWS]
            after = rz[at : at + ROWS]
            low = pltpu.roll(jnp.where(lane >= 112, before, own), 16, 1)
            high = pltpu.roll(jnp.where(lane < 16, after, own), 80, 1)
            window = jnp.where(e == 0, low, high)
            place = pos[0] * ROWS + (k - 2) * ROWS + row
            ok = jnp.logical_and(place >= 0, place < GLOBAL_ROWS)
            fields[f].append(jnp.where(ok, window, 0.0))
    h, u, v = (jnp.concatenate(f, axis=0) for f in fields)
    east = pltpu.roll(u, COLS - 1, 1) - pltpu.roll(u, 1, 1)
    north = jnp.concatenate([v[1:], v[:1]], axis=0) - jnp.concatenate([v[-1:], v[:-1]], axis=0)
    place = pos[0] * ROWS - 16 + iota((40, COLS), 0)
    ok = jnp.logical_and(place >= 0, place < GLOBAL_ROWS)
    base = jnp.where(ok, h - DEPTH * (east + north), 0.0)
    return jnp.concatenate([base, u, v, jnp.zeros((8, COLS), F32)], axis=0).T


def forward(lat, table, FR, FO, H, U, V):
    first = table[0:96]

    def start(f, r):
        lane = f * 40 + r + 6
        return jnp.broadcast_to(first[:, lane : lane + 1], (96, MEMBERS))

    def gains(r):
        ok = inside(lat, r)
        return jnp.where(ok, F32(GRAVITY), F32(0.0)), jnp.where(ok, F32(CORIOLIS), F32(0.0))

    for r in range(EXT):
        H[r, 8:104] = start(0, r) + FO[r, 8:104]
    for r in range(1, EXT - 1):
        g, c = gains(r)
        u, v = start(1, r), start(2, r)
        keep = 1.0 - FR[r, 8:104]
        U[r, 8:104] = keep * u - g * (H[r, 9:105] - H[r, 7:103]) + c * v
        V[r, 8:104] = keep * v - g * (H[r + 1, 8:104] - H[r - 1, 8:104]) - c * u

    def height_row(a, b, r):
        g, _ = gains(r)
        n = b - a
        east = U[r, pl.ds(a + 1, n)] - U[r, pl.ds(a - 1, n)]
        north = V[r + 1, pl.ds(a, n)] - V[r - 1, pl.ds(a, n)]
        H[r, pl.ds(a, n)] = H[r, pl.ds(a, n)] - g * (east + north) + FO[r, pl.ds(a, n)]

    def speed_row(a, b, r):
        g, c = gains(r)
        n = b - a
        u, v = U[r, pl.ds(a, n)], V[r, pl.ds(a, n)]
        keep = 1.0 - FR[r, pl.ds(a, n)]
        east = H[r, pl.ds(a + 1, n)] - H[r, pl.ds(a - 1, n)]
        north = H[r + 1, pl.ds(a, n)] - H[r - 1, pl.ds(a, n)]
        U[r, pl.ds(a, n)] = keep * u - g * east + c * v
        V[r, pl.ds(a, n)] = keep * v - g * north - c * u

    def sweep(row, reach, a, b):
        def body(i, carry):
            row(a, b, 10 - reach + 2 * i)
            row(a, b, 11 - reach + 2 * i)
            return carry

        lax.fori_loop(0, (ROWS + 2 * reach) // 2, body, 0)

    for step in range(1, STEPS):
        reach = 2 * (STEPS - 1 - step)
        a, b = (16, 96) if reach else (LEFT, RIGHT)
        sweep(height_row, reach, a, b)
        if reach:
            sweep(speed_row, reach - 1, a, b)


def gram(pos, H, weights, observed, keep, send):
    lines = ROWS * HALF
    h = H[10:18, LEFT:RIGHT].reshape(lines, MEMBERS)
    centre = jnp.mean(h, axis=1, keepdims=True)
    spread = h - centre
    weighted = spread * weights
    g = lax.dot_general(spread, weighted, (((0,), (0,)), ((), ())), precision=HIGHEST, preferred_element_type=F32)
    d = jnp.sum(weighted * (observed - centre), axis=0, keepdims=True)
    row, lane = iota((HALF, MEMBERS), 0), iota((HALF, MEMBERS), 1)
    top, bottom = g[:HALF], g[HALF:]
    packed = jnp.where(jnp.logical_and(lane < HALF, lane > row), pltpu.roll(bottom, HALF, 1), top)
    diagonal = jnp.sum(jnp.where(lane == row + HALF, bottom, 0.0), axis=0, keepdims=True)
    line = iota((8, MEMBERS), 0)
    rest = jnp.where(line == 0, d, jnp.where(line == 1, diagonal, 0.0))
    one = jnp.concatenate([packed[:32], rest], axis=0)
    two = jnp.concatenate([packed[32:], jnp.zeros((8, MEMBERS), F32)], axis=0)
    keep[...] = jnp.where(pos[1] == 0, one, two)
    send[...] = jnp.where(pos[1] == 0, two, one)


def first_run(pos, fr, fo, tiles, lz, rz, weights, observed, FR, FO, table, keep, send, H, U, V):
    del fr, fo
    at = 0
    for field, r, n in EDGE_ROWS:
        out = FO if field else FR
        out[r, LEFT - n : LEFT] = lz[at : at + n]
        out[r, RIGHT : RIGHT + n] = rz[at : at + n]
        at += n
    table[...] = initial_table(pos, tiles, lz, rz)
    forward(pos[0], table[...], FR, FO, H, U, V)
    gram(pos, H, weights[0], observed[0], keep, send)


def inverse(x):
    n = PIVOTS
    panels = [x[k : k + n] for k in range(0, MEMBERS, n)]
    row, lane = iota((n, MEMBERS), 0), iota((n, MEMBERS), 1)
    lower, scaled = [], []

    def spread(panel, column):
        return jnp.broadcast_to(panel[:, column : column + 1], (n, MEMBERS))

    for k in range(len(panels)):
        first = k * n
        block = jnp.logical_and(lane >= first, lane < first + n)
        columns = [spread(panels[k], first + j) for j in range(n)]
        top = jnp.where(block, jnp.where(lane - first == row, 1.0, 0.0), panels[k])
        lower.append(jnp.where(lane < first + n, top, 0.0))
        for j in range(n):
            over = 1.0 / columns[j][j : j + 1]

            def eliminate(m, j=j, over=over):
                pivot = m[j : j + 1] * over
                return jnp.where(row == j, pivot, m - columns[j] * pivot)

            top = eliminate(top)
            columns[j + 1 :] = [eliminate(m) for m in columns[j + 1 :]]
        scaled.append(jnp.where(lane < first + n, top, 0.0))
        for i in range(k + 1, len(panels)):
            terms = [spread(panels[i], first + j) * top[j : j + 1] for j in range(n)]
            while len(terms) > 1:
                terms = [a + b for a, b in zip(terms[::2], terms[1::2])]
            panels[i] = jnp.where(block, 0.0, panels[i]) - terms[0]
    lower, scaled = jnp.concatenate(lower, axis=0), jnp.concatenate(scaled, axis=0)
    return lax.dot_general(lower, scaled, (((0,), (0,)), ((), ())), precision=HIGHEST, preferred_element_type=F32)


def weights_of(pos, mine, other):
    one = jnp.where(pos[1] == 0, mine, other)
    two = jnp.where(pos[1] == 0, other, mine)
    packed = jnp.concatenate([one[:32], two[:32]], axis=0)
    d, diagonal = one[32:33], one[33:34]
    turned = jnp.concatenate([packed, jnp.zeros((HALF, MEMBERS), F32)], axis=0).T
    row, lane = iota((HALF, MEMBERS), 0), iota((HALF, MEMBERS), 1)
    a = jnp.where(lane <= row, packed, turned[:HALF])
    c = pltpu.roll(jnp.where(lane > row, packed, turned[:HALF]), HALF, 1)
    c = jnp.where(lane == row + HALF, diagonal, c)
    top = jnp.where(lane < HALF, a, packed)
    bottom = jnp.where(lane < HALF, turned[HALF:], c)
    g = jnp.concatenate([top, bottom], axis=0)
    row, lane = iota((MEMBERS, MEMBERS), 0), iota((MEMBERS, MEMBERS), 1)
    x = g * (1.0 / MEMBERS) + jnp.where(row == lane, 1.0, 0.0)
    x = inverse(x)
    shift = jnp.sum(x * d, axis=1, keepdims=True) * (1.0 / MEMBERS)
    z = x + shift
    return z - jnp.mean(z, axis=0, keepdims=True) + 1.0 / MEMBERS


def second_run(pos, mine, other, fr, fo, table, weights, observed, k1, keep, send, FR, FO, H, U, V):
    k = weights_of(pos, mine[...], other[...])
    k1[...] = k
    for src, out in ((fr, FR), (fo, FO)):
        new = jnp.dot(src[...].reshape(EXT * WIDE, MEMBERS), k, precision=HIGHEST, preferred_element_type=F32)
        out[...] = new.reshape(EXT, WIDE, MEMBERS)
    forward(pos[0], table[...], FR, FO, H, U, V)
    gram(pos, H, weights[1], observed[1], keep, send)


def last_update(pos, mine, other, k1, own_p, other_p, out):
    k = jnp.dot(k1[...], weights_of(pos, mine[...], other[...]), precision=HIGHEST, preferred_element_type=F32)

    first = pos[1] == 0
    kt = k.T
    kt = jnp.where(first, kt[:HALF], kt[HALF:])
    for start in [f * HALF * ROWS + r for f in range(2) for r in range(ROWS)]:
        block = both_cores(first, own_p, other_p, start, ROWS)
        out[pl.ds(start, HALF, stride=ROWS), :] = jnp.dot(kt, block, precision=HIGHEST, preferred_element_type=F32)


def swap(value):
    return lax.ppermute(value, "ens", [(0, 1), (1, 0)])


def moved(value, axes, by):
    n = lax.axis_size(axes)
    return lax.ppermute(value, axes, [(i, (i + by) % n) for i in range(n)])


def copied_sum(*refs):
    *parts, out = refs
    terms = [ref[k] for ref in parts for k in range(ref.shape[0])]
    total = terms[0]
    for term in terms[1:]:
        total = total + term
    for k in range(out.shape[0]):
        out[k] = total


def summed(copies, *parts):
    return pl.pallas_call(
        copied_sum,
        out_shape=shape(copies, *parts[0].shape[1:]),
        in_specs=[VMEM] * len(parts),
        out_specs=VMEM,
        compiler_params=pltpu.CompilerParams(vmem_limit_bytes=4 * 1024 * 1024),
    )(*parts)


def reduced(keep, send):
    parts = keep[None], swap(send)[None]
    for axes in (LAT, "lon"):
        parts = [lax.all_to_all(summed(lax.axis_size(axes), *parts), axes, 0, 0, tiled=True)]
    value = summed(1, *parts)[0]
    return value, swap(value)


def call(kernel, out_shape, scalars, *args, scratch=(), aliases=None):
    return pl.pallas_call(
        kernel,
        out_shape=out_shape,
        in_specs=[SMEM] + [VMEM] * len(args),
        out_specs=jax.tree.map(lambda _: VMEM, out_shape),
        scratch_shapes=list(scratch),
        input_output_aliases=aliases or {},
        compiler_params=params(),
    )(scalars, *args)


def per_device(parameters, initial_height, initial_speed, obs_slots, obs_values, obs_precision):
    pos = jnp.stack([lax.axis_index(LAT), lax.axis_index("ens")]).astype(jnp.int32)
    own_p = parameters.reshape(2 * HALF * ROWS, COLS)
    slots, values, precision = (
        x[:, 0].transpose(0, 2, 1).reshape(16, 128) for x in (obs_slots, obs_values, obs_precision)
    )
    two_far = shape(3 * HALF + INIT, COLS)
    own, up2, dn2, obs = pl.pallas_call(
        collect,
        out_shape=[shape(OWN + INIT, COLS), two_far, two_far, shape(32, 128)],
        in_specs=[pl.BlockSpec(memory_space=pl.ANY)] * 5,
        out_specs=[VMEM] * 4,
        scratch_shapes=[pltpu.VMEM((16, COLS), F32)] * 2 + [pltpu.SemaphoreType.DMA((5,))],
    )(own_p, initial_height, initial_speed.reshape(16, COLS), values, precision)
    near = [moved(own, LAT, 1), moved(own, LAT, -1)]
    far = [moved(up2, LAT, 2), moved(dn2, LAT, -2)]
    own_other = swap(own)
    obs = lax.all_to_all(obs, "lon", 0, 0, tiled=True)
    *halo, obs = lax.optimization_barrier((*near, *far, obs))
    blocks = [own, *halo]
    others = [own_other] + [swap(x) for x in halo]
    field = shape(EXT, WIDE, MEMBERS)
    half = shape(40, MEMBERS)
    square = shape(MEMBERS, MEMBERS)
    edge = shape(EDGE + 5 * INIT, MEMBERS)
    ext_fr, ext_fo, tiles, right, left = call(
        turn_rows, [field, field, shape(5 * INIT, COLS), edge, edge], pos, *blocks, *others
    )
    right, left, obs = lax.optimization_barrier((right, left, obs))
    lz, rz = moved(right, LON_ENS, 1), moved(left, LON_ENS, -1)
    obs = pl.pallas_call(
        by_xy, out_shape=shape(128, 128), in_specs=[VMEM], out_specs=VMEM, compiler_params=params()
    )(obs)
    obs = lax.all_to_all(obs, LAT, 0, 0, tiled=True)
    weights, observed = call(scatter_obs, [shape(2, 512, 128), shape(2, 512, 128)], pos, slots, obs)
    state = [pltpu.VMEM((EXT, WIDE, MEMBERS), F32)]
    ext_fr, ext_fo, table, keep, send = call(
        first_run, [field, field, square, half, half],
        pos, ext_fr, ext_fo, tiles, lz, rz, weights, observed,
        scratch=state * 3, aliases={1: 0, 2: 1},
    )
    mine, other = reduced(keep, send)
    k1, keep, send = call(
        second_run, [square, half, half],
        pos, mine, other, ext_fr, ext_fo, table, weights, observed,
        scratch=state * 5,
    )
    mine, other = reduced(keep, send)
    out = call(last_update, shape(2 * HALF * ROWS, COLS), pos, mine, other, k1, own_p, others[0])
    return out.reshape(parameters.shape)


def solution(mesh):
    torus = Mesh(
        mesh.devices.reshape(4, 4, mesh.shape["lon"], mesh.shape["ens"]),
        ("lat_0", "lat_1", "lon", "ens"),
    )
    in_specs = (
        P(None, "ens", LAT, "lon"),
        P(LAT, "lon"),
        P(None, LAT, "lon"),
        P(None, LAT_LON, None, None),
        P(None, LAT_LON, None, None),
        P(None, LAT_LON, None, None),
    )
    out_specs = P(None, "ens", LAT, "lon")
    return jax.shard_map(
        per_device, mesh=torus, in_specs=in_specs, out_specs=out_specs, check_vma=False
    )
```

```python
import functools

import jax
import jax.numpy as jnp
from jax import lax
from jax.experimental import pallas as pl
from jax.experimental.pallas import tpu as pltpu
from jax.sharding import Mesh
from jax.sharding import PartitionSpec as P

STEPS = 6
LAT = ("lat_0", "lat_1")
LAT_LON = ("lat_0", "lat_1", "lon")
LON_ENS = ("lon", "ens")

DEPTH = 0.7
GRAVITY = 0.7
CORIOLIS = 0.1

MEMBERS = 128
HALF = 64
ROWS = 8
COLS = 128
EXT = 28
WIDE = 112
LEFT = 24
RIGHT = LEFT + HALF
INIT = 24
GLOBAL_ROWS = 128
OWN = 2 * ROWS * HALF
PIVOTS = 16

F32 = jnp.float32
HIGHEST = lax.Precision.HIGHEST
VMEM = pl.BlockSpec(memory_space=pltpu.VMEM)
SMEM = pl.BlockSpec(memory_space=pltpu.SMEM)


def params():
    return pltpu.CompilerParams(vmem_limit_bytes=24 * 1024 * 1024)


def shape(*dims):
    return jax.ShapeDtypeStruct(dims, F32)


def iota(dims, axis):
    return lax.broadcasted_iota(jnp.int32, dims, axis)


def collect(own_hbm, height_hbm, speed_hbm, values_hbm, precision_hbm,
            out, up2, dn2, obs, values, precision, sems):
    pairs = (
        (values_hbm, values), (precision_hbm, precision), (own_hbm, out.at[:OWN]),
        (height_hbm, out.at[OWN : OWN + ROWS]), (speed_hbm, out.at[OWN + ROWS :]),
    )
    copies = [pltpu.make_async_copy(src, dst, sems.at[k]) for k, (src, dst) in enumerate(pairs)]
    for copy in copies:
        copy.start()
    for copy in copies[:2]:
        copy.wait()
    lines = [values[...], precision[...], jnp.zeros((96, MEMBERS), F32)]
    obs[...] = jnp.concatenate(lines, axis=0).T
    for copy in copies[2:]:
        copy.wait()
    for k, (f, up_row, down_row) in enumerate(((1, 6, 0), (1, 7, 1), (0, 7, 0))):
        start = f * HALF * ROWS
        up2[k * HALF : (k + 1) * HALF] = out[pl.ds(start + up_row, HALF, stride=ROWS), :]
        dn2[k * HALF : (k + 1) * HALF] = out[pl.ds(start + down_row, HALF, stride=ROWS), :]
    up2[3 * HALF :] = out[OWN:]
    dn2[3 * HALF :] = out[OWN:]


def edge_rows():
    rows = []
    for field, first in ((1, 0), (0, 1)):
        for r in range(first, EXT - first):
            away = max(10 - r, r - 17, 0)
            need = 9 + field - away
            rows.append((field, r, 16 if need > 8 else 8))
    return rows


EDGE_ROWS = edge_rows()
EDGE = sum(n for _, _, n in EDGE_ROWS)


def both_cores(first, mine, others, start, stride):
    lines = pl.ds(start, HALF, stride=stride)
    mine, others = mine[lines, :], others[lines, :]
    return jnp.concatenate([jnp.where(first, mine, others), jnp.where(first, others, mine)], axis=0)


def turn_rows(pos, own, m1, p1, m2, p2, own_o, m1_o, p1_o, m2_o, p2_o, FR, FO, tiles, right, left):
    def row_source(field, r):
        if 2 <= r < 26:
            which = (r - 2) // ROWS
            return (m1, own, p1)[which], (m1_o, own_o, p1_o)[which], field * HALF * ROWS + (r - 2) % ROWS, ROWS
        k = 2 if field == 0 else (r if r < 2 else r - 26)
        refs = (m2, m2_o) if r < 2 else (p2, p2_o)
        return *refs, k * HALF, 1

    first = pos[1] == 0
    at = 0
    for field, r, n in EDGE_ROWS:
        mine, others, start, stride = row_source(field, r)
        turned = both_cores(first, mine, others, start, stride).T
        turned = jnp.where(first, turned[:HALF], turned[HALF:])
        if field == 1 and not 10 <= r < 18:
            turned = jnp.where(inside(pos[0], r), turned, 0.0)
        (FO if field else FR)[r, LEFT:RIGHT] = turned
        right[at : at + n] = turned[HALF - n :]
        left[at : at + n] = turned[:n]
        at += n

    fields = ((m2, 3 * HALF), (m1, OWN), (own, OWN), (p1, OWN), (p2, 3 * HALF))
    for k, (ref, start) in enumerate(fields):
        tile = ref[start : start + INIT]
        for out, at in ((tiles, 0), (right, EDGE), (left, EDGE)):
            out[at + k * INIT : at + (k + 1) * INIT] = tile


def scatter_obs(pos, slots, received, weights, observed):
    received = received[...].T
    values, precision = received[:16], received[16:32]
    lines = ROWS * HALF
    k = iota((lines, MEMBERS), 0)
    cell = (k // HALF) * COLS + pos[1] * HALF + k % HALF
    for t in range(2):
        found_w = jnp.zeros((lines, MEMBERS), F32)
        found_y = jnp.zeros((lines, MEMBERS), F32)
        for s in range(8):
            at = t * 8 + s
            hit = cell == slots[at : at + 1, :]
            found_w = found_w + jnp.where(hit, precision[at : at + 1, :], 0.0)
            found_y = found_y + jnp.where(hit, values[at : at + 1, :], 0.0)
        weights[t] = jnp.broadcast_to(jnp.sum(found_w, axis=1, keepdims=True), (lines, MEMBERS))
        observed[t] = jnp.broadcast_to(jnp.sum(found_y, axis=1, keepdims=True), (lines, MEMBERS))


def inside(lat, r):
    row = lat * ROWS + r - 10
    return jnp.logical_and(row >= 0, row < GLOBAL_ROWS)


def initial_table(pos, tiles, lz, rz):
    lane = iota((ROWS, COLS), 1)
    row = iota((ROWS, COLS), 0)
    e = pos[1]
    fields = [[], [], []]
    for k in range(5):
        for f in range(3):
            at = k * INIT + f * ROWS
            own = tiles[at : at + ROWS]
            at += EDGE
            before = lz[at : at + ROWS]
            after = rz[at : at + ROWS]
            low = pltpu.roll(jnp.where(lane >= 112, before, own), 16, 1)
            high = pltpu.roll(jnp.where(lane < 16, after, own), 80, 1)
            window = jnp.where(e == 0, low, high)
            place = pos[0] * ROWS + (k - 2) * ROWS + row
            ok = jnp.logical_and(place >= 0, place < GLOBAL_ROWS)
            fields[f].append(jnp.where(ok, window, 0.0))
    h, u, v = (jnp.concatenate(f, axis=0) for f in fields)
    east = pltpu.roll(u, COLS - 1, 1) - pltpu.roll(u, 1, 1)
    north = jnp.concatenate([v[1:], v[:1]], axis=0) - jnp.concatenate([v[-1:], v[:-1]], axis=0)
    place = pos[0] * ROWS - 16 + iota((40, COLS), 0)
    ok = jnp.logical_and(place >= 0, place < GLOBAL_ROWS)
    base = jnp.where(ok, h - DEPTH * (east + north), 0.0)
    return jnp.concatenate([base, u, v, jnp.zeros((8, COLS), F32)], axis=0).T


def forward(lat, table, FR, FO, H, U, V):
    first = table[0:96]

    def start(f, r):
        lane = f * 40 + r + 6
        return jnp.broadcast_to(first[:, lane : lane + 1], (96, MEMBERS))

    def gains(r):
        ok = inside(lat, r)
        return jnp.where(ok, F32(GRAVITY), F32(0.0)), jnp.where(ok, F32(CORIOLIS), F32(0.0))

    for r in range(EXT):
        H[r, 8:104] = start(0, r) + FO[r, 8:104]
    for r in range(1, EXT - 1):
        g, c = gains(r)
        u, v = start(1, r), start(2, r)
        keep = 1.0 - FR[r, 8:104]
        U[r, 8:104] = keep * u - g * (H[r, 9:105] - H[r, 7:103]) + c * v
        V[r, 8:104] = keep * v - g * (H[r + 1, 8:104] - H[r - 1, 8:104]) - c * u

    def height_row(a, b, r):
        g, _ = gains(r)
        n = b - a
        east = U[r, pl.ds(a + 1, n)] - U[r, pl.ds(a - 1, n)]
        north = V[r + 1, pl.ds(a, n)] - V[r - 1, pl.ds(a, n)]
        H[r, pl.ds(a, n)] = H[r, pl.ds(a, n)] - g * (east + north) + FO[r, pl.ds(a, n)]

    def speed_row(a, b, r):
        g, c = gains(r)
        n = b - a
        u, v = U[r, pl.ds(a, n)], V[r, pl.ds(a, n)]
        keep = 1.0 - FR[r, pl.ds(a, n)]
        east = H[r, pl.ds(a + 1, n)] - H[r, pl.ds(a - 1, n)]
        north = H[r + 1, pl.ds(a, n)] - H[r - 1, pl.ds(a, n)]
        U[r, pl.ds(a, n)] = keep * u - g * east + c * v
        V[r, pl.ds(a, n)] = keep * v - g * north - c * u

    def sweep(row, reach, a, b):
        def body(i, carry):
            row(a, b, 10 - reach + 2 * i)
            row(a, b, 11 - reach + 2 * i)
            return carry

        lax.fori_loop(0, (ROWS + 2 * reach) // 2, body, 0)

    for step in range(1, STEPS):
        reach = 2 * (STEPS - 1 - step)
        a, b = (16, 96) if reach else (LEFT, RIGHT)
        sweep(height_row, reach, a, b)
        if reach:
            sweep(speed_row, reach - 1, a, b)


def gram(pos, H, weights, observed, keep, send):
    lines = ROWS * HALF
    h = H[10:18, LEFT:RIGHT].reshape(lines, MEMBERS)
    centre = jnp.mean(h, axis=1, keepdims=True)
    spread = h - centre
    weighted = spread * weights
    g = lax.dot_general(spread, weighted, (((0,), (0,)), ((), ())), precision=HIGHEST, preferred_element_type=F32)
    d = jnp.sum(weighted * (observed - centre), axis=0, keepdims=True)
    row, lane = iota((HALF, MEMBERS), 0), iota((HALF, MEMBERS), 1)
    top, bottom = g[:HALF], g[HALF:]
    packed = jnp.where(jnp.logical_and(lane < HALF, lane > row), pltpu.roll(bottom, HALF, 1), top)
    diagonal = jnp.sum(jnp.where(lane == row + HALF, bottom, 0.0), axis=0, keepdims=True)
    line = iota((8, MEMBERS), 0)
    rest = jnp.where(line == 0, d, jnp.where(line == 1, diagonal, 0.0))
    one = jnp.concatenate([packed[:32], rest], axis=0)
    two = jnp.concatenate([packed[32:], jnp.zeros((8, MEMBERS), F32)], axis=0)
    keep[...] = jnp.where(pos[1] == 0, one, two)
    send[...] = jnp.where(pos[1] == 0, two, one)


def first_run(pos, fr, fo, tiles, lz, rz, weights, observed, FR, FO, table, keep, send, H, U, V):
    del fr, fo
    at = 0
    for field, r, n in EDGE_ROWS:
        out = FO if field else FR
        out[r, LEFT - n : LEFT] = lz[at : at + n]
        out[r, RIGHT : RIGHT + n] = rz[at : at + n]
        at += n
    table[...] = initial_table(pos, tiles, lz, rz)
    forward(pos[0], table[...], FR, FO, H, U, V)
    gram(pos, H, weights[0], observed[0], keep, send)


def inverse(x):
    n = PIVOTS
    panels = [x[k : k + n] for k in range(0, MEMBERS, n)]
    row, lane = iota((n, MEMBERS), 0), iota((n, MEMBERS), 1)
    lower, scaled = [], []

    def spread(panel, column):
        return jnp.broadcast_to(panel[:, column : column + 1], (n, MEMBERS))

    for k in range(len(panels)):
        first = k * n
        block = jnp.logical_and(lane >= first, lane < first + n)
        columns = [spread(panels[k], first + j) for j in range(n)]
        top = jnp.where(block, jnp.where(lane - first == row, 1.0, 0.0), panels[k])
        lower.append(jnp.where(lane < first + n, top, 0.0))
        for j in range(n):
            over = 1.0 / columns[j][j : j + 1]

            def eliminate(m, j=j, over=over):
                pivot = m[j : j + 1] * over
                return jnp.where(row == j, pivot, m - columns[j] * pivot)

            top = eliminate(top)
            columns[j + 1 :] = [eliminate(m) for m in columns[j + 1 :]]
        scaled.append(jnp.where(lane < first + n, top, 0.0))
        for i in range(k + 1, len(panels)):
            terms = [spread(panels[i], first + j) * top[j : j + 1] for j in range(n)]
            while len(terms) > 1:
                terms = [a + b for a, b in zip(terms[::2], terms[1::2])]
            panels[i] = jnp.where(block, 0.0, panels[i]) - terms[0]
    lower, scaled = jnp.concatenate(lower, axis=0), jnp.concatenate(scaled, axis=0)
    return lax.dot_general(lower, scaled, (((0,), (0,)), ((), ())), precision=HIGHEST, preferred_element_type=F32)


def weights_of(parts):
    one, two = parts[0], parts[1]
    for k in range(2, parts.shape[0], 2):
        one, two = one + parts[k], two + parts[k + 1]
    packed = jnp.concatenate([one[:32], two[:32]], axis=0)
    d, diagonal = one[32:33], one[33:34]
    turned = jnp.concatenate([packed, jnp.zeros((HALF, MEMBERS), F32)], axis=0).T
    row, lane = iota((HALF, MEMBERS), 0), iota((HALF, MEMBERS), 1)
    a = jnp.where(lane <= row, packed, turned[:HALF])
    c = pltpu.roll(jnp.where(lane > row, packed, turned[:HALF]), HALF, 1)
    c = jnp.where(lane == row + HALF, diagonal, c)
    top = jnp.where(lane < HALF, a, packed)
    bottom = jnp.where(lane < HALF, turned[HALF:], c)
    g = jnp.concatenate([top, bottom], axis=0)
    row, lane = iota((MEMBERS, MEMBERS), 0), iota((MEMBERS, MEMBERS), 1)
    x = g * (1.0 / MEMBERS) + jnp.where(row == lane, 1.0, 0.0)
    x = inverse(x)
    shift = jnp.sum(x * d, axis=1, keepdims=True) * (1.0 / MEMBERS)
    z = x + shift
    return z - jnp.mean(z, axis=0, keepdims=True) + 1.0 / MEMBERS


def second_run(pos, parts, fr, fo, table, weights, observed, k1, keep, send, FR, FO, H, U, V):
    k = weights_of(parts)
    k1[...] = k
    for src, out in ((fr, FR), (fo, FO)):
        new = jnp.dot(src[...].reshape(EXT * WIDE, MEMBERS), k, precision=HIGHEST, preferred_element_type=F32)
        out[...] = new.reshape(EXT, WIDE, MEMBERS)
    forward(pos[0], table[...], FR, FO, H, U, V)
    gram(pos, H, weights[1], observed[1], keep, send)


def last_update(pos, parts, k1, own_p, other_p, out):
    k = jnp.dot(k1[...], weights_of(parts), precision=HIGHEST, preferred_element_type=F32)

    first = pos[1] == 0
    kt = k.T
    kt = jnp.where(first, kt[:HALF], kt[HALF:])
    for start in [f * HALF * ROWS + r for f in range(2) for r in range(ROWS)]:
        block = both_cores(first, own_p, other_p, start, ROWS)
        out[pl.ds(start, HALF, stride=ROWS), :] = jnp.dot(kt, block, precision=HIGHEST, preferred_element_type=F32)


def swap(value):
    return lax.ppermute(value, "ens", [(0, 1), (1, 0)])


def moved(value, axes, by):
    n = lax.axis_size(axes)
    return lax.ppermute(value, axes, [(i, (i + by) % n) for i in range(n)])


def copied_sum(*refs):
    *parts, out = refs
    terms = [ref[k] for ref in parts for k in range(ref.shape[0])]
    total = terms[0]
    for term in terms[1:]:
        total = total + term
    for k in range(out.shape[0]):
        out[k] = total


def summed(copies, *parts):
    return pl.pallas_call(
        copied_sum,
        out_shape=shape(copies, *parts[0].shape[1:]),
        in_specs=[VMEM] * len(parts),
        out_specs=VMEM,
        compiler_params=pltpu.CompilerParams(vmem_limit_bytes=4 * 1024 * 1024),
    )(*parts)


def reduced(keep, send):
    parts = [keep[None], swap(send)[None]]
    for axes in (LAT, LON_ENS):
        parts = [lax.all_to_all(summed(lax.axis_size(axes), *parts), axes, 0, 0, tiled=True)]
    return parts[0]


def call(kernel, out_shape, scalars, *args, scratch=(), aliases=None):
    return pl.pallas_call(
        kernel,
        out_shape=out_shape,
        in_specs=[SMEM] + [VMEM] * len(args),
        out_specs=jax.tree.map(lambda _: VMEM, out_shape),
        scratch_shapes=list(scratch),
        input_output_aliases=aliases or {},
        compiler_params=params(),
    )(scalars, *args)


def per_device(parameters, initial_height, initial_speed, obs_slots, obs_values, obs_precision):
    pos = jnp.stack([lax.axis_index(LAT), lax.axis_index("ens")]).astype(jnp.int32)
    own_p = parameters.reshape(2 * HALF * ROWS, COLS)
    slots, values, precision = (
        x[:, 0].transpose(0, 2, 1).reshape(16, 128) for x in (obs_slots, obs_values, obs_precision)
    )
    two_far = shape(3 * HALF + INIT, COLS)
    own, up2, dn2, obs = pl.pallas_call(
        collect,
        out_shape=[shape(OWN + INIT, COLS), two_far, two_far, shape(128, 128)],
        in_specs=[pl.BlockSpec(memory_space=pl.ANY)] * 5,
        out_specs=[VMEM] * 4,
        scratch_shapes=[pltpu.VMEM((16, COLS), F32)] * 2 + [pltpu.SemaphoreType.DMA((5,))],
    )(own_p, initial_height, initial_speed.reshape(16, COLS), values, precision)
    near = [moved(own, LAT, 1), moved(own, LAT, -1)]
    far = [moved(up2, LAT, 2), moved(dn2, LAT, -2)]
    own_other = swap(own)
    obs = lax.all_to_all(obs, LAT_LON, 0, 0, tiled=True)
    *halo, obs = lax.optimization_barrier((*near, *far, obs))
    blocks = [own, *halo]
    others = [own_other] + [swap(x) for x in halo]
    weights, observed = call(scatter_obs, [shape(2, 512, 128), shape(2, 512, 128)], pos, slots, obs)

    field = shape(EXT, WIDE, MEMBERS)
    half = shape(40, MEMBERS)
    square = shape(MEMBERS, MEMBERS)
    edge = shape(EDGE + 5 * INIT, MEMBERS)
    ext_fr, ext_fo, tiles, right, left = call(
        turn_rows, [field, field, shape(5 * INIT, COLS), edge, edge], pos, *blocks, *others
    )
    lz, rz = moved(right, LON_ENS, 1), moved(left, LON_ENS, -1)
    state = [pltpu.VMEM((EXT, WIDE, MEMBERS), F32)]
    ext_fr, ext_fo, table, keep, send = call(
        first_run, [field, field, square, half, half],
        pos, ext_fr, ext_fo, tiles, lz, rz, weights, observed,
        scratch=state * 3, aliases={1: 0, 2: 1},
    )
    parts = reduced(keep, send)
    k1, keep, send = call(
        second_run, [square, half, half],
        pos, parts, ext_fr, ext_fo, table, weights, observed,
        scratch=state * 5,
    )
    parts = reduced(keep, send)
    out = call(last_update, shape(2 * HALF * ROWS, COLS), pos, parts, k1, own_p, others[0])
    return out.reshape(parameters.shape)


def solution(mesh):
    torus = Mesh(
        mesh.devices.reshape(4, 4, mesh.shape["lon"], mesh.shape["ens"]),
        ("lat_0", "lat_1", "lon", "ens"),
    )
    in_specs = (
        P(None, "ens", LAT, "lon"),
        P(LAT, "lon"),
        P(None, LAT, "lon"),
        P(None, LAT_LON, None, None),
        P(None, LAT_LON, None, None),
        P(None, LAT_LON, None, None),
    )
    out_specs = P(None, "ens", LAT, "lon")
    return jax.shard_map(
        per_device, mesh=torus, in_specs=in_specs, out_specs=out_specs, check_vma=False
    )
```

```python
import functools

import jax
import jax.numpy as jnp
from jax import lax
from jax.experimental import pallas as pl
from jax.experimental.pallas import tpu as pltpu
from jax.sharding import Mesh
from jax.sharding import PartitionSpec as P

STEPS = 6
LAT = ("lat_0", "lat_1")
LAT_LON = ("lat_0", "lat_1", "lon")
LON_ENS = ("lon", "ens")

DEPTH = 0.7
GRAVITY = 0.7
CORIOLIS = 0.1

MEMBERS = 128
HALF = 64
ROWS = 8
COLS = 128
EXT = 28
WIDE = 112
LEFT = 24
RIGHT = LEFT + HALF
INIT = 24
GLOBAL_ROWS = 128
OWN = 2 * ROWS * HALF
PIVOTS = 16

F32 = jnp.float32
HIGHEST = lax.Precision.HIGHEST
VMEM = pl.BlockSpec(memory_space=pltpu.VMEM)
SMEM = pl.BlockSpec(memory_space=pltpu.SMEM)


def params():
    return pltpu.CompilerParams(vmem_limit_bytes=24 * 1024 * 1024)


def shape(*dims):
    return jax.ShapeDtypeStruct(dims, F32)


def iota(dims, axis):
    return lax.broadcasted_iota(jnp.int32, dims, axis)


def collect(own_hbm, height_hbm, speed_hbm, values_hbm, precision_hbm,
            out, up2, dn2, obs, values, precision, sems):
    pairs = (
        (values_hbm, values), (precision_hbm, precision), (own_hbm, out.at[:OWN]),
        (height_hbm, out.at[OWN : OWN + ROWS]), (speed_hbm, out.at[OWN + ROWS :]),
    )
    copies = [pltpu.make_async_copy(src, dst, sems.at[k]) for k, (src, dst) in enumerate(pairs)]
    for copy in copies:
        copy.start()
    for copy in copies[:2]:
        copy.wait()
    lines = [values[...], precision[...], jnp.zeros((96, MEMBERS), F32)]
    obs[...] = jnp.concatenate(lines, axis=0).T
    for copy in copies[2:]:
        copy.wait()
    for k, (f, up_row, down_row) in enumerate(((1, 6, 0), (1, 7, 1), (0, 7, 0))):
        start = f * HALF * ROWS
        up2[k * HALF : (k + 1) * HALF] = out[pl.ds(start + up_row, HALF, stride=ROWS), :]
        dn2[k * HALF : (k + 1) * HALF] = out[pl.ds(start + down_row, HALF, stride=ROWS), :]
    up2[3 * HALF :] = out[OWN:]
    dn2[3 * HALF :] = out[OWN:]


def edge_rows():
    rows = []
    for field, first in ((1, 0), (0, 1)):
        for r in range(first, EXT - first):
            away = max(10 - r, r - 17, 0)
            need = 9 + field - away
            rows.append((field, r, 16 if need > 8 else 8))
    return rows


EDGE_ROWS = edge_rows()
EDGE = sum(n for _, _, n in EDGE_ROWS)


def both_cores(first, mine, others, start, stride):
    lines = pl.ds(start, HALF, stride=stride)
    mine, others = mine[lines, :], others[lines, :]
    return jnp.concatenate([jnp.where(first, mine, others), jnp.where(first, others, mine)], axis=0)


def turn_rows(pos, own, m1, p1, m2, p2, own_o, m1_o, p1_o, m2_o, p2_o, FR, FO, tiles, right, left):
    def row_source(field, r):
        if 2 <= r < 26:
            which = (r - 2) // ROWS
            return (m1, own, p1)[which], (m1_o, own_o, p1_o)[which], field * HALF * ROWS + (r - 2) % ROWS, ROWS
        k = 2 if field == 0 else (r if r < 2 else r - 26)
        refs = (m2, m2_o) if r < 2 else (p2, p2_o)
        return *refs, k * HALF, 1

    first = pos[1] == 0
    at = 0
    for field, r, n in EDGE_ROWS:
        mine, others, start, stride = row_source(field, r)
        turned = both_cores(first, mine, others, start, stride).T
        turned = jnp.where(first, turned[:HALF], turned[HALF:])
        if field == 1 and not 10 <= r < 18:
            turned = jnp.where(inside(pos[0], r), turned, 0.0)
        (FO if field else FR)[r, LEFT:RIGHT] = turned
        right[at : at + n] = turned[HALF - n :]
        left[at : at + n] = turned[:n]
        at += n

    fields = ((m2, 3 * HALF), (m1, OWN), (own, OWN), (p1, OWN), (p2, 3 * HALF))
    for k, (ref, start) in enumerate(fields):
        tile = ref[start : start + INIT]
        for out, at in ((tiles, 0), (right, EDGE), (left, EDGE)):
            out[at + k * INIT : at + (k + 1) * INIT] = tile


def scatter_obs(pos, slots, received, weights, observed):
    received = received[...].T
    values, precision = received[:16], received[16:32]
    lines = ROWS * HALF
    k = iota((lines, MEMBERS), 0)
    cell = (k // HALF) * COLS + pos[1] * HALF + k % HALF
    for t in range(2):
        found_w = jnp.zeros((lines, MEMBERS), F32)
        found_y = jnp.zeros((lines, MEMBERS), F32)
        for s in range(8):
            at = t * 8 + s
            hit = cell == slots[at : at + 1, :]
            found_w = found_w + jnp.where(hit, precision[at : at + 1, :], 0.0)
            found_y = found_y + jnp.where(hit, values[at : at + 1, :], 0.0)
        weights[t] = jnp.broadcast_to(jnp.sum(found_w, axis=1, keepdims=True), (lines, MEMBERS))
        observed[t] = jnp.broadcast_to(jnp.sum(found_y, axis=1, keepdims=True), (lines, MEMBERS))


def inside(lat, r):
    row = lat * ROWS + r - 10
    return jnp.logical_and(row >= 0, row < GLOBAL_ROWS)


def initial_table(pos, tiles, lz, rz):
    lane = iota((ROWS, COLS), 1)
    row = iota((ROWS, COLS), 0)
    e = pos[1]
    fields = [[], [], []]
    for k in range(5):
        for f in range(3):
            at = k * INIT + f * ROWS
            own = tiles[at : at + ROWS]
            at += EDGE
            before = lz[at : at + ROWS]
            after = rz[at : at + ROWS]
            low = pltpu.roll(jnp.where(lane >= 112, before, own), 16, 1)
            high = pltpu.roll(jnp.where(lane < 16, after, own), 80, 1)
            window = jnp.where(e == 0, low, high)
            place = pos[0] * ROWS + (k - 2) * ROWS + row
            ok = jnp.logical_and(place >= 0, place < GLOBAL_ROWS)
            fields[f].append(jnp.where(ok, window, 0.0))
    h, u, v = (jnp.concatenate(f, axis=0) for f in fields)
    east = pltpu.roll(u, COLS - 1, 1) - pltpu.roll(u, 1, 1)
    north = jnp.concatenate([v[1:], v[:1]], axis=0) - jnp.concatenate([v[-1:], v[:-1]], axis=0)
    place = pos[0] * ROWS - 16 + iota((40, COLS), 0)
    ok = jnp.logical_and(place >= 0, place < GLOBAL_ROWS)
    base = jnp.where(ok, h - DEPTH * (east + north), 0.0)
    return jnp.concatenate([base, u, v, jnp.zeros((8, COLS), F32)], axis=0).T


def forward(lat, table, FR, FO, H, U, V):
    first = table[0:96]

    def start(f, r):
        lane = f * 40 + r + 6
        return jnp.broadcast_to(first[:, lane : lane + 1], (96, MEMBERS))

    def gains(r):
        ok = inside(lat, r)
        return jnp.where(ok, F32(GRAVITY), F32(0.0)), jnp.where(ok, F32(CORIOLIS), F32(0.0))

    for r in range(EXT):
        H[r, 8:104] = start(0, r) + FO[r, 8:104]
    for r in range(1, EXT - 1):
        g, c = gains(r)
        u, v = start(1, r), start(2, r)
        keep = 1.0 - FR[r, 8:104]
        U[r, 8:104] = keep * u - g * (H[r, 9:105] - H[r, 7:103]) + c * v
        V[r, 8:104] = keep * v - g * (H[r + 1, 8:104] - H[r - 1, 8:104]) - c * u

    def height_row(a, b, r):
        g, _ = gains(r)
        n = b - a
        east = U[r, pl.ds(a + 1, n)] - U[r, pl.ds(a - 1, n)]
        north = V[r + 1, pl.ds(a, n)] - V[r - 1, pl.ds(a, n)]
        H[r, pl.ds(a, n)] = H[r, pl.ds(a, n)] - g * (east + north) + FO[r, pl.ds(a, n)]

    def speed_row(a, b, r):
        g, c = gains(r)
        n = b - a
        u, v = U[r, pl.ds(a, n)], V[r, pl.ds(a, n)]
        keep = 1.0 - FR[r, pl.ds(a, n)]
        east = H[r, pl.ds(a + 1, n)] - H[r, pl.ds(a - 1, n)]
        north = H[r + 1, pl.ds(a, n)] - H[r - 1, pl.ds(a, n)]
        U[r, pl.ds(a, n)] = keep * u - g * east + c * v
        V[r, pl.ds(a, n)] = keep * v - g * north - c * u

    def sweep(row, reach, a, b):
        def body(i, carry):
            row(a, b, 10 - reach + 2 * i)
            row(a, b, 11 - reach + 2 * i)
            return carry

        lax.fori_loop(0, (ROWS + 2 * reach) // 2, body, 0)

    for step in range(1, STEPS):
        reach = 2 * (STEPS - 1 - step)
        a, b = (16, 96) if reach else (LEFT, RIGHT)
        sweep(height_row, reach, a, b)
        if reach:
            sweep(speed_row, reach - 1, a, b)


def gram(pos, H, weights, observed, keep, send):
    lines = ROWS * HALF
    h = H[10:18, LEFT:RIGHT].reshape(lines, MEMBERS)
    centre = jnp.mean(h, axis=1, keepdims=True)
    spread = h - centre
    weighted = spread * weights
    g = lax.dot_general(spread, weighted, (((0,), (0,)), ((), ())), precision=HIGHEST, preferred_element_type=F32)
    d = jnp.sum(weighted * (observed - centre), axis=0, keepdims=True)
    row, lane = iota((HALF, MEMBERS), 0), iota((HALF, MEMBERS), 1)
    top, bottom = g[:HALF], g[HALF:]
    packed = jnp.where(jnp.logical_and(lane < HALF, lane > row), pltpu.roll(bottom, HALF, 1), top)
    diagonal = jnp.sum(jnp.where(lane == row + HALF, bottom, 0.0), axis=0, keepdims=True)
    line = iota((8, MEMBERS), 0)
    rest = jnp.where(line == 0, d, jnp.where(line == 1, diagonal, 0.0))
    one = jnp.concatenate([packed[:32], rest], axis=0)
    two = jnp.concatenate([packed[32:], jnp.zeros((8, MEMBERS), F32)], axis=0)
    keep[...] = jnp.where(pos[1] == 0, one, two)
    send[...] = jnp.where(pos[1] == 0, two, one)


def first_run(pos, fr, fo, tiles, lz, rz, weights, observed, FR, FO, table, keep, send, H, U, V):
    del fr, fo
    at = 0
    for field, r, n in EDGE_ROWS:
        out = FO if field else FR
        out[r, LEFT - n : LEFT] = lz[at : at + n]
        out[r, RIGHT : RIGHT + n] = rz[at : at + n]
        at += n
    table[...] = initial_table(pos, tiles, lz, rz)
    forward(pos[0], table[...], FR, FO, H, U, V)
    gram(pos, H, weights[0], observed[0], keep, send)


def inverse(x):
    n = PIVOTS
    panels = [x[k : k + n] for k in range(0, MEMBERS, n)]
    row, lane = iota((n, MEMBERS), 0), iota((n, MEMBERS), 1)
    lower, scaled = [], []

    def spread(panel, column):
        return jnp.broadcast_to(panel[:, column : column + 1], (n, MEMBERS))

    for k in range(len(panels)):
        first = k * n
        block = jnp.logical_and(lane >= first, lane < first + n)
        columns = [spread(panels[k], first + j) for j in range(n)]
        top = jnp.where(block, jnp.where(lane - first == row, 1.0, 0.0), panels[k])
        lower.append(jnp.where(lane < first + n, top, 0.0))
        for j in range(n):
            over = 1.0 / columns[j][j : j + 1]

            def eliminate(m, j=j, over=over):
                pivot = m[j : j + 1] * over
                return jnp.where(row == j, pivot, m - columns[j] * pivot)

            top = eliminate(top)
            columns[j + 1 :] = [eliminate(m) for m in columns[j + 1 :]]
        scaled.append(jnp.where(lane < first + n, top, 0.0))
        for i in range(k + 1, len(panels)):
            terms = [spread(panels[i], first + j) * top[j : j + 1] for j in range(n)]
            while len(terms) > 1:
                terms = [a + b for a, b in zip(terms[::2], terms[1::2])]
            panels[i] = jnp.where(block, 0.0, panels[i]) - terms[0]
    lower, scaled = jnp.concatenate(lower, axis=0), jnp.concatenate(scaled, axis=0)
    return lax.dot_general(lower, scaled, (((0,), (0,)), ((), ())), precision=HIGHEST, preferred_element_type=F32)


def weights_of(pos, mine, other):
    one = jnp.where(pos[1] == 0, mine, other)
    two = jnp.where(pos[1] == 0, other, mine)
    packed = jnp.concatenate([one[:32], two[:32]], axis=0)
    d, diagonal = one[32:33], one[33:34]
    turned = jnp.concatenate([packed, jnp.zeros((HALF, MEMBERS), F32)], axis=0).T
    row, lane = iota((HALF, MEMBERS), 0), iota((HALF, MEMBERS), 1)
    a = jnp.where(lane <= row, packed, turned[:HALF])
    c = pltpu.roll(jnp.where(lane > row, packed, turned[:HALF]), HALF, 1)
    c = jnp.where(lane == row + HALF, diagonal, c)
    top = jnp.where(lane < HALF, a, packed)
    bottom = jnp.where(lane < HALF, turned[HALF:], c)
    g = jnp.concatenate([top, bottom], axis=0)
    row, lane = iota((MEMBERS, MEMBERS), 0), iota((MEMBERS, MEMBERS), 1)
    x = g * (1.0 / MEMBERS) + jnp.where(row == lane, 1.0, 0.0)
    x = inverse(x)
    shift = jnp.sum(x * d, axis=1, keepdims=True) * (1.0 / MEMBERS)
    z = x + shift
    return z - jnp.mean(z, axis=0, keepdims=True) + 1.0 / MEMBERS


def second_run(pos, mine, other, fr, fo, table, weights, observed, k1, keep, send, FR, FO, H, U, V):
    k = weights_of(pos, mine[...], other[...])
    k1[...] = k
    for src, out in ((fr, FR), (fo, FO)):
        old = src[:, 8:104].reshape(EXT * 96, MEMBERS)
        new = jnp.dot(old, k, precision=HIGHEST, preferred_element_type=F32)
        out[:, 8:104] = new.reshape(EXT, 96, MEMBERS)
    forward(pos[0], table[...], FR, FO, H, U, V)
    gram(pos, H, weights[1], observed[1], keep, send)


def last_update(pos, mine, other, k1, own_p, other_p, out):
    k = jnp.dot(k1[...], weights_of(pos, mine[...], other[...]), precision=HIGHEST, preferred_element_type=F32)

    first = pos[1] == 0
    kt = k.T
    kt = jnp.where(first, kt[:HALF], kt[HALF:])
    for start in [f * HALF * ROWS + r for f in range(2) for r in range(ROWS)]:
        block = both_cores(first, own_p, other_p, start, ROWS)
        out[pl.ds(start, HALF, stride=ROWS), :] = jnp.dot(kt, block, precision=HIGHEST, preferred_element_type=F32)


def swap(value):
    return lax.ppermute(value, "ens", [(0, 1), (1, 0)])


def moved(value, axes, by):
    n = lax.axis_size(axes)
    return lax.ppermute(value, axes, [(i, (i + by) % n) for i in range(n)])


def copied_sum(*refs):
    *parts, out = refs
    terms = [ref[k] for ref in parts for k in range(ref.shape[0])]
    total = terms[0]
    for term in terms[1:]:
        total = total + term
    for k in range(out.shape[0]):
        out[k] = total


def summed(copies, *parts):
    return pl.pallas_call(
        copied_sum,
        out_shape=shape(copies, *parts[0].shape[1:]),
        in_specs=[VMEM] * len(parts),
        out_specs=VMEM,
        compiler_params=pltpu.CompilerParams(vmem_limit_bytes=4 * 1024 * 1024),
    )(*parts)


def reduced(keep, send):
    parts = keep[None], swap(send)[None]
    for axes in (LAT, "lon"):
        parts = [lax.all_to_all(summed(lax.axis_size(axes), *parts), axes, 0, 0, tiled=True)]
    value = summed(1, *parts)[0]
    return value, swap(value)


def call(kernel, out_shape, scalars, *args, scratch=(), aliases=None):
    return pl.pallas_call(
        kernel,
        out_shape=out_shape,
        in_specs=[SMEM] + [VMEM] * len(args),
        out_specs=jax.tree.map(lambda _: VMEM, out_shape),
        scratch_shapes=list(scratch),
        input_output_aliases=aliases or {},
        compiler_params=params(),
    )(scalars, *args)


def per_device(parameters, initial_height, initial_speed, obs_slots, obs_values, obs_precision):
    pos = jnp.stack([lax.axis_index(LAT), lax.axis_index("ens")]).astype(jnp.int32)
    own_p = parameters.reshape(2 * HALF * ROWS, COLS)
    slots, values, precision = (
        x[:, 0].transpose(0, 2, 1).reshape(16, 128) for x in (obs_slots, obs_values, obs_precision)
    )
    two_far = shape(3 * HALF + INIT, COLS)
    own, up2, dn2, obs = pl.pallas_call(
        collect,
        out_shape=[shape(OWN + INIT, COLS), two_far, two_far, shape(128, 128)],
        in_specs=[pl.BlockSpec(memory_space=pl.ANY)] * 5,
        out_specs=[VMEM] * 4,
        scratch_shapes=[pltpu.VMEM((16, COLS), F32)] * 2 + [pltpu.SemaphoreType.DMA((5,))],
    )(own_p, initial_height, initial_speed.reshape(16, COLS), values, precision)
    near = [moved(own, LAT, 1), moved(own, LAT, -1)]
    far = [moved(up2, LAT, 2), moved(dn2, LAT, -2)]
    own_other = swap(own)
    obs = lax.all_to_all(obs, LAT_LON, 0, 0, tiled=True)
    *halo, obs = lax.optimization_barrier((*near, *far, obs))
    blocks = [own, *halo]
    others = [own_other] + [swap(x) for x in halo]
    weights, observed = call(scatter_obs, [shape(2, 512, 128), shape(2, 512, 128)], pos, slots, obs)

    field = shape(EXT, WIDE, MEMBERS)
    half = shape(40, MEMBERS)
    square = shape(MEMBERS, MEMBERS)
    edge = shape(EDGE + 5 * INIT, MEMBERS)
    ext_fr, ext_fo, tiles, right, left = call(
        turn_rows, [field, field, shape(5 * INIT, COLS), edge, edge], pos, *blocks, *others
    )
    lz, rz = moved(right, LON_ENS, 1), moved(left, LON_ENS, -1)
    state = [pltpu.VMEM((EXT, WIDE, MEMBERS), F32)]
    ext_fr, ext_fo, table, keep, send = call(
        first_run, [field, field, square, half, half],
        pos, ext_fr, ext_fo, tiles, lz, rz, weights, observed,
        scratch=state * 3, aliases={1: 0, 2: 1},
    )
    mine, other = reduced(keep, send)
    k1, keep, send = call(
        second_run, [square, half, half],
        pos, mine, other, ext_fr, ext_fo, table, weights, observed,
        scratch=state * 5,
    )
    mine, other = reduced(keep, send)
    out = call(last_update, shape(2 * HALF * ROWS, COLS), pos, mine, other, k1, own_p, others[0])
    return out.reshape(parameters.shape)


def solution(mesh):
    torus = Mesh(
        mesh.devices.reshape(4, 4, mesh.shape["lon"], mesh.shape["ens"]),
        ("lat_0", "lat_1", "lon", "ens"),
    )
    in_specs = (
        P(None, "ens", LAT, "lon"),
        P(LAT, "lon"),
        P(None, LAT, "lon"),
        P(None, LAT_LON, None, None),
        P(None, LAT_LON, None, None),
        P(None, LAT_LON, None, None),
    )
    out_specs = P(None, "ens", LAT, "lon")
    return jax.shard_map(
        per_device, mesh=torus, in_specs=in_specs, out_specs=out_specs, check_vma=False
    )
```

```python
import functools

import jax
import jax.numpy as jnp
from jax import lax
from jax.experimental import pallas as pl
from jax.experimental.pallas import tpu as pltpu
from jax.sharding import Mesh
from jax.sharding import PartitionSpec as P

STEPS = 6
LAT = ("lat_0", "lat_1")
LAT_LON = ("lat_0", "lat_1", "lon")
LON_ENS = ("lon", "ens")

DEPTH = 0.7
GRAVITY = 0.7
CORIOLIS = 0.1

MEMBERS = 128
HALF = 64
ROWS = 8
COLS = 128
EXT = 28
WIDE = 112
LEFT = 24
RIGHT = LEFT + HALF
INIT = 24
GLOBAL_ROWS = 128
OWN = 2 * ROWS * HALF
PIVOTS = 16

F32 = jnp.float32
HIGHEST = lax.Precision.HIGHEST
VMEM = pl.BlockSpec(memory_space=pltpu.VMEM)
SMEM = pl.BlockSpec(memory_space=pltpu.SMEM)


def params():
    return pltpu.CompilerParams(vmem_limit_bytes=24 * 1024 * 1024)


def shape(*dims):
    return jax.ShapeDtypeStruct(dims, F32)


def iota(dims, axis):
    return lax.broadcasted_iota(jnp.int32, dims, axis)


def collect(own_hbm, height_hbm, speed_hbm, values_hbm, precision_hbm,
            out, up2, dn2, obs, values, precision, sems):
    pairs = (
        (values_hbm, values), (precision_hbm, precision), (own_hbm, out.at[:OWN]),
        (height_hbm, out.at[OWN : OWN + ROWS]), (speed_hbm, out.at[OWN + ROWS :]),
    )
    copies = [pltpu.make_async_copy(src, dst, sems.at[k]) for k, (src, dst) in enumerate(pairs)]
    for copy in copies:
        copy.start()
    for copy in copies[:2]:
        copy.wait()
    lines = [values[...], precision[...], jnp.zeros((96, MEMBERS), F32)]
    obs[...] = jnp.concatenate(lines, axis=0).T
    for copy in copies[2:]:
        copy.wait()
    for k, (f, up_row, down_row) in enumerate(((1, 6, 0), (1, 7, 1), (0, 7, 0))):
        start = f * HALF * ROWS
        up2[k * HALF : (k + 1) * HALF] = out[pl.ds(start + up_row, HALF, stride=ROWS), :]
        dn2[k * HALF : (k + 1) * HALF] = out[pl.ds(start + down_row, HALF, stride=ROWS), :]
    up2[3 * HALF :] = out[OWN:]
    dn2[3 * HALF :] = out[OWN:]


def edge_rows():
    rows = []
    for field, first in ((1, 0), (0, 1)):
        for r in range(first, EXT - first):
            rows.append((field, r, 9 + field - max(10 - r, r - 17, 0)))
    return rows


EDGE_ROWS = edge_rows()
EDGE = (sum(n for _, _, n in EDGE_ROWS) + 7) // 8 * 8
NEAR = 16


def both_cores(first, mine, others, start, stride):
    lines = pl.ds(start, HALF, stride=stride)
    mine, others = mine[lines, :], others[lines, :]
    return jnp.concatenate([jnp.where(first, mine, others), jnp.where(first, others, mine)], axis=0)


def turn_rows(pos, own, m1, p1, m2, p2, own_o, m1_o, p1_o, m2_o, p2_o, FR, FO, tiles, right, left):
    def row_source(field, r):
        if 2 <= r < 26:
            which = (r - 2) // ROWS
            return (m1, own, p1)[which], (m1_o, own_o, p1_o)[which], field * HALF * ROWS + (r - 2) % ROWS, ROWS
        k = 2 if field == 0 else (r if r < 2 else r - 26)
        refs = (m2, m2_o) if r < 2 else (p2, p2_o)
        return *refs, k * HALF, 1

    first = pos[1] == 0
    at = 0
    for field, r, n in EDGE_ROWS:
        mine, others, start, stride = row_source(field, r)
        turned = both_cores(first, mine, others, start, stride).T
        turned = jnp.where(first, turned[:HALF], turned[HALF:])
        if field == 1 and not 10 <= r < 18:
            turned = jnp.where(inside(pos[0], r), turned, 0.0)
        (FO if field else FR)[r, LEFT:RIGHT] = turned
        if n:
            right[at : at + n] = turned[HALF - n :]
            left[at : at + n] = turned[:n]
        at += n

    fields = ((m2, 3 * HALF), (m1, OWN), (own, OWN), (p1, OWN), (p2, 3 * HALF))
    slot = iota((ROWS, COLS), 1) // NEAR
    packed = [[jnp.zeros((ROWS, COLS), F32)] * 2, [jnp.zeros((ROWS, COLS), F32)] * 2]
    for k, (ref, start) in enumerate(fields):
        for f in range(3):
            j = 3 * k + f
            tile = ref[start + f * ROWS : start + (f + 1) * ROWS]
            tiles[j * ROWS : (j + 1) * ROWS] = tile
            for side, first_lane in ((0, COLS - NEAR), (1, 0)):
                there = pltpu.roll(tile, (NEAR * (j % 8) - first_lane) % COLS, 1)
                packed[side][j // 8] = jnp.where(slot == j % 8, there, packed[side][j // 8])
    for side, out in ((0, right), (1, left)):
        out[EDGE : EDGE + ROWS] = packed[side][0]
        out[EDGE + ROWS : EDGE + 2 * ROWS] = packed[side][1]


def scatter_obs(pos, slots, received, weights, observed):
    received = received[...].T
    values, precision = received[:16], received[16:32]
    lines = ROWS * HALF
    k = iota((lines, MEMBERS), 0)
    cell = (k // HALF) * COLS + pos[1] * HALF + k % HALF
    for t in range(2):
        found_w = jnp.zeros((lines, MEMBERS), F32)
        found_y = jnp.zeros((lines, MEMBERS), F32)
        for s in range(8):
            at = t * 8 + s
            hit = cell == slots[at : at + 1, :]
            found_w = found_w + jnp.where(hit, precision[at : at + 1, :], 0.0)
            found_y = found_y + jnp.where(hit, values[at : at + 1, :], 0.0)
        weights[t] = jnp.broadcast_to(jnp.sum(found_w, axis=1, keepdims=True), (lines, MEMBERS))
        observed[t] = jnp.broadcast_to(jnp.sum(found_y, axis=1, keepdims=True), (lines, MEMBERS))


def inside(lat, r):
    row = lat * ROWS + r - 10
    return jnp.logical_and(row >= 0, row < GLOBAL_ROWS)


def initial_table(pos, tiles, lz, rz):
    lane = iota((ROWS, COLS), 1)
    row = iota((ROWS, COLS), 0)
    e = pos[1]
    fields = [[], [], []]
    for k in range(5):
        for f in range(3):
            at = k * INIT + f * ROWS
            own = tiles[at : at + ROWS]
            j = 3 * k + f
            at = EDGE + j // 8 * ROWS
            before = pltpu.roll(lz[at : at + ROWS], (COLS - NEAR - NEAR * (j % 8)) % COLS, 1)
            after = pltpu.roll(rz[at : at + ROWS], -NEAR * (j % 8) % COLS, 1)
            low = pltpu.roll(jnp.where(lane >= 112, before, own), 16, 1)
            high = pltpu.roll(jnp.where(lane < 16, after, own), 80, 1)
            window = jnp.where(e == 0, low, high)
            place = pos[0] * ROWS + (k - 2) * ROWS + row
            ok = jnp.logical_and(place >= 0, place < GLOBAL_ROWS)
            fields[f].append(jnp.where(ok, window, 0.0))
    h, u, v = (jnp.concatenate(f, axis=0) for f in fields)
    east = pltpu.roll(u, COLS - 1, 1) - pltpu.roll(u, 1, 1)
    north = jnp.concatenate([v[1:], v[:1]], axis=0) - jnp.concatenate([v[-1:], v[:-1]], axis=0)
    place = pos[0] * ROWS - 16 + iota((40, COLS), 0)
    ok = jnp.logical_and(place >= 0, place < GLOBAL_ROWS)
    base = jnp.where(ok, h - DEPTH * (east + north), 0.0)
    return jnp.concatenate([base, u, v, jnp.zeros((8, COLS), F32)], axis=0).T


def forward(lat, table, FR, FO, H, U, V):
    first = table[0:96]

    def start(f, r):
        lane = f * 40 + r + 6
        return jnp.broadcast_to(first[:, lane : lane + 1], (96, MEMBERS))

    def gains(r):
        ok = inside(lat, r)
        return jnp.where(ok, F32(GRAVITY), F32(0.0)), jnp.where(ok, F32(CORIOLIS), F32(0.0))

    for r in range(EXT):
        H[r, 8:104] = start(0, r) + FO[r, 8:104]
    for r in range(1, EXT - 1):
        g, c = gains(r)
        u, v = start(1, r), start(2, r)
        keep = 1.0 - FR[r, 8:104]
        U[r, 8:104] = keep * u - g * (H[r, 9:105] - H[r, 7:103]) + c * v
        V[r, 8:104] = keep * v - g * (H[r + 1, 8:104] - H[r - 1, 8:104]) - c * u

    def height_row(a, b, r):
        g, _ = gains(r)
        n = b - a
        east = U[r, pl.ds(a + 1, n)] - U[r, pl.ds(a - 1, n)]
        north = V[r + 1, pl.ds(a, n)] - V[r - 1, pl.ds(a, n)]
        H[r, pl.ds(a, n)] = H[r, pl.ds(a, n)] - g * (east + north) + FO[r, pl.ds(a, n)]

    def speed_row(a, b, r):
        g, c = gains(r)
        n = b - a
        u, v = U[r, pl.ds(a, n)], V[r, pl.ds(a, n)]
        keep = 1.0 - FR[r, pl.ds(a, n)]
        east = H[r, pl.ds(a + 1, n)] - H[r, pl.ds(a - 1, n)]
        north = H[r + 1, pl.ds(a, n)] - H[r - 1, pl.ds(a, n)]
        U[r, pl.ds(a, n)] = keep * u - g * east + c * v
        V[r, pl.ds(a, n)] = keep * v - g * north - c * u

    def sweep(row, reach, a, b):
        def body(i, carry):
            row(a, b, 10 - reach + 2 * i)
            row(a, b, 11 - reach + 2 * i)
            return carry

        lax.fori_loop(0, (ROWS + 2 * reach) // 2, body, 0)

    for step in range(1, STEPS):
        reach = 2 * (STEPS - 1 - step)
        a, b = (16, 96) if reach else (LEFT, RIGHT)
        sweep(height_row, reach, a, b)
        if reach:
            sweep(speed_row, reach - 1, a, b)


def gram(pos, H, weights, observed, keep, send):
    lines = ROWS * HALF
    h = H[10:18, LEFT:RIGHT].reshape(lines, MEMBERS)
    centre = jnp.mean(h, axis=1, keepdims=True)
    spread = h - centre
    weighted = spread * weights
    g = lax.dot_general(spread, weighted, (((0,), (0,)), ((), ())), precision=HIGHEST, preferred_element_type=F32)
    d = jnp.sum(weighted * (observed - centre), axis=0, keepdims=True)
    row, lane = iota((HALF, MEMBERS), 0), iota((HALF, MEMBERS), 1)
    top, bottom = g[:HALF], g[HALF:]
    packed = jnp.where(jnp.logical_and(lane < HALF, lane > row), pltpu.roll(bottom, HALF, 1), top)
    diagonal = jnp.sum(jnp.where(lane == row + HALF, bottom, 0.0), axis=0, keepdims=True)
    line = iota((8, MEMBERS), 0)
    rest = jnp.where(line == 0, d, jnp.where(line == 1, diagonal, 0.0))
    one = jnp.concatenate([packed[:32], rest], axis=0)
    two = jnp.concatenate([packed[32:], jnp.zeros((8, MEMBERS), F32)], axis=0)
    keep[...] = jnp.where(pos[1] == 0, one, two)
    send[...] = jnp.where(pos[1] == 0, two, one)


def first_run(pos, fr, fo, tiles, lz, rz, weights, observed, FR, FO, table, keep, send, H, U, V):
    del fr, fo
    at = 0
    for field, r, n in EDGE_ROWS:
        out = FO if field else FR
        if n:
            out[r, LEFT - n : LEFT] = lz[at : at + n]
            out[r, RIGHT : RIGHT + n] = rz[at : at + n]
        at += n
    table[...] = initial_table(pos, tiles, lz, rz)
    forward(pos[0], table[...], FR, FO, H, U, V)
    gram(pos, H, weights[0], observed[0], keep, send)


def inverse(x):
    n = PIVOTS
    panels = [x[k : k + n] for k in range(0, MEMBERS, n)]
    row, lane = iota((n, MEMBERS), 0), iota((n, MEMBERS), 1)
    lower, scaled = [], []

    def spread(panel, column):
        return jnp.broadcast_to(panel[:, column : column + 1], (n, MEMBERS))

    for k in range(len(panels)):
        first = k * n
        block = jnp.logical_and(lane >= first, lane < first + n)
        columns = [spread(panels[k], first + j) for j in range(n)]
        top = jnp.where(block, jnp.where(lane - first == row, 1.0, 0.0), panels[k])
        lower.append(jnp.where(lane < first + n, top, 0.0))
        for j in range(n):
            over = 1.0 / columns[j][j : j + 1]

            def eliminate(m, j=j, over=over):
                pivot = m[j : j + 1] * over
                return jnp.where(row == j, pivot, m - columns[j] * pivot)

            top = eliminate(top)
            columns[j + 1 :] = [eliminate(m) for m in columns[j + 1 :]]
        scaled.append(jnp.where(lane < first + n, top, 0.0))
        for i in range(k + 1, len(panels)):
            terms = [spread(panels[i], first + j) * top[j : j + 1] for j in range(n)]
            while len(terms) > 1:
                terms = [a + b for a, b in zip(terms[::2], terms[1::2])]
            panels[i] = jnp.where(block, 0.0, panels[i]) - terms[0]
    lower, scaled = jnp.concatenate(lower, axis=0), jnp.concatenate(scaled, axis=0)
    return lax.dot_general(lower, scaled, (((0,), (0,)), ((), ())), precision=HIGHEST, preferred_element_type=F32)


def weights_of(pos, mine, other):
    one = jnp.where(pos[1] == 0, mine, other)
    two = jnp.where(pos[1] == 0, other, mine)
    packed = jnp.concatenate([one[:32], two[:32]], axis=0)
    d, diagonal = one[32:33], one[33:34]
    turned = jnp.concatenate([packed, jnp.zeros((HALF, MEMBERS), F32)], axis=0).T
    row, lane = iota((HALF, MEMBERS), 0), iota((HALF, MEMBERS), 1)
    a = jnp.where(lane <= row, packed, turned[:HALF])
    c = pltpu.roll(jnp.where(lane > row, packed, turned[:HALF]), HALF, 1)
    c = jnp.where(lane == row + HALF, diagonal, c)
    top = jnp.where(lane < HALF, a, packed)
    bottom = jnp.where(lane < HALF, turned[HALF:], c)
    g = jnp.concatenate([top, bottom], axis=0)
    row, lane = iota((MEMBERS, MEMBERS), 0), iota((MEMBERS, MEMBERS), 1)
    x = g * (1.0 / MEMBERS) + jnp.where(row == lane, 1.0, 0.0)
    x = inverse(x)
    shift = jnp.sum(x * d, axis=1, keepdims=True) * (1.0 / MEMBERS)
    z = x + shift
    return z - jnp.mean(z, axis=0, keepdims=True) + 1.0 / MEMBERS


def second_run(pos, mine, other, fr, fo, table, weights, observed, k1, keep, send, FR, FO, H, U, V):
    k = weights_of(pos, mine[...], other[...])
    k1[...] = k
    for src, out in ((fr, FR), (fo, FO)):
        old = src[:, 8:104].reshape(EXT * 96, MEMBERS)
        new = jnp.dot(old, k, precision=HIGHEST, preferred_element_type=F32)
        out[:, 8:104] = new.reshape(EXT, 96, MEMBERS)
    forward(pos[0], table[...], FR, FO, H, U, V)
    gram(pos, H, weights[1], observed[1], keep, send)


def last_update(pos, mine, other, k1, own_p, other_p, out):
    k = jnp.dot(k1[...], weights_of(pos, mine[...], other[...]), precision=HIGHEST, preferred_element_type=F32)

    first = pos[1] == 0
    kt = k.T
    kt = jnp.where(first, kt[:HALF], kt[HALF:])
    for start in [f * HALF * ROWS + r for f in range(2) for r in range(ROWS)]:
        block = both_cores(first, own_p, other_p, start, ROWS)
        out[pl.ds(start, HALF, stride=ROWS), :] = jnp.dot(kt, block, precision=HIGHEST, preferred_element_type=F32)


def swap(value):
    return lax.ppermute(value, "ens", [(0, 1), (1, 0)])


def moved(value, axes, by):
    n = lax.axis_size(axes)
    return lax.ppermute(value, axes, [(i, (i + by) % n) for i in range(n)])


def copied_sum(*refs):
    *parts, out = refs
    terms = [ref[k] for ref in parts for k in range(ref.shape[0])]
    total = terms[0]
    for term in terms[1:]:
        total = total + term
    for k in range(out.shape[0]):
        out[k] = total


def summed(copies, *parts):
    return pl.pallas_call(
        copied_sum,
        out_shape=shape(copies, *parts[0].shape[1:]),
        in_specs=[VMEM] * len(parts),
        out_specs=VMEM,
        compiler_params=pltpu.CompilerParams(vmem_limit_bytes=4 * 1024 * 1024),
    )(*parts)


def reduced(keep, send):
    parts = keep[None], swap(send)[None]
    for axes in (LAT, "lon"):
        parts = [lax.all_to_all(summed(lax.axis_size(axes), *parts), axes, 0, 0, tiled=True)]
    value = summed(1, *parts)[0]
    return value, swap(value)


def call(kernel, out_shape, scalars, *args, scratch=(), aliases=None):
    return pl.pallas_call(
        kernel,
        out_shape=out_shape,
        in_specs=[SMEM] + [VMEM] * len(args),
        out_specs=jax.tree.map(lambda _: VMEM, out_shape),
        scratch_shapes=list(scratch),
        input_output_aliases=aliases or {},
        compiler_params=params(),
    )(scalars, *args)


def per_device(parameters, initial_height, initial_speed, obs_slots, obs_values, obs_precision):
    pos = jnp.stack([lax.axis_index(LAT), lax.axis_index("ens")]).astype(jnp.int32)
    own_p = parameters.reshape(2 * HALF * ROWS, COLS)
    slots, values, precision = (
        x[:, 0].transpose(0, 2, 1).reshape(16, 128) for x in (obs_slots, obs_values, obs_precision)
    )
    two_far = shape(3 * HALF + INIT, COLS)
    own, up2, dn2, obs = pl.pallas_call(
        collect,
        out_shape=[shape(OWN + INIT, COLS), two_far, two_far, shape(128, 128)],
        in_specs=[pl.BlockSpec(memory_space=pl.ANY)] * 5,
        out_specs=[VMEM] * 4,
        scratch_shapes=[pltpu.VMEM((16, COLS), F32)] * 2 + [pltpu.SemaphoreType.DMA((5,))],
    )(own_p, initial_height, initial_speed.reshape(16, COLS), values, precision)
    near = [moved(own, LAT, 1), moved(own, LAT, -1)]
    far = [moved(up2, LAT, 2), moved(dn2, LAT, -2)]
    own_other = swap(own)
    obs = lax.all_to_all(obs, LAT_LON, 0, 0, tiled=True)
    *halo, obs = lax.optimization_barrier((*near, *far, obs))
    blocks = [own, *halo]
    others = [own_other] + [swap(x) for x in halo]
    weights, observed = call(scatter_obs, [shape(2, 512, 128), shape(2, 512, 128)], pos, slots, obs)

    field = shape(EXT, WIDE, MEMBERS)
    half = shape(40, MEMBERS)
    square = shape(MEMBERS, MEMBERS)
    edge = shape(EDGE + 2 * ROWS, MEMBERS)
    ext_fr, ext_fo, tiles, right, left = call(
        turn_rows, [field, field, shape(5 * INIT, COLS), edge, edge], pos, *blocks, *others
    )
    lz, rz = moved(right, LON_ENS, 1), moved(left, LON_ENS, -1)
    state = [pltpu.VMEM((EXT, WIDE, MEMBERS), F32)]
    ext_fr, ext_fo, table, keep, send = call(
        first_run, [field, field, square, half, half],
        pos, ext_fr, ext_fo, tiles, lz, rz, weights, observed,
        scratch=state * 3, aliases={1: 0, 2: 1},
    )
    mine, other = reduced(keep, send)
    k1, keep, send = call(
        second_run, [square, half, half],
        pos, mine, other, ext_fr, ext_fo, table, weights, observed,
        scratch=state * 5,
    )
    mine, other = reduced(keep, send)
    out = call(last_update, shape(2 * HALF * ROWS, COLS), pos, mine, other, k1, own_p, others[0])
    return out.reshape(parameters.shape)


def solution(mesh):
    torus = Mesh(
        mesh.devices.reshape(4, 4, mesh.shape["lon"], mesh.shape["ens"]),
        ("lat_0", "lat_1", "lon", "ens"),
    )
    in_specs = (
        P(None, "ens", LAT, "lon"),
        P(LAT, "lon"),
        P(None, LAT, "lon"),
        P(None, LAT_LON, None, None),
        P(None, LAT_LON, None, None),
        P(None, LAT_LON, None, None),
    )
    out_specs = P(None, "ens", LAT, "lon")
    return jax.shard_map(
        per_device, mesh=torus, in_specs=in_specs, out_specs=out_specs, check_vma=False
    )
```

```python
import functools

import jax
import jax.numpy as jnp
from jax import lax
from jax.experimental import pallas as pl
from jax.experimental.pallas import tpu as pltpu
from jax.sharding import Mesh
from jax.sharding import PartitionSpec as P

STEPS = 6
LAT = ("lat_0", "lat_1")
LAT_LON = ("lat_0", "lat_1", "lon")
LON_ENS = ("lon", "ens")

DEPTH = 0.7
GRAVITY = 0.7
CORIOLIS = 0.1

MEMBERS = 128
HALF = 64
ROWS = 8
COLS = 128
EXT = 28
WIDE = 112
LEFT = 24
RIGHT = LEFT + HALF
INIT = 24
GLOBAL_ROWS = 128
OWN = 2 * ROWS * HALF
PIVOTS = 16

F32 = jnp.float32
HIGHEST = lax.Precision.HIGHEST
VMEM = pl.BlockSpec(memory_space=pltpu.VMEM)
SMEM = pl.BlockSpec(memory_space=pltpu.SMEM)


def params():
    return pltpu.CompilerParams(vmem_limit_bytes=24 * 1024 * 1024)


def shape(*dims):
    return jax.ShapeDtypeStruct(dims, F32)


def iota(dims, axis):
    return lax.broadcasted_iota(jnp.int32, dims, axis)


def collect(own_hbm, height_hbm, speed_hbm, values_hbm, precision_hbm,
            out, up2, dn2, obs, values, precision, sems):
    pairs = (
        (values_hbm, values), (precision_hbm, precision), (own_hbm, out.at[:OWN]),
        (height_hbm, out.at[OWN : OWN + ROWS]), (speed_hbm, out.at[OWN + ROWS :]),
    )
    copies = [pltpu.make_async_copy(src, dst, sems.at[k]) for k, (src, dst) in enumerate(pairs)]
    for copy in copies:
        copy.start()
    for copy in copies[:2]:
        copy.wait()
    lines = [values[...], precision[...], jnp.zeros((96, MEMBERS), F32)]
    obs[...] = jnp.concatenate(lines, axis=0).T
    for copy in copies[2:]:
        copy.wait()
    for k, (f, up_row, down_row) in enumerate(((1, 6, 0), (1, 7, 1), (0, 7, 0))):
        start = f * HALF * ROWS
        up2[k * HALF : (k + 1) * HALF] = out[pl.ds(start + up_row, HALF, stride=ROWS), :]
        dn2[k * HALF : (k + 1) * HALF] = out[pl.ds(start + down_row, HALF, stride=ROWS), :]
    up2[3 * HALF :] = out[OWN:]
    dn2[3 * HALF :] = out[OWN:]


def edge_rows():
    rows = []
    for field, first in ((1, 0), (0, 1)):
        for r in range(first, EXT - first):
            rows.append((field, r, 9 + field - max(10 - r, r - 17, 0)))
    return rows


EDGE_ROWS = edge_rows()
EDGE = (sum(n for _, _, n in EDGE_ROWS) + 7) // 8 * 8
NEAR = 16


def both_cores(first, mine, others, start, stride):
    lines = pl.ds(start, HALF, stride=stride)
    mine, others = mine[lines, :], others[lines, :]
    return jnp.concatenate([jnp.where(first, mine, others), jnp.where(first, others, mine)], axis=0)


def turn_own(pos, own, own_o, out):
    first = pos[1] == 0
    for k in range(2 * ROWS):
        turned = both_cores(first, own, own_o, k // ROWS * HALF * ROWS + k % ROWS, ROWS).T
        out[k * HALF : (k + 1) * HALF] = jnp.where(first, turned[:HALF], turned[HALF:])
    out[OWN:] = own[OWN:]


def turn_rows(pos, own, m1, p1, m2, p2, m1_o, p1_o, m2_o, p2_o, FR, FO, tiles, right, left):
    def row_source(field, r):
        if 2 <= r < 10:
            return m1, m1_o, field * HALF * ROWS + r - 2, ROWS
        if 18 <= r < 26:
            return p1, p1_o, field * HALF * ROWS + r - 18, ROWS
        k = 2 if field == 0 else (r if r < 2 else r - 26)
        refs = (m2, m2_o) if r < 2 else (p2, p2_o)
        return *refs, k * HALF, 1

    first = pos[1] == 0
    at = 0
    for field, r, n in EDGE_ROWS:
        if 10 <= r < 18:
            k = field * ROWS + r - 10
            turned = own[k * HALF : (k + 1) * HALF]
        else:
            turned = both_cores(first, *row_source(field, r)).T
            turned = jnp.where(first, turned[:HALF], turned[HALF:])
            if field == 1:
                turned = jnp.where(inside(pos[0], r), turned, 0.0)
        (FO if field else FR)[r, LEFT:RIGHT] = turned
        if n:
            right[at : at + n] = turned[HALF - n :]
            left[at : at + n] = turned[:n]
        at += n

    fields = ((m2, 3 * HALF), (m1, OWN), (own, OWN), (p1, OWN), (p2, 3 * HALF))
    slot = iota((ROWS, COLS), 1) // NEAR
    packed = [[jnp.zeros((ROWS, COLS), F32)] * 2, [jnp.zeros((ROWS, COLS), F32)] * 2]
    for k, (ref, start) in enumerate(fields):
        for f in range(3):
            j = 3 * k + f
            tile = ref[start + f * ROWS : start + (f + 1) * ROWS]
            tiles[j * ROWS : (j + 1) * ROWS] = tile
            for side, first_lane in ((0, COLS - NEAR), (1, 0)):
                there = pltpu.roll(tile, (NEAR * (j % 8) - first_lane) % COLS, 1)
                packed[side][j // 8] = jnp.where(slot == j % 8, there, packed[side][j // 8])
    for side, out in ((0, right), (1, left)):
        out[EDGE : EDGE + ROWS] = packed[side][0]
        out[EDGE + ROWS : EDGE + 2 * ROWS] = packed[side][1]


def scatter_obs(pos, slots, received, weights, observed):
    received = received[...].T
    values, precision = received[:16], received[16:32]
    lines = ROWS * HALF
    k = iota((lines, MEMBERS), 0)
    cell = (k // HALF) * COLS + pos[1] * HALF + k % HALF
    for t in range(2):
        found_w = jnp.zeros((lines, MEMBERS), F32)
        found_y = jnp.zeros((lines, MEMBERS), F32)
        for s in range(8):
            at = t * 8 + s
            hit = cell == slots[at : at + 1, :]
            found_w = found_w + jnp.where(hit, precision[at : at + 1, :], 0.0)
            found_y = found_y + jnp.where(hit, values[at : at + 1, :], 0.0)
        weights[t] = jnp.broadcast_to(jnp.sum(found_w, axis=1, keepdims=True), (lines, MEMBERS))
        observed[t] = jnp.broadcast_to(jnp.sum(found_y, axis=1, keepdims=True), (lines, MEMBERS))


def inside(lat, r):
    row = lat * ROWS + r - 10
    return jnp.logical_and(row >= 0, row < GLOBAL_ROWS)


def initial_table(pos, tiles, lz, rz):
    lane = iota((ROWS, COLS), 1)
    row = iota((ROWS, COLS), 0)
    e = pos[1]
    fields = [[], [], []]
    for k in range(5):
        for f in range(3):
            at = k * INIT + f * ROWS
            own = tiles[at : at + ROWS]
            j = 3 * k + f
            at = EDGE + j // 8 * ROWS
            before = pltpu.roll(lz[at : at + ROWS], (COLS - NEAR - NEAR * (j % 8)) % COLS, 1)
            after = pltpu.roll(rz[at : at + ROWS], -NEAR * (j % 8) % COLS, 1)
            low = pltpu.roll(jnp.where(lane >= 112, before, own), 16, 1)
            high = pltpu.roll(jnp.where(lane < 16, after, own), 80, 1)
            window = jnp.where(e == 0, low, high)
            place = pos[0] * ROWS + (k - 2) * ROWS + row
            ok = jnp.logical_and(place >= 0, place < GLOBAL_ROWS)
            fields[f].append(jnp.where(ok, window, 0.0))
    h, u, v = (jnp.concatenate(f, axis=0) for f in fields)
    east = pltpu.roll(u, COLS - 1, 1) - pltpu.roll(u, 1, 1)
    north = jnp.concatenate([v[1:], v[:1]], axis=0) - jnp.concatenate([v[-1:], v[:-1]], axis=0)
    place = pos[0] * ROWS - 16 + iota((40, COLS), 0)
    ok = jnp.logical_and(place >= 0, place < GLOBAL_ROWS)
    base = jnp.where(ok, h - DEPTH * (east + north), 0.0)
    return jnp.concatenate([base, u, v, jnp.zeros((8, COLS), F32)], axis=0).T


def forward(lat, table, FR, FO, H, U, V):
    first = table[0:96]

    def start(f, r):
        lane = f * 40 + r + 6
        return jnp.broadcast_to(first[:, lane : lane + 1], (96, MEMBERS))

    def gains(r):
        ok = inside(lat, r)
        return jnp.where(ok, F32(GRAVITY), F32(0.0)), jnp.where(ok, F32(CORIOLIS), F32(0.0))

    for r in range(EXT):
        H[r, 8:104] = start(0, r) + FO[r, 8:104]
    for r in range(1, EXT - 1):
        g, c = gains(r)
        u, v = start(1, r), start(2, r)
        keep = 1.0 - FR[r, 8:104]
        U[r, 8:104] = keep * u - g * (H[r, 9:105] - H[r, 7:103]) + c * v
        V[r, 8:104] = keep * v - g * (H[r + 1, 8:104] - H[r - 1, 8:104]) - c * u

    def height_row(a, b, r):
        g, _ = gains(r)
        n = b - a
        east = U[r, pl.ds(a + 1, n)] - U[r, pl.ds(a - 1, n)]
        north = V[r + 1, pl.ds(a, n)] - V[r - 1, pl.ds(a, n)]
        H[r, pl.ds(a, n)] = H[r, pl.ds(a, n)] - g * (east + north) + FO[r, pl.ds(a, n)]

    def speed_row(a, b, r):
        g, c = gains(r)
        n = b - a
        u, v = U[r, pl.ds(a, n)], V[r, pl.ds(a, n)]
        keep = 1.0 - FR[r, pl.ds(a, n)]
        east = H[r, pl.ds(a + 1, n)] - H[r, pl.ds(a - 1, n)]
        north = H[r + 1, pl.ds(a, n)] - H[r - 1, pl.ds(a, n)]
        U[r, pl.ds(a, n)] = keep * u - g * east + c * v
        V[r, pl.ds(a, n)] = keep * v - g * north - c * u

    def sweep(row, reach, a, b):
        def body(i, carry):
            row(a, b, 10 - reach + 2 * i)
            row(a, b, 11 - reach + 2 * i)
            return carry

        lax.fori_loop(0, (ROWS + 2 * reach) // 2, body, 0)

    for step in range(1, STEPS):
        reach = 2 * (STEPS - 1 - step)
        a, b = (16, 96) if reach else (LEFT, RIGHT)
        sweep(height_row, reach, a, b)
        if reach:
            sweep(speed_row, reach - 1, a, b)


def gram(pos, H, weights, observed, keep, send):
    lines = ROWS * HALF
    h = H[10:18, LEFT:RIGHT].reshape(lines, MEMBERS)
    centre = jnp.mean(h, axis=1, keepdims=True)
    spread = h - centre
    weighted = spread * weights
    g = lax.dot_general(spread, weighted, (((0,), (0,)), ((), ())), precision=HIGHEST, preferred_element_type=F32)
    d = jnp.sum(weighted * (observed - centre), axis=0, keepdims=True)
    row, lane = iota((HALF, MEMBERS), 0), iota((HALF, MEMBERS), 1)
    top, bottom = g[:HALF], g[HALF:]
    packed = jnp.where(jnp.logical_and(lane < HALF, lane > row), pltpu.roll(bottom, HALF, 1), top)
    diagonal = jnp.sum(jnp.where(lane == row + HALF, bottom, 0.0), axis=0, keepdims=True)
    line = iota((8, MEMBERS), 0)
    rest = jnp.where(line == 0, d, jnp.where(line == 1, diagonal, 0.0))
    one = jnp.concatenate([packed[:32], rest], axis=0)
    two = jnp.concatenate([packed[32:], jnp.zeros((8, MEMBERS), F32)], axis=0)
    keep[...] = jnp.where(pos[1] == 0, one, two)
    send[...] = jnp.where(pos[1] == 0, two, one)


def first_run(pos, fr, fo, tiles, lz, rz, weights, observed, FR, FO, table, keep, send, H, U, V):
    del fr, fo
    at = 0
    for field, r, n in EDGE_ROWS:
        out = FO if field else FR
        if n:
            out[r, LEFT - n : LEFT] = lz[at : at + n]
            out[r, RIGHT : RIGHT + n] = rz[at : at + n]
        at += n
    table[...] = initial_table(pos, tiles, lz, rz)
    forward(pos[0], table[...], FR, FO, H, U, V)
    gram(pos, H, weights[0], observed[0], keep, send)


def inverse(x):
    n = PIVOTS
    panels = [x[k : k + n] for k in range(0, MEMBERS, n)]
    row, lane = iota((n, MEMBERS), 0), iota((n, MEMBERS), 1)
    lower, scaled = [], []

    def spread(panel, column):
        return jnp.broadcast_to(panel[:, column : column + 1], (n, MEMBERS))

    for k in range(len(panels)):
        first = k * n
        block = jnp.logical_and(lane >= first, lane < first + n)
        columns = [spread(panels[k], first + j) for j in range(n)]
        top = jnp.where(block, jnp.where(lane - first == row, 1.0, 0.0), panels[k])
        lower.append(jnp.where(lane < first + n, top, 0.0))
        for j in range(n):
            over = 1.0 / columns[j][j : j + 1]

            def eliminate(m, j=j, over=over):
                pivot = m[j : j + 1] * over
                return jnp.where(row == j, pivot, m - columns[j] * pivot)

            top = eliminate(top)
            columns[j + 1 :] = [eliminate(m) for m in columns[j + 1 :]]
        scaled.append(jnp.where(lane < first + n, top, 0.0))
        for i in range(k + 1, len(panels)):
            terms = [spread(panels[i], first + j) * top[j : j + 1] for j in range(n)]
            while len(terms) > 1:
                terms = [a + b for a, b in zip(terms[::2], terms[1::2])]
            panels[i] = jnp.where(block, 0.0, panels[i]) - terms[0]
    lower, scaled = jnp.concatenate(lower, axis=0), jnp.concatenate(scaled, axis=0)
    return lax.dot_general(lower, scaled, (((0,), (0,)), ((), ())), precision=HIGHEST, preferred_element_type=F32)


def weights_of(pos, mine, other):
    one = jnp.where(pos[1] == 0, mine, other)
    two = jnp.where(pos[1] == 0, other, mine)
    packed = jnp.concatenate([one[:32], two[:32]], axis=0)
    d, diagonal = one[32:33], one[33:34]
    turned = jnp.concatenate([packed, jnp.zeros((HALF, MEMBERS), F32)], axis=0).T
    row, lane = iota((HALF, MEMBERS), 0), iota((HALF, MEMBERS), 1)
    a = jnp.where(lane <= row, packed, turned[:HALF])
    c = pltpu.roll(jnp.where(lane > row, packed, turned[:HALF]), HALF, 1)
    c = jnp.where(lane == row + HALF, diagonal, c)
    top = jnp.where(lane < HALF, a, packed)
    bottom = jnp.where(lane < HALF, turned[HALF:], c)
    g = jnp.concatenate([top, bottom], axis=0)
    row, lane = iota((MEMBERS, MEMBERS), 0), iota((MEMBERS, MEMBERS), 1)
    x = g * (1.0 / MEMBERS) + jnp.where(row == lane, 1.0, 0.0)
    x = inverse(x)
    shift = jnp.sum(x * d, axis=1, keepdims=True) * (1.0 / MEMBERS)
    z = x + shift
    return z - jnp.mean(z, axis=0, keepdims=True) + 1.0 / MEMBERS


def second_run(pos, mine, other, fr, fo, table, weights, observed, k1, keep, send, FR, FO, H, U, V):
    k = weights_of(pos, mine[...], other[...])
    k1[...] = k
    for src, out in ((fr, FR), (fo, FO)):
        old = src[:, 8:104].reshape(EXT * 96, MEMBERS)
        new = jnp.dot(old, k, precision=HIGHEST, preferred_element_type=F32)
        out[:, 8:104] = new.reshape(EXT, 96, MEMBERS)
    forward(pos[0], table[...], FR, FO, H, U, V)
    gram(pos, H, weights[1], observed[1], keep, send)


def last_update(pos, mine, other, k1, own_p, other_p, out):
    k = jnp.dot(k1[...], weights_of(pos, mine[...], other[...]), precision=HIGHEST, preferred_element_type=F32)

    first = pos[1] == 0
    kt = k.T
    kt = jnp.where(first, kt[:HALF], kt[HALF:])
    for start in [f * HALF * ROWS + r for f in range(2) for r in range(ROWS)]:
        block = both_cores(first, own_p, other_p, start, ROWS)
        out[pl.ds(start, HALF, stride=ROWS), :] = jnp.dot(kt, block, precision=HIGHEST, preferred_element_type=F32)


def swap(value):
    return lax.ppermute(value, "ens", [(0, 1), (1, 0)])


def moved(value, axes, by):
    n = lax.axis_size(axes)
    return lax.ppermute(value, axes, [(i, (i + by) % n) for i in range(n)])


def copied_sum(*refs):
    *parts, out = refs
    terms = [ref[k] for ref in parts for k in range(ref.shape[0])]
    total = terms[0]
    for term in terms[1:]:
        total = total + term
    for k in range(out.shape[0]):
        out[k] = total


def summed(copies, *parts):
    return pl.pallas_call(
        copied_sum,
        out_shape=shape(copies, *parts[0].shape[1:]),
        in_specs=[VMEM] * len(parts),
        out_specs=VMEM,
        compiler_params=pltpu.CompilerParams(vmem_limit_bytes=4 * 1024 * 1024),
    )(*parts)


def reduced(keep, send):
    parts = keep[None], swap(send)[None]
    for axes in (LAT, "lon"):
        parts = [lax.all_to_all(summed(lax.axis_size(axes), *parts), axes, 0, 0, tiled=True)]
    value = summed(1, *parts)[0]
    return value, swap(value)


def call(kernel, out_shape, scalars, *args, scratch=(), aliases=None):
    return pl.pallas_call(
        kernel,
        out_shape=out_shape,
        in_specs=[SMEM] + [VMEM] * len(args),
        out_specs=jax.tree.map(lambda _: VMEM, out_shape),
        scratch_shapes=list(scratch),
        input_output_aliases=aliases or {},
        compiler_params=params(),
    )(scalars, *args)


def per_device(parameters, initial_height, initial_speed, obs_slots, obs_values, obs_precision):
    pos = jnp.stack([lax.axis_index(LAT), lax.axis_index("ens")]).astype(jnp.int32)
    own_p = parameters.reshape(2 * HALF * ROWS, COLS)
    slots, values, precision = (
        x[:, 0].transpose(0, 2, 1).reshape(16, 128) for x in (obs_slots, obs_values, obs_precision)
    )
    two_far = shape(3 * HALF + INIT, COLS)
    own, up2, dn2, obs = pl.pallas_call(
        collect,
        out_shape=[shape(OWN + INIT, COLS), two_far, two_far, shape(128, 128)],
        in_specs=[pl.BlockSpec(memory_space=pl.ANY)] * 5,
        out_specs=[VMEM] * 4,
        scratch_shapes=[pltpu.VMEM((16, COLS), F32)] * 2 + [pltpu.SemaphoreType.DMA((5,))],
    )(own_p, initial_height, initial_speed.reshape(16, COLS), values, precision)
    near = [moved(own, LAT, 1), moved(own, LAT, -1)]
    far = [moved(up2, LAT, 2), moved(dn2, LAT, -2)]
    own_other = swap(own)
    obs = lax.all_to_all(obs, LAT_LON, 0, 0, tiled=True)
    turned = call(turn_own, shape(OWN + INIT, MEMBERS), pos, own, own_other)
    *halo, obs, turned = lax.optimization_barrier((*near, *far, obs, turned))
    others = [swap(x) for x in halo]
    weights, observed = call(scatter_obs, [shape(2, 512, 128), shape(2, 512, 128)], pos, slots, obs)

    field = shape(EXT, WIDE, MEMBERS)
    half = shape(40, MEMBERS)
    square = shape(MEMBERS, MEMBERS)
    edge = shape(EDGE + 2 * ROWS, MEMBERS)
    ext_fr, ext_fo, tiles, right, left = call(
        turn_rows, [field, field, shape(5 * INIT, COLS), edge, edge], pos, turned, *halo, *others
    )
    lz, rz = moved(right, LON_ENS, 1), moved(left, LON_ENS, -1)
    state = [pltpu.VMEM((EXT, WIDE, MEMBERS), F32)]
    ext_fr, ext_fo, table, keep, send = call(
        first_run, [field, field, square, half, half],
        pos, ext_fr, ext_fo, tiles, lz, rz, weights, observed,
        scratch=state * 3, aliases={1: 0, 2: 1},
    )
    mine, other = reduced(keep, send)
    k1, keep, send = call(
        second_run, [square, half, half],
        pos, mine, other, ext_fr, ext_fo, table, weights, observed,
        scratch=state * 5,
    )
    mine, other = reduced(keep, send)
    out = call(last_update, shape(2 * HALF * ROWS, COLS), pos, mine, other, k1, own_p, own_other)
    return out.reshape(parameters.shape)


def solution(mesh):
    torus = Mesh(
        mesh.devices.reshape(4, 4, mesh.shape["lon"], mesh.shape["ens"]),
        ("lat_0", "lat_1", "lon", "ens"),
    )
    in_specs = (
        P(None, "ens", LAT, "lon"),
        P(LAT, "lon"),
        P(None, LAT, "lon"),
        P(None, LAT_LON, None, None),
        P(None, LAT_LON, None, None),
        P(None, LAT_LON, None, None),
    )
    out_specs = P(None, "ens", LAT, "lon")
    return jax.shard_map(
        per_device, mesh=torus, in_specs=in_specs, out_specs=out_specs, check_vma=False
    )
```

```python
import functools

import jax
import jax.numpy as jnp
from jax import lax
from jax.experimental import pallas as pl
from jax.experimental.pallas import tpu as pltpu
from jax.sharding import Mesh
from jax.sharding import PartitionSpec as P

STEPS = 6
LAT = ("lat_0", "lat_1")
LAT_LON = ("lat_0", "lat_1", "lon")
LON_ENS = ("lon", "ens")

DEPTH = 0.7
GRAVITY = 0.7
CORIOLIS = 0.1

MEMBERS = 128
HALF = 64
ROWS = 8
COLS = 128
EXT = 28
WIDE = 112
LEFT = 24
RIGHT = LEFT + HALF
INIT = 24
GLOBAL_ROWS = 128
OWN = 2 * ROWS * HALF
PIVOTS = 16

F32 = jnp.float32
HIGHEST = lax.Precision.HIGHEST
VMEM = pl.BlockSpec(memory_space=pltpu.VMEM)
SMEM = pl.BlockSpec(memory_space=pltpu.SMEM)


def params():
    return pltpu.CompilerParams(vmem_limit_bytes=24 * 1024 * 1024)


def shape(*dims):
    return jax.ShapeDtypeStruct(dims, F32)


def iota(dims, axis):
    return lax.broadcasted_iota(jnp.int32, dims, axis)


def collect(own_hbm, height_hbm, speed_hbm, values_hbm, precision_hbm,
            out, up2, dn2, obs, values, precision, sems):
    pairs = (
        (values_hbm, values), (precision_hbm, precision), (own_hbm, out.at[:OWN]),
        (height_hbm, out.at[OWN : OWN + ROWS]), (speed_hbm, out.at[OWN + ROWS :]),
    )
    copies = [pltpu.make_async_copy(src, dst, sems.at[k]) for k, (src, dst) in enumerate(pairs)]
    for copy in copies:
        copy.start()
    for copy in copies[:2]:
        copy.wait()
    lines = [values[...], precision[...], jnp.zeros((96, MEMBERS), F32)]
    obs[...] = jnp.concatenate(lines, axis=0).T[:, :32]
    for copy in copies[2:]:
        copy.wait()
    for k, (f, up_row, down_row) in enumerate(((1, 6, 0), (1, 7, 1), (0, 7, 0))):
        start = f * HALF * ROWS
        up2[k * HALF : (k + 1) * HALF] = out[pl.ds(start + up_row, HALF, stride=ROWS), :]
        dn2[k * HALF : (k + 1) * HALF] = out[pl.ds(start + down_row, HALF, stride=ROWS), :]
    up2[3 * HALF :] = out[OWN:]
    dn2[3 * HALF :] = out[OWN:]


def edge_rows():
    rows = []
    for field, first in ((1, 0), (0, 1)):
        for r in range(first, EXT - first):
            rows.append((field, r, 9 + field - max(10 - r, r - 17, 0)))
    return rows


EDGE_ROWS = edge_rows()
EDGE = (sum(n for _, _, n in EDGE_ROWS) + 7) // 8 * 8
NEAR = 16


def both_cores(first, mine, others, start, stride):
    lines = pl.ds(start, HALF, stride=stride)
    mine, others = mine[lines, :], others[lines, :]
    return jnp.concatenate([jnp.where(first, mine, others), jnp.where(first, others, mine)], axis=0)


def turn_own(pos, own, own_o, out):
    first = pos[1] == 0
    for k in range(2 * ROWS):
        turned = both_cores(first, own, own_o, k // ROWS * HALF * ROWS + k % ROWS, ROWS).T
        out[k * HALF : (k + 1) * HALF] = jnp.where(first, turned[:HALF], turned[HALF:])
    out[OWN:] = own[OWN:]


def turn_rows(pos, own, m1, p1, m2, p2, m1_o, p1_o, m2_o, p2_o, FR, FO, tiles, right, left):
    def row_source(field, r):
        if 2 <= r < 10:
            return m1, m1_o, field * HALF * ROWS + r - 2, ROWS
        if 18 <= r < 26:
            return p1, p1_o, field * HALF * ROWS + r - 18, ROWS
        k = 2 if field == 0 else (r if r < 2 else r - 26)
        refs = (m2, m2_o) if r < 2 else (p2, p2_o)
        return *refs, k * HALF, 1

    first = pos[1] == 0
    at = 0
    for field, r, n in EDGE_ROWS:
        if 10 <= r < 18:
            k = field * ROWS + r - 10
            turned = own[k * HALF : (k + 1) * HALF]
        else:
            turned = both_cores(first, *row_source(field, r)).T
            turned = jnp.where(first, turned[:HALF], turned[HALF:])
            if field == 1:
                turned = jnp.where(inside(pos[0], r), turned, 0.0)
        (FO if field else FR)[r, LEFT:RIGHT] = turned
        if n:
            right[at : at + n] = turned[HALF - n :]
            left[at : at + n] = turned[:n]
        at += n

    fields = ((m2, 3 * HALF), (m1, OWN), (own, OWN), (p1, OWN), (p2, 3 * HALF))
    slot = iota((ROWS, COLS), 1) // NEAR
    packed = [[jnp.zeros((ROWS, COLS), F32)] * 2, [jnp.zeros((ROWS, COLS), F32)] * 2]
    for k, (ref, start) in enumerate(fields):
        for f in range(3):
            j = 3 * k + f
            tile = ref[start + f * ROWS : start + (f + 1) * ROWS]
            tiles[j * ROWS : (j + 1) * ROWS] = tile
            for side, first_lane in ((0, COLS - NEAR), (1, 0)):
                there = pltpu.roll(tile, (NEAR * (j % 8) - first_lane) % COLS, 1)
                packed[side][j // 8] = jnp.where(slot == j % 8, there, packed[side][j // 8])
    for side, out in ((0, right), (1, left)):
        out[EDGE : EDGE + ROWS] = packed[side][0]
        out[EDGE + ROWS : EDGE + 2 * ROWS] = packed[side][1]


def scatter_obs(pos, slots, received, weights, observed):
    received = jnp.concatenate([received[...], jnp.zeros((MEMBERS, 96), F32)], axis=1).T
    values, precision = received[:16], received[16:32]
    lines = ROWS * HALF
    k = iota((lines, MEMBERS), 0)
    cell = (k // HALF) * COLS + pos[1] * HALF + k % HALF
    for t in range(2):
        found_w = jnp.zeros((lines, MEMBERS), F32)
        found_y = jnp.zeros((lines, MEMBERS), F32)
        for s in range(8):
            at = t * 8 + s
            hit = cell == slots[at : at + 1, :]
            found_w = found_w + jnp.where(hit, precision[at : at + 1, :], 0.0)
            found_y = found_y + jnp.where(hit, values[at : at + 1, :], 0.0)
        weights[t] = jnp.broadcast_to(jnp.sum(found_w, axis=1, keepdims=True), (lines, MEMBERS))
        observed[t] = jnp.broadcast_to(jnp.sum(found_y, axis=1, keepdims=True), (lines, MEMBERS))


def inside(lat, r):
    row = lat * ROWS + r - 10
    return jnp.logical_and(row >= 0, row < GLOBAL_ROWS)


def initial_table(pos, tiles, lz, rz):
    lane = iota((ROWS, COLS), 1)
    row = iota((ROWS, COLS), 0)
    e = pos[1]
    fields = [[], [], []]
    for k in range(5):
        for f in range(3):
            at = k * INIT + f * ROWS
            own = tiles[at : at + ROWS]
            j = 3 * k + f
            at = EDGE + j // 8 * ROWS
            before = pltpu.roll(lz[at : at + ROWS], (COLS - NEAR - NEAR * (j % 8)) % COLS, 1)
            after = pltpu.roll(rz[at : at + ROWS], -NEAR * (j % 8) % COLS, 1)
            low = pltpu.roll(jnp.where(lane >= 112, before, own), 16, 1)
            high = pltpu.roll(jnp.where(lane < 16, after, own), 80, 1)
            window = jnp.where(e == 0, low, high)
            place = pos[0] * ROWS + (k - 2) * ROWS + row
            ok = jnp.logical_and(place >= 0, place < GLOBAL_ROWS)
            fields[f].append(jnp.where(ok, window, 0.0))
    h, u, v = (jnp.concatenate(f, axis=0) for f in fields)
    east = pltpu.roll(u, COLS - 1, 1) - pltpu.roll(u, 1, 1)
    north = jnp.concatenate([v[1:], v[:1]], axis=0) - jnp.concatenate([v[-1:], v[:-1]], axis=0)
    place = pos[0] * ROWS - 16 + iota((40, COLS), 0)
    ok = jnp.logical_and(place >= 0, place < GLOBAL_ROWS)
    base = jnp.where(ok, h - DEPTH * (east + north), 0.0)
    return jnp.concatenate([base, u, v, jnp.zeros((8, COLS), F32)], axis=0).T


def forward(lat, table, FR, FO, H, U, V):
    first = table[0:96]

    def start(f, r):
        lane = f * 40 + r + 6
        return jnp.broadcast_to(first[:, lane : lane + 1], (96, MEMBERS))

    def gains(r):
        ok = inside(lat, r)
        return jnp.where(ok, F32(GRAVITY), F32(0.0)), jnp.where(ok, F32(CORIOLIS), F32(0.0))

    for r in range(EXT):
        H[r, 8:104] = start(0, r) + FO[r, 8:104]
    for r in range(1, EXT - 1):
        g, c = gains(r)
        u, v = start(1, r), start(2, r)
        keep = 1.0 - FR[r, 8:104]
        U[r, 8:104] = keep * u - g * (H[r, 9:105] - H[r, 7:103]) + c * v
        V[r, 8:104] = keep * v - g * (H[r + 1, 8:104] - H[r - 1, 8:104]) - c * u

    def height_row(a, b, r):
        g, _ = gains(r)
        n = b - a
        east = U[r, pl.ds(a + 1, n)] - U[r, pl.ds(a - 1, n)]
        north = V[r + 1, pl.ds(a, n)] - V[r - 1, pl.ds(a, n)]
        H[r, pl.ds(a, n)] = H[r, pl.ds(a, n)] - g * (east + north) + FO[r, pl.ds(a, n)]

    def speed_row(a, b, r):
        g, c = gains(r)
        n = b - a
        u, v = U[r, pl.ds(a, n)], V[r, pl.ds(a, n)]
        keep = 1.0 - FR[r, pl.ds(a, n)]
        east = H[r, pl.ds(a + 1, n)] - H[r, pl.ds(a - 1, n)]
        north = H[r + 1, pl.ds(a, n)] - H[r - 1, pl.ds(a, n)]
        U[r, pl.ds(a, n)] = keep * u - g * east + c * v
        V[r, pl.ds(a, n)] = keep * v - g * north - c * u

    def sweep(row, reach, a, b):
        def body(i, carry):
            row(a, b, 10 - reach + 2 * i)
            row(a, b, 11 - reach + 2 * i)
            return carry

        lax.fori_loop(0, (ROWS + 2 * reach) // 2, body, 0)

    for step in range(1, STEPS):
        reach = 2 * (STEPS - 1 - step)
        a, b = (16, 96) if reach else (LEFT, RIGHT)
        sweep(height_row, reach, a, b)
        if reach:
            sweep(speed_row, reach - 1, a, b)


def gram(pos, H, weights, observed, keep, send):
    lines = ROWS * HALF
    h = H[10:18, LEFT:RIGHT].reshape(lines, MEMBERS)
    centre = jnp.mean(h, axis=1, keepdims=True)
    spread = h - centre
    weighted = spread * weights
    g = lax.dot_general(spread, weighted, (((0,), (0,)), ((), ())), precision=HIGHEST, preferred_element_type=F32)
    d = jnp.sum(weighted * (observed - centre), axis=0, keepdims=True)
    row, lane = iota((HALF, MEMBERS), 0), iota((HALF, MEMBERS), 1)
    top, bottom = g[:HALF], g[HALF:]
    packed = jnp.where(jnp.logical_and(lane < HALF, lane > row), pltpu.roll(bottom, HALF, 1), top)
    diagonal = jnp.sum(jnp.where(lane == row + HALF, bottom, 0.0), axis=0, keepdims=True)
    line = iota((8, MEMBERS), 0)
    rest = jnp.where(line == 0, d, jnp.where(line == 1, diagonal, 0.0))
    one = jnp.concatenate([packed[:32], rest], axis=0)
    two = jnp.concatenate([packed[32:], jnp.zeros((8, MEMBERS), F32)], axis=0)
    keep[...] = jnp.where(pos[1] == 0, one, two)
    send[...] = jnp.where(pos[1] == 0, two, one)


def first_run(pos, fr, fo, tiles, lz, rz, weights, observed, FR, FO, table, keep, send, H, U, V):
    del fr, fo
    at = 0
    for field, r, n in EDGE_ROWS:
        out = FO if field else FR
        if n:
            out[r, LEFT - n : LEFT] = lz[at : at + n]
            out[r, RIGHT : RIGHT + n] = rz[at : at + n]
        at += n
    table[...] = initial_table(pos, tiles, lz, rz)
    forward(pos[0], table[...], FR, FO, H, U, V)
    gram(pos, H, weights[0], observed[0], keep, send)


def inverse(x):
    n = PIVOTS
    panels = [x[k : k + n] for k in range(0, MEMBERS, n)]
    row, lane = iota((n, MEMBERS), 0), iota((n, MEMBERS), 1)
    lower, scaled = [], []

    def spread(panel, column):
        return jnp.broadcast_to(panel[:, column : column + 1], (n, MEMBERS))

    for k in range(len(panels)):
        first = k * n
        block = jnp.logical_and(lane >= first, lane < first + n)
        columns = [spread(panels[k], first + j) for j in range(n)]
        top = jnp.where(block, jnp.where(lane - first == row, 1.0, 0.0), panels[k])
        lower.append(jnp.where(lane < first + n, top, 0.0))
        for j in range(n):
            over = 1.0 / columns[j][j : j + 1]

            def eliminate(m, j=j, over=over):
                pivot = m[j : j + 1] * over
                return jnp.where(row == j, pivot, m - columns[j] * pivot)

            top = eliminate(top)
            columns[j + 1 :] = [eliminate(m) for m in columns[j + 1 :]]
        scaled.append(jnp.where(lane < first + n, top, 0.0))
        for i in range(k + 1, len(panels)):
            terms = [spread(panels[i], first + j) * top[j : j + 1] for j in range(n)]
            while len(terms) > 1:
                terms = [a + b for a, b in zip(terms[::2], terms[1::2])]
            panels[i] = jnp.where(block, 0.0, panels[i]) - terms[0]
    lower, scaled = jnp.concatenate(lower, axis=0), jnp.concatenate(scaled, axis=0)
    return lax.dot_general(lower, scaled, (((0,), (0,)), ((), ())), precision=HIGHEST, preferred_element_type=F32)


def weights_of(pos, mine, other):
    one = jnp.where(pos[1] == 0, mine, other)
    two = jnp.where(pos[1] == 0, other, mine)
    packed = jnp.concatenate([one[:32], two[:32]], axis=0)
    d, diagonal = one[32:33], one[33:34]
    turned = jnp.concatenate([packed, jnp.zeros((HALF, MEMBERS), F32)], axis=0).T
    row, lane = iota((HALF, MEMBERS), 0), iota((HALF, MEMBERS), 1)
    a = jnp.where(lane <= row, packed, turned[:HALF])
    c = pltpu.roll(jnp.where(lane > row, packed, turned[:HALF]), HALF, 1)
    c = jnp.where(lane == row + HALF, diagonal, c)
    top = jnp.where(lane < HALF, a, packed)
    bottom = jnp.where(lane < HALF, turned[HALF:], c)
    g = jnp.concatenate([top, bottom], axis=0)
    row, lane = iota((MEMBERS, MEMBERS), 0), iota((MEMBERS, MEMBERS), 1)
    x = g * (1.0 / MEMBERS) + jnp.where(row == lane, 1.0, 0.0)
    x = inverse(x)
    shift = jnp.sum(x * d, axis=1, keepdims=True) * (1.0 / MEMBERS)
    z = x + shift
    return z - jnp.mean(z, axis=0, keepdims=True) + 1.0 / MEMBERS


def second_run(pos, mine, other, fr, fo, table, weights, observed, k1, keep, send, FR, FO, H, U, V):
    k = weights_of(pos, mine[...], other[...])
    k1[...] = k
    for src, out in ((fr, FR), (fo, FO)):
        old = src[:, 8:104].reshape(EXT * 96, MEMBERS)
        new = jnp.dot(old, k, precision=HIGHEST, preferred_element_type=F32)
        out[:, 8:104] = new.reshape(EXT, 96, MEMBERS)
    forward(pos[0], table[...], FR, FO, H, U, V)
    gram(pos, H, weights[1], observed[1], keep, send)


def last_update(pos, mine, other, k1, own_p, other_p, out):
    k = jnp.dot(k1[...], weights_of(pos, mine[...], other[...]), precision=HIGHEST, preferred_element_type=F32)

    first = pos[1] == 0
    kt = k.T
    kt = jnp.where(first, kt[:HALF], kt[HALF:])
    for start in [f * HALF * ROWS + r for f in range(2) for r in range(ROWS)]:
        block = both_cores(first, own_p, other_p, start, ROWS)
        out[pl.ds(start, HALF, stride=ROWS), :] = jnp.dot(kt, block, precision=HIGHEST, preferred_element_type=F32)


def swap(value):
    return lax.ppermute(value, "ens", [(0, 1), (1, 0)])


def moved(value, axes, by):
    n = lax.axis_size(axes)
    return lax.ppermute(value, axes, [(i, (i + by) % n) for i in range(n)])


def copied_sum(*refs):
    *parts, out = refs
    terms = [ref[k] for ref in parts for k in range(ref.shape[0])]
    total = terms[0]
    for term in terms[1:]:
        total = total + term
    for k in range(out.shape[0]):
        out[k] = total


def summed(copies, *parts):
    return pl.pallas_call(
        copied_sum,
        out_shape=shape(copies, *parts[0].shape[1:]),
        in_specs=[VMEM] * len(parts),
        out_specs=VMEM,
        compiler_params=pltpu.CompilerParams(vmem_limit_bytes=4 * 1024 * 1024),
    )(*parts)


def reduced(keep, send):
    parts = keep[None], swap(send)[None]
    for axes in (LAT, "lon"):
        parts = [lax.all_to_all(summed(lax.axis_size(axes), *parts), axes, 0, 0, tiled=True)]
    value = summed(1, *parts)[0]
    return value, swap(value)


def call(kernel, out_shape, scalars, *args, scratch=(), aliases=None):
    return pl.pallas_call(
        kernel,
        out_shape=out_shape,
        in_specs=[SMEM] + [VMEM] * len(args),
        out_specs=jax.tree.map(lambda _: VMEM, out_shape),
        scratch_shapes=list(scratch),
        input_output_aliases=aliases or {},
        compiler_params=params(),
    )(scalars, *args)


def per_device(parameters, initial_height, initial_speed, obs_slots, obs_values, obs_precision):
    pos = jnp.stack([lax.axis_index(LAT), lax.axis_index("ens")]).astype(jnp.int32)
    own_p = parameters.reshape(2 * HALF * ROWS, COLS)
    slots, values, precision = (
        x[:, 0].transpose(0, 2, 1).reshape(16, 128) for x in (obs_slots, obs_values, obs_precision)
    )
    two_far = shape(3 * HALF + INIT, COLS)
    own, up2, dn2, obs = pl.pallas_call(
        collect,
        out_shape=[shape(OWN + INIT, COLS), two_far, two_far, shape(128, 32)],
        in_specs=[pl.BlockSpec(memory_space=pl.ANY)] * 5,
        out_specs=[VMEM] * 4,
        scratch_shapes=[pltpu.VMEM((16, COLS), F32)] * 2 + [pltpu.SemaphoreType.DMA((5,))],
    )(own_p, initial_height, initial_speed.reshape(16, COLS), values, precision)
    near = [moved(own, LAT, 1), moved(own, LAT, -1)]
    far = [moved(up2, LAT, 2), moved(dn2, LAT, -2)]
    own_other = swap(own)
    obs = lax.all_to_all(obs, LAT_LON, 0, 0, tiled=True)
    turned = call(turn_own, shape(OWN + INIT, MEMBERS), pos, own, own_other)
    *halo, obs, turned = lax.optimization_barrier((*near, *far, obs, turned))
    others = [swap(x) for x in halo]
    weights, observed = call(scatter_obs, [shape(2, 512, 128), shape(2, 512, 128)], pos, slots, obs)

    field = shape(EXT, WIDE, MEMBERS)
    half = shape(40, MEMBERS)
    square = shape(MEMBERS, MEMBERS)
    edge = shape(EDGE + 2 * ROWS, MEMBERS)
    ext_fr, ext_fo, tiles, right, left = call(
        turn_rows, [field, field, shape(5 * INIT, COLS), edge, edge], pos, turned, *halo, *others
    )
    lz, rz = moved(right, LON_ENS, 1), moved(left, LON_ENS, -1)
    state = [pltpu.VMEM((EXT, WIDE, MEMBERS), F32)]
    ext_fr, ext_fo, table, keep, send = call(
        first_run, [field, field, square, half, half],
        pos, ext_fr, ext_fo, tiles, lz, rz, weights, observed,
        scratch=state * 3, aliases={1: 0, 2: 1},
    )
    mine, other = reduced(keep, send)
    k1, keep, send = call(
        second_run, [square, half, half],
        pos, mine, other, ext_fr, ext_fo, table, weights, observed,
        scratch=state * 5,
    )
    mine, other = reduced(keep, send)
    out = call(last_update, shape(2 * HALF * ROWS, COLS), pos, mine, other, k1, own_p, own_other)
    return out.reshape(parameters.shape)


def solution(mesh):
    torus = Mesh(
        mesh.devices.reshape(4, 4, mesh.shape["lon"], mesh.shape["ens"]),
        ("lat_0", "lat_1", "lon", "ens"),
    )
    in_specs = (
        P(None, "ens", LAT, "lon"),
        P(LAT, "lon"),
        P(None, LAT, "lon"),
        P(None, LAT_LON, None, None),
        P(None, LAT_LON, None, None),
        P(None, LAT_LON, None, None),
    )
    out_specs = P(None, "ens", LAT, "lon")
    return jax.shard_map(
        per_device, mesh=torus, in_specs=in_specs, out_specs=out_specs, check_vma=False
    )
```

```python
import functools

import jax
import jax.numpy as jnp
from jax import lax
from jax.experimental import pallas as pl
from jax.experimental.pallas import tpu as pltpu
from jax.sharding import Mesh
from jax.sharding import PartitionSpec as P

STEPS = 6
LAT = ("lat_0", "lat_1")
LAT_LON = ("lat_0", "lat_1", "lon")
LON_ENS = ("lon", "ens")

DEPTH = 0.7
GRAVITY = 0.7
CORIOLIS = 0.1

MEMBERS = 128
HALF = 64
ROWS = 8
COLS = 128
EXT = 28
WIDE = 112
LEFT = 24
RIGHT = LEFT + HALF
INIT = 24
GLOBAL_ROWS = 128
OWN = 2 * ROWS * HALF
PIVOTS = 16

F32 = jnp.float32
HIGHEST = lax.Precision.HIGHEST
VMEM = pl.BlockSpec(memory_space=pltpu.VMEM)
SMEM = pl.BlockSpec(memory_space=pltpu.SMEM)


def params():
    return pltpu.CompilerParams(vmem_limit_bytes=24 * 1024 * 1024)


def shape(*dims):
    return jax.ShapeDtypeStruct(dims, F32)


def iota(dims, axis):
    return lax.broadcasted_iota(jnp.int32, dims, axis)


def collect(own_hbm, height_hbm, speed_hbm, values_hbm, precision_hbm,
            out, up2, dn2, obs, values, precision, sems):
    pairs = (
        (values_hbm, values), (precision_hbm, precision), (own_hbm, out.at[:OWN]),
        (height_hbm, out.at[OWN : OWN + ROWS]), (speed_hbm, out.at[OWN + ROWS :]),
    )
    copies = [pltpu.make_async_copy(src, dst, sems.at[k]) for k, (src, dst) in enumerate(pairs)]
    for copy in copies:
        copy.start()
    for copy in copies[:2]:
        copy.wait()
    lines = [values[...], precision[...], jnp.zeros((96, MEMBERS), F32)]
    obs[...] = jnp.concatenate(lines, axis=0).T
    for copy in copies[2:]:
        copy.wait()
    for k, (f, up_row, down_row) in enumerate(((1, 6, 0), (1, 7, 1), (0, 7, 0))):
        start = f * HALF * ROWS
        up2[k * HALF : (k + 1) * HALF] = out[pl.ds(start + up_row, HALF, stride=ROWS), :]
        dn2[k * HALF : (k + 1) * HALF] = out[pl.ds(start + down_row, HALF, stride=ROWS), :]
    up2[3 * HALF :] = out[OWN:]
    dn2[3 * HALF :] = out[OWN:]


def edge_rows():
    rows = []
    for field, first in ((1, 0), (0, 1)):
        for r in range(first, EXT - first):
            rows.append((field, r, 9 + field - max(10 - r, r - 17, 0)))
    return rows


EDGE_ROWS = edge_rows()
EDGE = (sum(n for _, _, n in EDGE_ROWS) + 7) // 8 * 8
NEAR = 16


def both_cores(first, mine, others, start, stride):
    lines = pl.ds(start, HALF, stride=stride)
    mine, others = mine[lines, :], others[lines, :]
    return jnp.concatenate([jnp.where(first, mine, others), jnp.where(first, others, mine)], axis=0)


def turn_own(pos, own, own_o, out):
    first = pos[1] == 0
    for k in range(2 * ROWS):
        turned = both_cores(first, own, own_o, k // ROWS * HALF * ROWS + k % ROWS, ROWS).T
        out[k * HALF : (k + 1) * HALF] = jnp.where(first, turned[:HALF], turned[HALF:])
    out[OWN:] = own[OWN:]


def turn_rows(pos, own, m1, p1, m2, p2, m1_o, p1_o, m2_o, p2_o, FR, FO, tiles, right, left):
    def row_source(field, r):
        if 2 <= r < 10:
            return m1, m1_o, field * HALF * ROWS + r - 2, ROWS
        if 18 <= r < 26:
            return p1, p1_o, field * HALF * ROWS + r - 18, ROWS
        k = 2 if field == 0 else (r if r < 2 else r - 26)
        refs = (m2, m2_o) if r < 2 else (p2, p2_o)
        return *refs, k * HALF, 1

    first = pos[1] == 0
    at = 0
    for field, r, n in EDGE_ROWS:
        if 10 <= r < 18:
            k = field * ROWS + r - 10
            turned = own[k * HALF : (k + 1) * HALF]
        else:
            turned = both_cores(first, *row_source(field, r)).T
            turned = jnp.where(first, turned[:HALF], turned[HALF:])
            if field == 1:
                turned = jnp.where(inside(pos[0], r), turned, 0.0)
        (FO if field else FR)[r, LEFT:RIGHT] = turned
        if n:
            right[at : at + n] = turned[HALF - n :]
            left[at : at + n] = turned[:n]
        at += n

    fields = ((m2, 3 * HALF), (m1, OWN), (own, OWN), (p1, OWN), (p2, 3 * HALF))
    slot = iota((ROWS, COLS), 1) // NEAR
    packed = [[jnp.zeros((ROWS, COLS), F32)] * 2, [jnp.zeros((ROWS, COLS), F32)] * 2]
    for k, (ref, start) in enumerate(fields):
        for f in range(3):
            j = 3 * k + f
            tile = ref[start + f * ROWS : start + (f + 1) * ROWS]
            tiles[j * ROWS : (j + 1) * ROWS] = tile
            for side, first_lane in ((0, COLS - NEAR), (1, 0)):
                there = pltpu.roll(tile, (NEAR * (j % 8) - first_lane) % COLS, 1)
                packed[side][j // 8] = jnp.where(slot == j % 8, there, packed[side][j // 8])
    for side, out in ((0, right), (1, left)):
        out[EDGE : EDGE + ROWS] = packed[side][0]
        out[EDGE + ROWS : EDGE + 2 * ROWS] = packed[side][1]


def scatter_obs(pos, slots, received, weights, observed):
    received = received[...].T
    values, precision = received[:16], received[16:32]
    lines = ROWS * HALF
    k = iota((lines, MEMBERS), 0)
    cell = (k // HALF) * COLS + pos[1] * HALF + k % HALF
    for t in range(2):
        found_w = jnp.zeros((lines, MEMBERS), F32)
        found_y = jnp.zeros((lines, MEMBERS), F32)
        for s in range(8):
            at = t * 8 + s
            hit = cell == slots[at : at + 1, :]
            found_w = found_w + jnp.where(hit, precision[at : at + 1, :], 0.0)
            found_y = found_y + jnp.where(hit, values[at : at + 1, :], 0.0)
        weights[t] = jnp.broadcast_to(jnp.sum(found_w, axis=1, keepdims=True), (lines, MEMBERS))
        observed[t] = jnp.broadcast_to(jnp.sum(found_y, axis=1, keepdims=True), (lines, MEMBERS))


def inside(lat, r):
    row = lat * ROWS + r - 10
    return jnp.logical_and(row >= 0, row < GLOBAL_ROWS)


def initial_table(pos, tiles, lz, rz):
    lane = iota((ROWS, COLS), 1)
    row = iota((ROWS, COLS), 0)
    e = pos[1]
    fields = [[], [], []]
    for k in range(5):
        for f in range(3):
            at = k * INIT + f * ROWS
            own = tiles[at : at + ROWS]
            j = 3 * k + f
            at = EDGE + j // 8 * ROWS
            before = pltpu.roll(lz[at : at + ROWS], (COLS - NEAR - NEAR * (j % 8)) % COLS, 1)
            after = pltpu.roll(rz[at : at + ROWS], -NEAR * (j % 8) % COLS, 1)
            low = pltpu.roll(jnp.where(lane >= 112, before, own), 16, 1)
            high = pltpu.roll(jnp.where(lane < 16, after, own), 80, 1)
            window = jnp.where(e == 0, low, high)
            place = pos[0] * ROWS + (k - 2) * ROWS + row
            ok = jnp.logical_and(place >= 0, place < GLOBAL_ROWS)
            fields[f].append(jnp.where(ok, window, 0.0))
    h, u, v = (jnp.concatenate(f, axis=0) for f in fields)
    east = pltpu.roll(u, COLS - 1, 1) - pltpu.roll(u, 1, 1)
    north = jnp.concatenate([v[1:], v[:1]], axis=0) - jnp.concatenate([v[-1:], v[:-1]], axis=0)
    place = pos[0] * ROWS - 16 + iota((40, COLS), 0)
    ok = jnp.logical_and(place >= 0, place < GLOBAL_ROWS)
    base = jnp.where(ok, h - DEPTH * (east + north), 0.0)
    return jnp.concatenate([base, u, v, jnp.zeros((8, COLS), F32)], axis=0).T


def forward(lat, table, FR, FO, H, U, V):
    first = table[0:96]

    def start(f, r):
        lane = f * 40 + r + 6
        return jnp.broadcast_to(first[:, lane : lane + 1], (96, MEMBERS))

    def gains(r):
        ok = inside(lat, r)
        return jnp.where(ok, F32(GRAVITY), F32(0.0)), jnp.where(ok, F32(CORIOLIS), F32(0.0))

    for r in range(EXT):
        H[r, 8:104] = start(0, r) + FO[r, 8:104]
    for r in range(1, EXT - 1):
        g, c = gains(r)
        u, v = start(1, r), start(2, r)
        keep = 1.0 - FR[r, 8:104]
        U[r, 8:104] = keep * u - g * (H[r, 9:105] - H[r, 7:103]) + c * v
        V[r, 8:104] = keep * v - g * (H[r + 1, 8:104] - H[r - 1, 8:104]) - c * u

    def height_row(a, b, r):
        g, _ = gains(r)
        n = b - a
        east = U[r, pl.ds(a + 1, n)] - U[r, pl.ds(a - 1, n)]
        north = V[r + 1, pl.ds(a, n)] - V[r - 1, pl.ds(a, n)]
        H[r, pl.ds(a, n)] = H[r, pl.ds(a, n)] - g * (east + north) + FO[r, pl.ds(a, n)]

    def speed_row(a, b, r):
        g, c = gains(r)
        n = b - a
        u, v = U[r, pl.ds(a, n)], V[r, pl.ds(a, n)]
        keep = 1.0 - FR[r, pl.ds(a, n)]
        east = H[r, pl.ds(a + 1, n)] - H[r, pl.ds(a - 1, n)]
        north = H[r + 1, pl.ds(a, n)] - H[r - 1, pl.ds(a, n)]
        U[r, pl.ds(a, n)] = keep * u - g * east + c * v
        V[r, pl.ds(a, n)] = keep * v - g * north - c * u

    def sweep(row, reach, a, b):
        def body(i, carry):
            row(a, b, 10 - reach + 2 * i)
            row(a, b, 11 - reach + 2 * i)
            return carry

        lax.fori_loop(0, (ROWS + 2 * reach) // 2, body, 0, unroll=True)

    for step in range(1, STEPS):
        reach = 2 * (STEPS - 1 - step)
        a, b = (16, 96) if reach else (LEFT, RIGHT)
        sweep(height_row, reach, a, b)
        if reach:
            sweep(speed_row, reach - 1, a, b)


def gram(pos, H, weights, observed, keep, send):
    lines = ROWS * HALF
    h = H[10:18, LEFT:RIGHT].reshape(lines, MEMBERS)
    centre = jnp.mean(h, axis=1, keepdims=True)
    spread = h - centre
    weighted = spread * weights
    g = lax.dot_general(spread, weighted, (((0,), (0,)), ((), ())), precision=HIGHEST, preferred_element_type=F32)
    d = jnp.sum(weighted * (observed - centre), axis=0, keepdims=True)
    row, lane = iota((HALF, MEMBERS), 0), iota((HALF, MEMBERS), 1)
    top, bottom = g[:HALF], g[HALF:]
    packed = jnp.where(jnp.logical_and(lane < HALF, lane > row), pltpu.roll(bottom, HALF, 1), top)
    diagonal = jnp.sum(jnp.where(lane == row + HALF, bottom, 0.0), axis=0, keepdims=True)
    line = iota((8, MEMBERS), 0)
    rest = jnp.where(line == 0, d, jnp.where(line == 1, diagonal, 0.0))
    one = jnp.concatenate([packed[:32], rest], axis=0)
    two = jnp.concatenate([packed[32:], jnp.zeros((8, MEMBERS), F32)], axis=0)
    keep[...] = jnp.where(pos[1] == 0, one, two)
    send[...] = jnp.where(pos[1] == 0, two, one)


def first_run(pos, fr, fo, tiles, lz, rz, weights, observed, FR, FO, table, keep, send, H, U, V):
    del fr, fo
    at = 0
    for field, r, n in EDGE_ROWS:
        out = FO if field else FR
        if n:
            out[r, LEFT - n : LEFT] = lz[at : at + n]
            out[r, RIGHT : RIGHT + n] = rz[at : at + n]
        at += n
    table[...] = initial_table(pos, tiles, lz, rz)
    forward(pos[0], table[...], FR, FO, H, U, V)
    gram(pos, H, weights[0], observed[0], keep, send)


def inverse(x):
    n = PIVOTS
    panels = [x[k : k + n] for k in range(0, MEMBERS, n)]
    row, lane = iota((n, MEMBERS), 0), iota((n, MEMBERS), 1)
    lower, scaled = [], []

    def spread(panel, column):
        return jnp.broadcast_to(panel[:, column : column + 1], (n, MEMBERS))

    for k in range(len(panels)):
        first = k * n
        block = jnp.logical_and(lane >= first, lane < first + n)
        columns = [spread(panels[k], first + j) for j in range(n)]
        top = jnp.where(block, jnp.where(lane - first == row, 1.0, 0.0), panels[k])
        lower.append(jnp.where(lane < first + n, top, 0.0))
        for j in range(n):
            over = 1.0 / columns[j][j : j + 1]

            def eliminate(m, j=j, over=over):
                pivot = m[j : j + 1] * over
                return jnp.where(row == j, pivot, m - columns[j] * pivot)

            top = eliminate(top)
            columns[j + 1 :] = [eliminate(m) for m in columns[j + 1 :]]
        scaled.append(jnp.where(lane < first + n, top, 0.0))
        for i in range(k + 1, len(panels)):
            terms = [spread(panels[i], first + j) * top[j : j + 1] for j in range(n)]
            while len(terms) > 1:
                terms = [a + b for a, b in zip(terms[::2], terms[1::2])]
            panels[i] = jnp.where(block, 0.0, panels[i]) - terms[0]
    lower, scaled = jnp.concatenate(lower, axis=0), jnp.concatenate(scaled, axis=0)
    return lax.dot_general(lower, scaled, (((0,), (0,)), ((), ())), precision=HIGHEST, preferred_element_type=F32)


def weights_of(pos, mine, other):
    one = jnp.where(pos[1] == 0, mine, other)
    two = jnp.where(pos[1] == 0, other, mine)
    packed = jnp.concatenate([one[:32], two[:32]], axis=0)
    d, diagonal = one[32:33], one[33:34]
    turned = jnp.concatenate([packed, jnp.zeros((HALF, MEMBERS), F32)], axis=0).T
    row, lane = iota((HALF, MEMBERS), 0), iota((HALF, MEMBERS), 1)
    a = jnp.where(lane <= row, packed, turned[:HALF])
    c = pltpu.roll(jnp.where(lane > row, packed, turned[:HALF]), HALF, 1)
    c = jnp.where(lane == row + HALF, diagonal, c)
    top = jnp.where(lane < HALF, a, packed)
    bottom = jnp.where(lane < HALF, turned[HALF:], c)
    g = jnp.concatenate([top, bottom], axis=0)
    row, lane = iota((MEMBERS, MEMBERS), 0), iota((MEMBERS, MEMBERS), 1)
    x = g * (1.0 / MEMBERS) + jnp.where(row == lane, 1.0, 0.0)
    x = inverse(x)
    shift = jnp.sum(x * d, axis=1, keepdims=True) * (1.0 / MEMBERS)
    z = x + shift
    return z - jnp.mean(z, axis=0, keepdims=True) + 1.0 / MEMBERS


def second_run(pos, mine, other, fr, fo, table, weights, observed, k1, keep, send, FR, FO, H, U, V):
    k = weights_of(pos, mine[...], other[...])
    k1[...] = k
    for src, out in ((fr, FR), (fo, FO)):
        old = src[:, 8:104].reshape(EXT * 96, MEMBERS)
        new = jnp.dot(old, k, precision=HIGHEST, preferred_element_type=F32)
        out[:, 8:104] = new.reshape(EXT, 96, MEMBERS)
    forward(pos[0], table[...], FR, FO, H, U, V)
    gram(pos, H, weights[1], observed[1], keep, send)


def last_update(pos, mine, other, k1, own_p, other_p, out):
    k = jnp.dot(k1[...], weights_of(pos, mine[...], other[...]), precision=HIGHEST, preferred_element_type=F32)

    first = pos[1] == 0
    kt = k.T
    kt = jnp.where(first, kt[:HALF], kt[HALF:])
    for start in [f * HALF * ROWS + r for f in range(2) for r in range(ROWS)]:
        block = both_cores(first, own_p, other_p, start, ROWS)
        out[pl.ds(start, HALF, stride=ROWS), :] = jnp.dot(kt, block, precision=HIGHEST, preferred_element_type=F32)


def swap(value):
    return lax.ppermute(value, "ens", [(0, 1), (1, 0)])


def moved(value, axes, by):
    n = lax.axis_size(axes)
    return lax.ppermute(value, axes, [(i, (i + by) % n) for i in range(n)])


def copied_sum(*refs):
    *parts, out = refs
    terms = [ref[k] for ref in parts for k in range(ref.shape[0])]
    total = terms[0]
    for term in terms[1:]:
        total = total + term
    for k in range(out.shape[0]):
        out[k] = total


def summed(copies, *parts):
    return pl.pallas_call(
        copied_sum,
        out_shape=shape(copies, *parts[0].shape[1:]),
        in_specs=[VMEM] * len(parts),
        out_specs=VMEM,
        compiler_params=pltpu.CompilerParams(vmem_limit_bytes=4 * 1024 * 1024),
    )(*parts)


def reduced(keep, send):
    parts = keep[None], swap(send)[None]
    for axes in (LAT, "lon"):
        parts = [lax.all_to_all(summed(lax.axis_size(axes), *parts), axes, 0, 0, tiled=True)]
    value = summed(1, *parts)[0]
    return value, swap(value)


def call(kernel, out_shape, scalars, *args, scratch=(), aliases=None):
    return pl.pallas_call(
        kernel,
        out_shape=out_shape,
        in_specs=[SMEM] + [VMEM] * len(args),
        out_specs=jax.tree.map(lambda _: VMEM, out_shape),
        scratch_shapes=list(scratch),
        input_output_aliases=aliases or {},
        compiler_params=params(),
    )(scalars, *args)


def per_device(parameters, initial_height, initial_speed, obs_slots, obs_values, obs_precision):
    pos = jnp.stack([lax.axis_index(LAT), lax.axis_index("ens")]).astype(jnp.int32)
    own_p = parameters.reshape(2 * HALF * ROWS, COLS)
    slots, values, precision = (
        x[:, 0].transpose(0, 2, 1).reshape(16, 128) for x in (obs_slots, obs_values, obs_precision)
    )
    two_far = shape(3 * HALF + INIT, COLS)
    own, up2, dn2, obs = pl.pallas_call(
        collect,
        out_shape=[shape(OWN + INIT, COLS), two_far, two_far, shape(128, 128)],
        in_specs=[pl.BlockSpec(memory_space=pl.ANY)] * 5,
        out_specs=[VMEM] * 4,
        scratch_shapes=[pltpu.VMEM((16, COLS), F32)] * 2 + [pltpu.SemaphoreType.DMA((5,))],
    )(own_p, initial_height, initial_speed.reshape(16, COLS), values, precision)
    near = [moved(own, LAT, 1), moved(own, LAT, -1)]
    far = [moved(up2, LAT, 2), moved(dn2, LAT, -2)]
    own_other = swap(own)
    obs = lax.all_to_all(obs, LAT_LON, 0, 0, tiled=True)
    turned = call(turn_own, shape(OWN + INIT, MEMBERS), pos, own, own_other)
    *halo, obs, turned = lax.optimization_barrier((*near, *far, obs, turned))
    others = [swap(x) for x in halo]
    weights, observed = call(scatter_obs, [shape(2, 512, 128), shape(2, 512, 128)], pos, slots, obs)

    field = shape(EXT, WIDE, MEMBERS)
    half = shape(40, MEMBERS)
    square = shape(MEMBERS, MEMBERS)
    edge = shape(EDGE + 2 * ROWS, MEMBERS)
    ext_fr, ext_fo, tiles, right, left = call(
        turn_rows, [field, field, shape(5 * INIT, COLS), edge, edge], pos, turned, *halo, *others
    )
    lz, rz = moved(right, LON_ENS, 1), moved(left, LON_ENS, -1)
    state = [pltpu.VMEM((EXT, WIDE, MEMBERS), F32)]
    ext_fr, ext_fo, table, keep, send = call(
        first_run, [field, field, square, half, half],
        pos, ext_fr, ext_fo, tiles, lz, rz, weights, observed,
        scratch=state * 3, aliases={1: 0, 2: 1},
    )
    mine, other = reduced(keep, send)
    k1, keep, send = call(
        second_run, [square, half, half],
        pos, mine, other, ext_fr, ext_fo, table, weights, observed,
        scratch=state * 5,
    )
    mine, other = reduced(keep, send)
    out = call(last_update, shape(2 * HALF * ROWS, COLS), pos, mine, other, k1, own_p, own_other)
    return out.reshape(parameters.shape)


def solution(mesh):
    torus = Mesh(
        mesh.devices.reshape(4, 4, mesh.shape["lon"], mesh.shape["ens"]),
        ("lat_0", "lat_1", "lon", "ens"),
    )
    in_specs = (
        P(None, "ens", LAT, "lon"),
        P(LAT, "lon"),
        P(None, LAT, "lon"),
        P(None, LAT_LON, None, None),
        P(None, LAT_LON, None, None),
        P(None, LAT_LON, None, None),
    )
    out_specs = P(None, "ens", LAT, "lon")
    return jax.shard_map(
        per_device, mesh=torus, in_specs=in_specs, out_specs=out_specs, check_vma=False
    )
```
